32 devices in a mesh: groups: 2 (over y), tile: 4 (over z), chan: 2 (over x), sub: 2 (over core).
Axes of the slice: x: 2, y: 2, z: 4, core: 2. Of those that a mesh axis runs over, the one named last changes fastest.
Arguments:
- latent: bfloat16 [16, 8, 20, 512], P(('groups', 'sub'), None, 'tile', 'chan'), parts along dimension 0, may hold values from -34 to 34
- extents: int32 [4], replicated, may hold values from 1 to 4, as said below
- gain_one: float32 [512], P('chan'), may hold values from 0.1 to 1.9
- weight_one: bfloat16 [3, 3, 3, 512, 512], P(None, None, None, 'tile', 'chan'), may hold values from -0.0546875 to 0.0546875
- gain_two: float32 [512], P('chan'), may hold values from 0.1 to 1.9
- weight_two: bfloat16 [3, 3, 3, 512, 512], P(None, None, None, 'tile', 'chan'), may hold values from -0.0546875 to 0.0546875
Outputs:
- decoded: bfloat16 [16, 16, 40, 512], P(('groups', 'sub'), None, 'tile', 'chan'), parts along dimension 0
The draws below stay inside these ranges and needn't reach their ends.
There are 2 independent parts, one for each index of `groups`. The reference program is written for one: setup_inputs(seed, part) draws one part's arguments, and reference() takes and returns one part's arrays. A program takes and returns all parts, laid end to end along the dimension named above; an argument that names none is the same for every part. Nothing has to cross between parts.
Inputs may be any that keep to these rules, and one draw needn't show every extreme that they name: `extents`: entry i is how many columns of tile i + 1 tile i decodes with its own; the last entry is not used. Among the used entries, the value 4 and the value 1 both occur.
All inputs are finite; a program needn't handle non-finite values.
Results may differ from the reference program's by a relative error of at most 0.0042.
Values may be sent and summed in bfloat16 or wider, within the bound.
No kernel may reach another device: no remote copies, remote signals or barrier semaphores. Data moves between devices by JAX's collectives and lax.ppermute only.
A program may use at most 64 MiB of HBM per device.

```python
import jax
import jax.numpy as jnp
from jax import lax

CH = 512
GROUPS = 32
ROWS = 8
TILE_W = 5
INTERSECTION = 4
FRAMES = 8
TILES = 4
COLS = 20


def draw_latent(key, part):
    keys = jax.random.split(key, 4)
    shape = (FRAMES, ROWS, COLS, CH)
    steps = jnp.arange(FRAMES).astype(jnp.float32) / (FRAMES - 1)
    frame_scale = 0.6 * jnp.power(3.0, steps) * jax.random.uniform(keys[1], (FRAMES,), jnp.float32, 0.8, 1.2)
    chan_scale = jnp.exp(jax.random.uniform(keys[2], (CH,), jnp.float32, jnp.log(0.3), jnp.log(3.0)))
    col_scale = jax.random.uniform(keys[3], (COLS,), jnp.float32, 0.7, 1.3)
    base = jnp.clip(jax.random.normal(keys[0], shape, jnp.float32), -4.0, 4.0)
    values = base * frame_scale[:, None, None, None] * col_scale[None, None, :, None] * chan_scale
    return values.astype(jnp.bfloat16)


def draw_extents(key, part):
    keys = jax.random.split(jax.random.fold_in(key, 11), 3)
    tile_ids = jnp.arange(TILES, dtype=jnp.int32)
    values = jax.random.randint(keys[0], (TILES,), 1, INTERSECTION + 1, jnp.int32)
    chosen = jax.random.randint(keys[1], (), 0, TILES - 1, jnp.int32)
    offset = jax.random.randint(keys[2], (), 0, TILES - 2, jnp.int32)
    lowest = (chosen + 1 + offset) % (TILES - 1)
    values = jnp.where(tile_ids == lowest, 1, values)
    values = jnp.where(tile_ids == chosen, INTERSECTION, values)
    return values.astype(jnp.int32)


def block_scale(stream_key, dims, pieces, least, top_value):
    def one(axis_at, blocks):
        heights = jax.random.uniform(jax.random.fold_in(jax.random.fold_in(stream_key, 6), axis_at), (blocks,), jnp.float32, least / len(pieces), top_value / len(pieces))
        return jnp.repeat(jnp.exp(heights), dims[axis_at] // blocks).reshape((-1,) + (1,) * (len(dims) - axis_at - 1))

    loudness = one(*pieces[0])
    for cut in pieces[1:]:
        loudness = loudness * one(*cut)
    return loudness


def noise(own_key, extent, width, most, cuts=(), held_as=jnp.bfloat16):
    level = block_scale(own_key, extent, cuts, -0.22, 0.18) if cuts else 1.0
    values = jax.random.normal(own_key, extent, jnp.float32) * width * level
    return jnp.minimum(jnp.maximum(values, -most), most).astype(held_as)


def setup_inputs(seed: int = 0, part: int = 0) -> dict:
    key_list = jax.random.split(jax.random.key(seed), 7)
    part_splits = jax.random.split(jax.random.fold_in(key_list[6], part), 7)
    latent = draw_latent(jax.random.fold_in(jax.random.fold_in(key_list[6], part), 71), part)
    extents = draw_extents(jax.random.fold_in(key_list[6], 71), part)
    gain_one = jnp.clip(1.0 + 0.18 * jax.random.normal(key_list[2], (CH,), jnp.float32), 0.1, 1.9)
    weight_one = noise(key_list[3], (3, 3, 3, CH, CH), (27 * CH) ** -0.5, 0.0546875, ((3, 4), (4, 2)))
    gain_two = jnp.clip(1.0 + 0.18 * jax.random.normal(key_list[4], (CH,), jnp.float32), 0.1, 1.9)
    weight_two = noise(key_list[5], (3, 3, 3, CH, CH), (27 * CH) ** -0.5, 0.0546875, ((3, 4), (4, 2)))
    return {"latent": latent, "extents": extents, "gain_one": gain_one, "weight_one": weight_one, "gain_two": gain_two, "weight_two": weight_two}


eps = 1e-06

def convolve(inputs, kernel):
    result = lax.conv_general_dilated(inputs[None], kernel, (1, 1, 1), [(0, 0), (1, 1), (1, 1)], dimension_numbers=('NDHWC', 'DHWIO', 'NDHWC'), preferred_element_type=jnp.float32)
    return result[0]

def group_norm(values, gain, count):
    group_size = CH // GROUPS
    grouped = values.reshape(values.shape[:-1] + (values.shape[-1] // group_size, group_size))
    totals = lax.optimization_barrier(jnp.sum(grouped, axis=(0, 1, 2, 4)))
    squares = lax.optimization_barrier(jnp.sum(grouped * grouped, axis=(0, 1, 2, 4)))
    size = count * group_size
    mean_val = totals / size
    variance = squares / size - mean_val * mean_val
    scaled = (grouped - mean_val[:, None]) * lax.rsqrt(variance + eps)[:, None]
    return scaled.reshape(values.shape) * gain.astype(jnp.float32)

def causal_pad(values):
    return jnp.concatenate([values[:1], values[:1], values], axis=0)

def blend_ramp(prior):
    positions = jnp.arange(2 * INTERSECTION).astype(jnp.float32) + 0.5
    limit = (2 * prior).astype(jnp.float32)[..., None]
    denom = (2 * jnp.maximum(prior, 1)).astype(jnp.float32)[..., None]
    return jnp.where(positions < limit, positions / denom, 1.0)

def decode_tile(tile_in, valid, count, gain_one, weight_one, gain_two, weight_two):
    mask = valid[None, None, :, None]
    source = tile_in.astype(jnp.float32)
    hidden = (jax.nn.silu(group_norm(source, gain_one, count)) * mask).astype(jnp.bfloat16)
    first = (convolve(causal_pad(hidden), weight_one) * mask).astype(jnp.bfloat16)
    first = lax.optimization_barrier(first)
    hidden_two = (jax.nn.silu(group_norm(first.astype(jnp.float32), gain_two, count)) * mask).astype(jnp.bfloat16)
    second = convolve(causal_pad(hidden_two), weight_two)
    return ((source + second) * mask).astype(jnp.bfloat16)

def reference(latent, extents, gain_one, weight_one, gain_two, weight_two):
    span = TILE_W + INTERSECTION
    padded = jnp.concatenate([latent, jnp.zeros((FRAMES, ROWS, INTERSECTION, CH), jnp.bfloat16)], axis=2)
    tile_ids = jnp.arange(TILES, dtype=jnp.int32)
    reaches = jnp.where(tile_ids == TILES - 1, 0, extents).astype(jnp.int32)
    columns = jnp.arange(span, dtype=jnp.int32)

    def tile_out(tile_id):
        reach = jnp.sum(jnp.where(tile_ids == tile_id, reaches, 0))
        valid = (columns < TILE_W + reach).astype(jnp.float32)
        window = lax.dynamic_slice_in_dim(padded, (tile_id * TILE_W).astype(jnp.int32), span, 2)
        window = jnp.where(valid[None, None, :, None] > 0, window, jnp.zeros_like(window))
        count = (TILE_W + reach).astype(jnp.float32) * (FRAMES * ROWS)
        return decode_tile(window, valid, count, gain_one, weight_one, gain_two, weight_two)
    decoded_tiles = lax.map(tile_out, tile_ids)
    larger = jnp.repeat(jnp.repeat(decoded_tiles, 2, axis=2), 2, axis=3)
    own = larger[:, :, :, :2 * TILE_W]
    tails = larger[:, :, :, 2 * TILE_W:]
    arrived = jnp.concatenate([jnp.zeros_like(tails[:1]), tails[:-1]], axis=0)
    prior = jnp.concatenate([jnp.zeros((1,), jnp.int32), reaches[:-1]])
    ramp = blend_ramp(prior)[:, None, None, :, None]
    head = own[:, :, :, :2 * INTERSECTION].astype(jnp.float32) * ramp + arrived.astype(jnp.float32) * (1.0 - ramp)
    joined = jnp.concatenate([head.astype(jnp.bfloat16), own[:, :, :, 2 * INTERSECTION:]], axis=3)
    return jnp.transpose(joined, (1, 2, 0, 3, 4)).reshape(FRAMES, 2 * ROWS, 2 * COLS, CH)
```

```python
import functools

import jax
import jax.numpy as jnp
from jax import lax
from jax.experimental import pallas as pl
from jax.experimental.pallas import tpu as pltpu
from jax.sharding import PartitionSpec as P

CH = 512
GROUPS = 32
INTERSECTION = 4
LANES = 128


eps = 1e-06


def shifted(array, axis, by):
    peers = lax.axis_size(axis)
    pairs = [(i, i + by) for i in range(peers) if 0 <= i + by < peers]
    return lax.ppermute(array, axis, pairs)


def blend_ramp(prior):
    positions = jnp.arange(2 * INTERSECTION).astype(jnp.float32) + 0.5
    limit = (2 * prior).astype(jnp.float32)[..., None]
    denom = (2 * jnp.maximum(prior, 1)).astype(jnp.float32)[..., None]
    return jnp.where(positions < limit, positions / denom, 1.0)


def convolve(inputs, kernel):
    result = lax.conv_general_dilated(
        inputs[None],
        kernel,
        (1, 1, 1),
        [(0, 0), (1, 1), (1, 1)],
        dimension_numbers=("NDHWC", "DHWIO", "NDHWC"),
        preferred_element_type=jnp.float32,
    )
    return result[0]


def group_norm(values, gain, count):
    group_size = CH // GROUPS
    grouped = values.reshape(values.shape[:-1] + (values.shape[-1] // group_size, group_size))
    totals, squares = lax.psum(
        (jnp.sum(grouped, axis=(0, 1, 2, 4)), jnp.sum(grouped * grouped, axis=(0, 1, 2, 4))), "sub"
    )
    size = count * group_size
    mean_val = totals / size
    variance = squares / size - mean_val * mean_val
    scaled = (grouped - mean_val[:, None]) * lax.rsqrt(variance + eps)[:, None]
    return scaled.reshape(values.shape) * gain


def causal_pad(values):
    earlier = shifted(values[-2:], "sub", 1)
    repeated = jnp.concatenate([values[:1], values[:1]], axis=0)
    leading = jnp.where(lax.axis_index("sub") == 0, repeated, earlier)
    return jnp.concatenate([leading, values], axis=0)


def channel_conv(padded_in, weight):
    full_in = lax.all_gather(padded_in, "chan", axis=3, tiled=True)
    out_count = weight.shape[4]
    share = weight.shape[3] // lax.axis_size("sub")
    portion = lax.dynamic_slice_in_dim(weight, lax.axis_index("sub") * share, share, 3)
    fetched = lax.all_gather(portion, "tile", axis=3, tiled=True)
    sectioned = fetched.reshape(3, 3, 3, lax.axis_size("tile"), 1, share, out_count)
    whole = lax.all_gather(sectioned, "sub", axis=4, tiled=True).reshape(3, 3, 3, -1, out_count)
    return convolve(full_in, whole)


def upscale(values):
    return jnp.repeat(jnp.repeat(values, 2, axis=1), 2, axis=2)


def reach_and_prior(extents):
    tile_count = lax.axis_size("tile")
    place = lax.axis_index("tile")
    tile_ids = jnp.arange(tile_count, dtype=jnp.int32)
    reaches = jnp.where(tile_ids == tile_count - 1, 0, extents)
    reach = jnp.sum(jnp.where(tile_ids == place, reaches, 0))
    prior = jnp.sum(jnp.where(tile_ids == place - 1, reaches, 0))
    return reach, prior


def gather_plan(latent, extents, gain_one, weight_one, gain_two, weight_two):
    frame_count, row_count, col_count, chan_count = latent.shape
    reach, prior = reach_and_prior(extents)
    incoming = shifted(latent[:, :, :INTERSECTION, :], "tile", -1)
    window = jnp.concatenate([latent, incoming], axis=2)
    valid = (jnp.arange(col_count + INTERSECTION, dtype=jnp.int32) < col_count + reach).astype(
        jnp.float32
    )
    mask = valid[None, None, :, None]
    window = jnp.where(mask > 0, window, jnp.zeros_like(window))
    count = (col_count + reach).astype(jnp.float32) * (
        frame_count * lax.axis_size("sub") * row_count
    )
    source = window.astype(jnp.float32)
    hidden = (jax.nn.silu(group_norm(source, gain_one, count)) * mask).astype(jnp.bfloat16)
    first = (channel_conv(causal_pad(hidden), weight_one) * mask).astype(jnp.bfloat16)
    first = lax.optimization_barrier(first)
    hidden_two = (
        jax.nn.silu(group_norm(first.astype(jnp.float32), gain_two, count)) * mask
    ).astype(jnp.bfloat16)
    second = channel_conv(causal_pad(hidden_two), weight_two)
    result = ((source + second) * mask).astype(jnp.bfloat16)
    larger = upscale(result)
    own = larger[:, :, : 2 * col_count]
    arrived = shifted(larger[:, :, 2 * col_count :], "tile", 1)
    ramp = blend_ramp(prior)[None, None, :, None]
    head = own[:, :, : 2 * INTERSECTION].astype(jnp.float32) * ramp + arrived.astype(
        jnp.float32
    ) * (1.0 - ramp)
    return jnp.concatenate([head.astype(jnp.bfloat16), own[:, :, 2 * INTERSECTION :]], axis=2)


def normalized(values, gain, count, mask):
    chans = values.shape[-1]
    group_size = CH // GROUPS
    rows = lax.broadcasted_iota(jnp.int32, (chans, chans), 0) // group_size
    cols = lax.broadcasted_iota(jnp.int32, (chans, chans), 1) // group_size
    same = (rows == cols).astype(jnp.float32)
    total = jnp.sum(values, axis=(0, 1, 2)).reshape(1, chans)
    square = jnp.sum(values * values, axis=(0, 1, 2)).reshape(1, chans)
    both = jnp.concatenate([jnp.broadcast_to(total, (8, chans)), jnp.broadcast_to(square, (8, chans))], 0)
    sums = jnp.dot(both, same, precision=lax.Precision.HIGHEST, preferred_element_type=jnp.float32)
    size = count * group_size
    mean = sums[0:1] / size
    variance = sums[8:9] / size - mean * mean
    rate = lax.rsqrt(variance + eps)
    shape = (1, 1, 1, chans)
    scaled = (values - mean.reshape(shape)) * rate.reshape(shape) * gain.reshape(shape)
    return (scaled / (1.0 + jnp.exp(-scaled))) * mask


def column_mask(cols, limit):
    ids = lax.broadcasted_iota(jnp.int32, (1, cols, 8, LANES), 1)
    return (ids < limit).astype(jnp.float32)


def prep_kernel(scal_ref, gain_ref, win_ref, h_ref):
    limit = scal_ref[0]
    halves, chan_parts, frames, cols, rows, width = win_ref.shape
    count = limit.astype(jnp.float32) * (halves * frames * rows)
    mask = column_mask(cols, limit)
    for block in range(chan_parts * width // LANES):
        part, lane = divmod(block * LANES, width)
        values = jnp.concatenate(
            [win_ref[half, part, :, :, :, lane : lane + LANES] for half in range(halves)], 0
        ).astype(jnp.float32)
        values = jnp.where(mask > 0, values, 0.0)
        gain = gain_ref[:, block * LANES : (block + 1) * LANES]
        h_ref[block] = normalized(values, gain, count, mask).astype(jnp.bfloat16)


def fill_patches(h_ref, block, patch_ref):
    frames, cols, rows, width = h_ref.shape[1:]
    ids = lax.broadcasted_iota(jnp.int32, (cols, rows, width), 1)
    empty = jnp.zeros((rows, width), jnp.float32)
    for t in range(frames):
        here = h_ref[block, t].astype(jnp.float32)
        for b in range(3):
            if b == 1:
                moved = here
            else:
                moved = pltpu.roll(here, 1 if b == 0 else rows - 1, 1)
                moved = jnp.where(ids == (0 if b == 0 else rows - 1), 0.0, moved)
            flat = moved.reshape(cols * rows, width)
            for d in range(3):
                if d == 0:
                    piece = jnp.concatenate([empty, flat], 0)
                elif d == 1:
                    piece = jnp.concatenate([flat, empty], 0)
                else:
                    piece = jnp.concatenate([flat[rows:], empty, empty], 0)
                piece = piece.astype(jnp.bfloat16)
                lane = (b * 3 + d) * width
                patch_ref[t + 2, :, lane : lane + width] = piece
                if t == 0:
                    patch_ref[0, :, lane : lane + width] = piece
                    patch_ref[1, :, lane : lane + width] = piece


def add_block(h_ref, block, weight_ref, patch_ref, acc_ref):
    fill_patches(h_ref, block, patch_ref)
    frames = h_ref.shape[1]
    pitch = patch_ref.shape[1]
    for a in range(3):
        left = patch_ref[a : a + frames].reshape(frames * pitch, patch_ref.shape[2])
        acc_ref[...] += jnp.dot(left, weight_ref[a], preferred_element_type=jnp.float32)


def conv_all(scal_ref, h_ref, weight_refs, patch_ref, acc_ref):
    blocks = h_ref.shape[0]
    acc_ref[...] = jnp.zeros_like(acc_ref)
    for i, weight_ref in enumerate(weight_refs):
        block = scal_ref[1 + i]

        @pl.when((block >= 0) & (block < blocks))
        def _(block=block, weight_ref=weight_ref):
            add_block(h_ref, block, weight_ref, patch_ref, acc_ref)


def result_of(acc_ref, frames, cols, rows):
    pitch = acc_ref.shape[0] // frames
    whole = acc_ref[...].reshape(frames, pitch, LANES)
    return whole[:, : cols * rows].reshape(frames, cols, rows, LANES)


def first_kernel(scal_ref, gain_ref, h_ref, *refs):
    weight_refs, out_ref, patch_ref, acc_ref = refs[:-3], refs[-3], refs[-2], refs[-1]
    conv_all(scal_ref, h_ref, weight_refs, patch_ref, acc_ref)
    frames, cols, rows = h_ref.shape[1:4]
    limit = scal_ref[0]
    mask = column_mask(cols, limit)
    count = limit.astype(jnp.float32) * (frames * rows)
    first = (result_of(acc_ref, frames, cols, rows) * mask).astype(jnp.bfloat16)
    out_ref[...] = normalized(first.astype(jnp.float32), gain_ref[...], count, mask).astype(
        jnp.bfloat16
    )


def second_kernel(scal_ref, source_ref, h_ref, *refs):
    weight_refs, out_ref, patch_ref, acc_ref = refs[:-3], refs[-3], refs[-2], refs[-1]
    conv_all(scal_ref, h_ref, weight_refs, patch_ref, acc_ref)
    frames, cols, rows = h_ref.shape[1:4]
    mask = column_mask(cols, scal_ref[0])
    source = source_ref[...].astype(jnp.float32)
    out_ref[...] = ((source + result_of(acc_ref, frames, cols, rows)) * mask).astype(jnp.bfloat16)


def conv_call(kernel, scalars, extra, hidden, weights):
    blocks, frames, cols, rows, width = hidden.shape
    pitch = (cols + 1) * rows
    vmem = pl.BlockSpec(memory_space=pltpu.VMEM)
    return pl.pallas_call(
        kernel,
        out_shape=jax.ShapeDtypeStruct((frames, cols, rows, LANES), jnp.bfloat16),
        in_specs=[pl.BlockSpec(memory_space=pltpu.SMEM)] + [vmem] * (2 + len(weights)),
        out_specs=vmem,
        scratch_shapes=[
            pltpu.VMEM((frames + 2, pitch, 9 * width), jnp.bfloat16),
            pltpu.VMEM((frames * pitch, LANES), jnp.float32),
        ],
    )(scalars, extra, hidden, *weights)


def relayed(weight):
    tiles, subs = lax.axis_size("tile"), lax.axis_size("sub")
    out_share = weight.shape[4] // lax.axis_size("groups")
    own = lax.dynamic_slice_in_dim(weight, lax.axis_index("groups") * out_share, out_share, 4)
    own = own.reshape(3, -1, out_share)
    held, pieces = own, [own]
    for step in range(1, tiles):
        pairs = [(z * subs, (z + 1) * subs) for z in range(step - 1, tiles - 1)]
        pairs += [(z * subs + 1, (z - 1) * subs + 1) for z in range(1, tiles - step + 1)]
        held = lax.ppermute(held, ("tile", "sub"), pairs)
        pieces += [held, lax.ppermute(held, "sub", [(0, 1), (1, 0)])]
    return pieces


def share_plan(latent, extents, gain_one, weight_one, gain_two, weight_two):
    frame_count, row_count, col_count, chan_count = latent.shape
    tiles, clips, chans = lax.axis_size("tile"), lax.axis_size("groups"), lax.axis_size("chan")
    place, clip, sub = lax.axis_index("tile"), lax.axis_index("groups"), lax.axis_index("sub")
    reach, prior = reach_and_prior(extents)
    span = col_count + INTERSECTION
    share = chan_count // clips

    first_weights = relayed(weight_one)
    second_weights = relayed(weight_two)
    signs = jnp.where(sub == 0, -1, 1)
    owners = [place]
    for step in range(1, tiles):
        owners += [place + signs * step, place - signs * step]
    scalars = jnp.stack([col_count + reach] + owners).astype(jnp.int32)

    by_col = jnp.transpose(latent, (0, 2, 1, 3))
    incoming = shifted(by_col[:, :INTERSECTION], "tile", -1)
    window = jnp.concatenate([by_col, incoming], axis=1)
    turned = lax.ppermute(window, ("groups", "sub"), [(0, 0), (1, 2), (2, 1), (3, 3)])
    windows = lax.all_gather(turned, ("groups", "chan"), axis=0, tiled=False)
    windows = windows.reshape((clips, chans) + turned.shape)
    gain_all = lax.all_gather(gain_one, "chan", axis=0, tiled=True).reshape(1, -1)
    vmem = pl.BlockSpec(memory_space=pltpu.VMEM)
    frames = clips * frame_count
    hidden = pl.pallas_call(
        prep_kernel,
        out_shape=jax.ShapeDtypeStruct(
            (chans * chan_count // LANES, frames, span, row_count, LANES), jnp.bfloat16
        ),
        in_specs=[pl.BlockSpec(memory_space=pltpu.SMEM), vmem, vmem],
        out_specs=vmem,
    )(scalars, gain_all, windows)
    gain_share = lax.dynamic_slice_in_dim(gain_two, clip * share, share, 0).reshape(1, -1)
    hidden_two = conv_call(first_kernel, scalars, gain_share, hidden, first_weights)
    gathered = lax.all_gather(hidden_two, ("chan", "groups"), axis=0, tiled=False)
    mine = lax.dynamic_index_in_dim(windows, lax.axis_index("chan"), 1, keepdims=False)
    mine = lax.dynamic_slice_in_dim(mine, clip * share, share, 4)
    source = mine.reshape(frames, span, row_count, share)
    result = conv_call(second_kernel, scalars, source, gathered, second_weights)

    halves = result.reshape(clips, frame_count, span, row_count, share)
    owned, tails = [], []
    for turn in range(2):
        part = lax.dynamic_index_in_dim(halves, clip ^ turn, 0, keepdims=False)
        pairs = [(g * 2 + c, c * 2 + (g ^ turn)) for g in range(2) for c in range(2)]
        owned.append(lax.ppermute(part[:, :col_count], ("groups", "sub"), pairs))
        onward = [
            ((g * tiles + z) * 2 + c, (c * tiles + z + 1) * 2 + (g ^ turn))
            for g in range(2)
            for z in range(tiles - 1)
            for c in range(2)
        ]
        tails.append(lax.ppermute(part[:, col_count:], ("groups", "tile", "sub"), onward))

    def joined(pair):
        straight = jnp.concatenate(pair, axis=3)
        crossed = jnp.concatenate(pair[::-1], axis=3)
        return jnp.where(sub == 0, straight, crossed)

    own, tail = joined(owned), joined(tails)
    ramp = blend_ramp(prior)[None, :, None, None]
    head = jnp.repeat(own[:, :INTERSECTION].astype(jnp.float32), 2, axis=1) * ramp + jnp.repeat(
        tail.astype(jnp.float32), 2, axis=1
    ) * (1.0 - ramp)
    rest = jnp.repeat(own[:, INTERSECTION:], 2, axis=1)
    decoded = jnp.concatenate([head.astype(jnp.bfloat16), rest], axis=1)
    decoded = jnp.repeat(decoded, 2, axis=2)
    return jnp.transpose(decoded, (0, 2, 1, 3))


def shards(latent, extents, gain_one, weight_one, gain_two, weight_two):
    rows_held, cols_held = weight_one.shape[3:]
    even = lax.axis_size("groups") == 2 and lax.axis_size("sub") == 2
    fits = rows_held == LANES and cols_held == 2 * LANES and latent.shape[1] == 8
    plan = share_plan if even and fits else gather_plan
    return plan(latent, extents, gain_one, weight_one, gain_two, weight_two)


def solution(mesh):
    placed = (
        P(("groups", "sub"), None, "tile", "chan"),
        P(),
        P("chan"),
        P(None, None, None, "tile", "chan"),
        P("chan"),
        P(None, None, None, "tile", "chan"),
    )
    return jax.shard_map(
        shards,
        mesh=mesh,
        in_specs=placed,
        out_specs=P(("groups", "sub"), None, "tile", "chan"),
        check_vma=False,
    )
```

```python
import functools

import jax
import jax.numpy as jnp
from jax import lax
from jax.experimental import pallas as pl
from jax.experimental.pallas import tpu as pltpu
from jax.sharding import PartitionSpec as P


CH = 512
GROUPS = 32
INTERSECTION = 4
LANES = 128
FIRST_SPLIT = 3
SECOND_SPLIT = 5


eps = 1e-06


def shifted(array, axis, by):
    peers = lax.axis_size(axis)
    pairs = [(i, i + by) for i in range(peers) if 0 <= i + by < peers]
    return lax.ppermute(array, axis, pairs)


def blend_ramp(prior):
    positions = jnp.arange(2 * INTERSECTION).astype(jnp.float32) + 0.5
    limit = (2 * prior).astype(jnp.float32)[..., None]
    denom = (2 * jnp.maximum(prior, 1)).astype(jnp.float32)[..., None]
    return jnp.where(positions < limit, positions / denom, 1.0)


def convolve(inputs, kernel):
    result = lax.conv_general_dilated(
        inputs[None],
        kernel,
        (1, 1, 1),
        [(0, 0), (1, 1), (1, 1)],
        dimension_numbers=("NDHWC", "DHWIO", "NDHWC"),
        preferred_element_type=jnp.float32,
    )
    return result[0]


def group_norm(values, gain, count):
    group_size = CH // GROUPS
    grouped = values.reshape(values.shape[:-1] + (values.shape[-1] // group_size, group_size))
    totals, squares = lax.psum(
        (jnp.sum(grouped, axis=(0, 1, 2, 4)), jnp.sum(grouped * grouped, axis=(0, 1, 2, 4))), "sub"
    )
    size = count * group_size
    mean_val = totals / size
    variance = squares / size - mean_val * mean_val
    scaled = (grouped - mean_val[:, None]) * lax.rsqrt(variance + eps)[:, None]
    return scaled.reshape(values.shape) * gain


def causal_pad(values):
    earlier = shifted(values[-2:], "sub", 1)
    repeated = jnp.concatenate([values[:1], values[:1]], axis=0)
    leading = jnp.where(lax.axis_index("sub") == 0, repeated, earlier)
    return jnp.concatenate([leading, values], axis=0)


def channel_conv(padded_in, weight):
    full_in = lax.all_gather(padded_in, "chan", axis=3, tiled=True)
    out_count = weight.shape[4]
    share = weight.shape[3] // lax.axis_size("sub")
    portion = lax.dynamic_slice_in_dim(weight, lax.axis_index("sub") * share, share, 3)
    fetched = lax.all_gather(portion, "tile", axis=3, tiled=True)
    sectioned = fetched.reshape(3, 3, 3, lax.axis_size("tile"), 1, share, out_count)
    whole = lax.all_gather(sectioned, "sub", axis=4, tiled=True).reshape(3, 3, 3, -1, out_count)
    return convolve(full_in, whole)


def upscale(values):
    return jnp.repeat(jnp.repeat(values, 2, axis=1), 2, axis=2)


def reach_and_prior(extents):
    tile_count = lax.axis_size("tile")
    place = lax.axis_index("tile")
    tile_ids = jnp.arange(tile_count, dtype=jnp.int32)
    reaches = jnp.where(tile_ids == tile_count - 1, 0, extents)
    reach = jnp.sum(jnp.where(tile_ids == place, reaches, 0))
    prior = jnp.sum(jnp.where(tile_ids == place - 1, reaches, 0))
    return reach, prior


def gather_plan(latent, extents, gain_one, weight_one, gain_two, weight_two):
    frame_count, row_count, col_count, _ = latent.shape
    reach, prior = reach_and_prior(extents)
    incoming = shifted(latent[:, :, :INTERSECTION, :], "tile", -1)
    window = jnp.concatenate([latent, incoming], axis=2)
    valid = (jnp.arange(col_count + INTERSECTION, dtype=jnp.int32) < col_count + reach).astype(
        jnp.float32
    )
    mask = valid[None, None, :, None]
    window = jnp.where(mask > 0, window, jnp.zeros_like(window))
    count = (col_count + reach).astype(jnp.float32) * (
        frame_count * lax.axis_size("sub") * row_count
    )
    source = window.astype(jnp.float32)
    hidden = (jax.nn.silu(group_norm(source, gain_one, count)) * mask).astype(jnp.bfloat16)
    first = (channel_conv(causal_pad(hidden), weight_one) * mask).astype(jnp.bfloat16)
    first = lax.optimization_barrier(first)
    hidden_two = (
        jax.nn.silu(group_norm(first.astype(jnp.float32), gain_two, count)) * mask
    ).astype(jnp.bfloat16)
    second = channel_conv(causal_pad(hidden_two), weight_two)
    result = ((source + second) * mask).astype(jnp.bfloat16)
    larger = upscale(result)
    own = larger[:, :, : 2 * col_count]
    arrived = shifted(larger[:, :, 2 * col_count :], "tile", 1)
    ramp = blend_ramp(prior)[None, None, :, None]
    head = own[:, :, : 2 * INTERSECTION].astype(jnp.float32) * ramp + arrived.astype(
        jnp.float32
    ) * (1.0 - ramp)
    return jnp.concatenate([head.astype(jnp.bfloat16), own[:, :, 2 * INTERSECTION :]], axis=2)


def normalized(values, gain, count, mask):
    chans = values.shape[-1]
    group_size = CH // GROUPS
    rows = lax.broadcasted_iota(jnp.int32, (chans, chans), 0) // group_size
    cols = lax.broadcasted_iota(jnp.int32, (chans, chans), 1) // group_size
    same = (rows == cols).astype(jnp.float32)
    total = jnp.sum(values, axis=(0, 1, 2)).reshape(1, chans)
    square = jnp.sum(values * values, axis=(0, 1, 2)).reshape(1, chans)
    both = jnp.concatenate([jnp.broadcast_to(total, (8, chans)), jnp.broadcast_to(square, (8, chans))], 0)
    sums = jnp.dot(both, same, precision=lax.Precision.HIGHEST, preferred_element_type=jnp.float32)
    size = count * group_size
    mean = sums[0:1] / size
    variance = sums[8:9] / size - mean * mean
    rate = lax.rsqrt(variance + eps)
    shape = (1, 1, 1, chans)
    scaled = (values - mean.reshape(shape)) * rate.reshape(shape) * gain.reshape(shape)
    return (scaled / (1.0 + jnp.exp(-scaled))) * mask


def column_mask(cols, limit):
    ids = lax.broadcasted_iota(jnp.int32, (1, cols, 8, LANES), 1)
    return (ids < limit).astype(jnp.float32)


def window_limit(extents_ref, cols):
    place = lax.axis_index("tile")
    reach = jnp.where(place == lax.axis_size("tile") - 1, 0, extents_ref[place])
    return cols - INTERSECTION + reach


def owner_of(slot):
    step = (slot + 1) // 2
    ahead = (lax.axis_index("sub") == 0) == (slot % 2 == 0)
    return lax.axis_index("tile") + jnp.where(ahead, step, -step)


def prepare(limit, gain_refs, win_refs, h_ref, source_ref):
    clip, chan = lax.axis_index("groups"), lax.axis_index("chan")
    frames, cols, rows, width = win_refs[0].shape
    count = limit.astype(jnp.float32) * (2 * frames * rows)
    mask = column_mask(cols, limit)
    for away, gain_ref in enumerate(gain_refs):
        for piece in range(width // LANES):
            lanes = slice(piece * LANES, (piece + 1) * LANES)
            both = [win_refs[2 * turn + away][:, :, :, lanes] for turn in range(2)]
            values = jnp.concatenate(both, 0).astype(jnp.float32)
            values = jnp.where(mask > 0, values, 0.0)
            done = normalized(values, gain_ref[:, lanes], count, mask).astype(jnp.bfloat16)
            block = (chan ^ away) * (width // LANES) + piece
            for turn in range(2):
                rows_at = pl.ds((clip ^ turn) * frames, frames)
                h_ref[block, rows_at] = done[turn * frames : (turn + 1) * frames]
                if away == 0:

                    @pl.when(clip == piece)
                    def _(rows_at=rows_at, turn=turn, both=both):
                        source_ref[rows_at] = both[turn]


def fill_patches(h_ref, block, patch_ref):
    frames, cols, rows, width = h_ref.shape[1:]
    ids = lax.broadcasted_iota(jnp.int32, (cols, rows, width), 1)
    empty = jnp.zeros((rows, width), jnp.float32)
    for t in range(frames):
        here = h_ref[block, t].astype(jnp.float32)
        for b in range(3):
            if b == 1:
                moved = here
            else:
                moved = pltpu.roll(here, 1 if b == 0 else rows - 1, 1)
                moved = jnp.where(ids == (0 if b == 0 else rows - 1), 0.0, moved)
            flat = moved.reshape(cols * rows, width)
            for d in range(3):
                if d == 0:
                    piece = jnp.concatenate([empty, flat], 0)
                elif d == 1:
                    piece = jnp.concatenate([flat, empty], 0)
                else:
                    piece = jnp.concatenate([flat[rows:], empty, empty], 0)
                piece = piece.astype(jnp.bfloat16)
                lane = (b * 3 + d) * width
                patch_ref[t + 2, :, lane : lane + width] = piece
                if t == 0:
                    patch_ref[0, :, lane : lane + width] = piece
                    patch_ref[1, :, lane : lane + width] = piece


def add_block(h_ref, block, weight_ref, patch_ref, wide_ref, acc_ref):
    fill_patches(h_ref, block, patch_ref)
    frames = h_ref.shape[1]
    pitch, depth = patch_ref.shape[1:]
    both = jnp.concatenate([weight_ref[0], weight_ref[1]], axis=1)
    left = patch_ref[: frames + 1].reshape((frames + 1) * pitch, depth)
    wide_ref[...] += jnp.dot(left, both, preferred_element_type=jnp.float32)
    left = patch_ref[2:].reshape(frames * pitch, depth)
    acc_ref[...] += jnp.dot(left, weight_ref[2], preferred_element_type=jnp.float32)


def weight_copies(slots, weight_refs, held_ref, sem_ref):
    copies = []
    for i, (slot, weight_ref) in enumerate(zip(slots, weight_refs)):
        owner = owner_of(slot)
        there = (owner >= 0) & (owner < lax.axis_size("tile"))
        copy = pltpu.make_async_copy(weight_ref, held_ref.at[i], sem_ref.at[i])
        copies.append((owner, there, copy))
    return copies


def start_weights(copies):
    for _, there, copy in copies:

        @pl.when(there)
        def _(copy=copy):
            copy.start()


def add_blocks(copies, h_ref, held_ref, patch_ref, wide_ref, acc_ref):
    wide_ref[...] = jnp.zeros_like(wide_ref)
    for i, (owner, there, copy) in enumerate(copies):

        @pl.when(there)
        def _(i=i, owner=owner, copy=copy):
            copy.wait()
            add_block(h_ref, owner, held_ref.at[i], patch_ref, wide_ref, acc_ref)

    shift = patch_ref.shape[1]
    count = acc_ref.shape[0]
    acc_ref[...] += wide_ref[:count, :LANES] + wide_ref[shift : shift + count, LANES:]


def result_of(acc_ref, frames, cols, rows):
    pitch = acc_ref.shape[0] // frames
    whole = acc_ref[...].reshape(frames, pitch, LANES)
    return whole[:, : cols * rows].reshape(frames, cols, rows, LANES)


def fetch_blocks(near_refs, h_ref, sem_ref):
    own = lax.axis_index("chan") * 2 + lax.axis_index("groups")
    copies = [
        pltpu.make_async_copy(near_ref, h_ref.at[own ^ code], sem_ref.at[code])
        for code, near_ref in enumerate(near_refs)
    ]
    for copy in copies:
        copy.start()
    return copies


def first_begin(slots, extents_ref, gain_ref, far_gain_ref, *refs):
    win_refs, weight_refs = refs[:4], refs[4 : 4 + len(slots)]
    h_ref, source_ref, acc_ref, patch_ref, wide_ref, held_ref, sem_ref = refs[4 + len(slots) :]
    copies = weight_copies(slots, weight_refs, held_ref, sem_ref)
    start_weights(copies)
    limit = window_limit(extents_ref, h_ref.shape[2])
    prepare(limit, (gain_ref, far_gain_ref), win_refs, h_ref, source_ref)
    acc_ref[...] = jnp.zeros_like(acc_ref)
    add_blocks(copies, h_ref, held_ref, patch_ref, wide_ref, acc_ref)


def first_end(slots, extents_ref, gain_ref, h_ref, begun_ref, *refs):
    weight_refs = refs[: len(slots)]
    out_ref, acc_ref, patch_ref, wide_ref, held_ref, sem_ref = refs[len(slots) :]
    copies = weight_copies(slots, weight_refs, held_ref, sem_ref)
    start_weights(copies)
    acc_ref[...] = begun_ref[...]
    add_blocks(copies, h_ref, held_ref, patch_ref, wide_ref, acc_ref)
    frames, cols, rows = h_ref.shape[1:4]
    limit = window_limit(extents_ref, cols)
    mask = column_mask(cols, limit)
    count = limit.astype(jnp.float32) * (frames * rows)
    first = (result_of(acc_ref, frames, cols, rows) * mask).astype(jnp.bfloat16)
    share = pl.multiple_of(lax.axis_index("groups") * LANES, LANES)
    gain = gain_ref[:, pl.ds(share, LANES)]
    done = normalized(first.astype(jnp.float32), gain, count, mask)
    out_ref[...] = done.astype(jnp.bfloat16)


def second_begin(slots, *refs):
    near_refs, weight_refs = refs[:4], refs[4 : 4 + len(slots)]
    acc_ref, h_ref, h_sem_ref, patch_ref, wide_ref, held_ref, sem_ref = refs[4 + len(slots) :]
    fetched = fetch_blocks(near_refs, h_ref, h_sem_ref)
    copies = weight_copies(slots, weight_refs, held_ref, sem_ref)
    start_weights(copies)
    acc_ref[...] = jnp.zeros_like(acc_ref)
    for copy in fetched:
        copy.wait()
    add_blocks(copies, h_ref, held_ref, patch_ref, wide_ref, acc_ref)


def second_end(slots, extents_ref, source_ref, begun_ref, *refs):
    near_refs, weight_refs = refs[:4], refs[4 : 4 + len(slots)]
    out_refs, rest = refs[4 + len(slots) : 8 + len(slots)], refs[8 + len(slots) :]
    done_ref, acc_ref, h_ref, h_sem_ref, patch_ref, wide_ref, held_ref, sem_ref = rest
    fetched = fetch_blocks(near_refs, h_ref, h_sem_ref)
    copies = weight_copies(slots, weight_refs, held_ref, sem_ref)
    start_weights(copies)
    acc_ref[...] = begun_ref[...]
    for copy in fetched:
        copy.wait()
    add_blocks(copies, h_ref, held_ref, patch_ref, wide_ref, acc_ref)
    frames, cols, rows = h_ref.shape[1:4]
    mask = column_mask(cols, window_limit(extents_ref, cols))
    source = source_ref[...].astype(jnp.float32)
    done = (source + result_of(acc_ref, frames, cols, rows)) * mask
    done_ref[...] = done.astype(jnp.bfloat16)
    half, kept = frames // 2, cols - INTERSECTION
    for turn in range(2):
        rows_at = pl.ds((lax.axis_index("groups") ^ turn) * half, half)
        out_refs[turn][...] = done_ref[rows_at, :kept]
        out_refs[2 + turn][...] = done_ref[rows_at, kept:]


def relayed(weight):
    tiles, subs = lax.axis_size("tile"), lax.axis_size("sub")
    out_share = weight.shape[4] // lax.axis_size("groups")
    own = lax.dynamic_slice_in_dim(weight, lax.axis_index("groups") * out_share, out_share, 4)
    own = own.reshape(3, -1, out_share)
    held, pieces = own, [own]
    for step in range(1, tiles):
        pairs = [(z * subs, (z + 1) * subs) for z in range(step - 1, tiles - 1)]
        pairs += [(z * subs + 1, (z - 1) * subs + 1) for z in range(1, tiles - step + 1)]
        held = lax.ppermute(held, ("tile", "sub"), pairs)
        pieces += [held, lax.ppermute(held, "sub", [(0, 1), (1, 0)])]
    return pieces


def by_distance(array):
    got = [array]
    for code in range(1, 4):
        pairs = [(i, i ^ code) for i in range(4)]
        got.append(lax.ppermute(array, ("groups", "chan"), pairs))
    return got


def share_plan(latent, extents, gain_one, weight_one, gain_two, weight_two):
    frame_count, row_count, col_count, chan_count = latent.shape
    tiles, clips = lax.axis_size("tile"), lax.axis_size("groups")
    sub = lax.axis_index("sub")
    _, prior = reach_and_prior(extents)
    span = col_count + INTERSECTION
    share = chan_count // clips
    frames = clips * frame_count
    pitch = (span + 1) * row_count
    taps = weight_one.shape[1] * weight_one.shape[2]
    vmem, smem = pl.BlockSpec(memory_space=pltpu.VMEM), pl.BlockSpec(memory_space=pltpu.SMEM)
    anywhere = pl.BlockSpec(memory_space=pl.ANY)
    final = jax.ShapeDtypeStruct((frames, span, row_count, share), jnp.bfloat16)
    blocks = jax.ShapeDtypeStruct((tiles,) + final.shape, jnp.bfloat16)
    total = jax.ShapeDtypeStruct((frames * pitch, share), jnp.float32)

    def scratch(slots):
        return [
            pltpu.VMEM((frames + 2, pitch, taps * LANES), jnp.bfloat16),
            pltpu.VMEM(((frames + 1) * pitch, 2 * share), jnp.float32),
            pltpu.VMEM((len(slots), 3, taps * LANES, share), jnp.bfloat16),
            pltpu.SemaphoreType.DMA((len(slots),)),
        ]

    def chosen(weights, slots):
        return [weights[slot] for slot in slots]

    h_scratch = [pltpu.VMEM(blocks.shape, jnp.bfloat16), pltpu.SemaphoreType.DMA((tiles,))]
    acc_scratch = [pltpu.VMEM(total.shape, jnp.float32)]

    by_col = jnp.transpose(latent, (0, 2, 1, 3))
    incoming = shifted(by_col[:, :INTERSECTION], "tile", -1)
    window = jnp.concatenate([by_col, incoming], axis=1)
    windows = []
    for turn in range(2):
        for away in range(2):
            pairs = [
                ((c * 2 + (x ^ away)) * 2 + (g ^ turn), (g * 2 + x) * 2 + c)
                for g in range(2)
                for x in range(2)
                for c in range(2)
            ]
            windows.append(lax.ppermute(window, ("groups", "chan", "sub"), pairs))
    first_weights = relayed(weight_one)
    second_weights = relayed(weight_two)
    own_gain = gain_one.reshape(1, -1)
    other_gain = lax.ppermute(own_gain, "chan", [(0, 1), (1, 0)])
    slots = tuple(range(2 * tiles - 1))
    early, late = slots[:FIRST_SPLIT], slots[FIRST_SPLIT:]
    hidden, source, begun = pl.pallas_call(
        functools.partial(first_begin, early),
        out_shape=(blocks, final, total),
        in_specs=[smem] + [vmem] * 6 + [anywhere] * len(early),
        out_specs=(vmem,) * 3,
        scratch_shapes=scratch(early),
    )(extents, own_gain, other_gain, *windows, *chosen(first_weights, early))
    hidden_two = pl.pallas_call(
        functools.partial(first_end, late),
        out_shape=final,
        in_specs=[smem] + [vmem] * 3 + [anywhere] * len(late),
        out_specs=vmem,
        scratch_shapes=acc_scratch + scratch(late),
    )(extents, gain_two.reshape(1, -1), hidden, begun, *chosen(first_weights, late))
    near = by_distance(hidden_two)
    near = [near[0], near[2], near[1], near[3]]
    early, late = slots[:SECOND_SPLIT], slots[SECOND_SPLIT:]
    begun = pl.pallas_call(
        functools.partial(second_begin, early),
        out_shape=total,
        in_specs=[anywhere] * (tiles + len(early)),
        out_specs=vmem,
        scratch_shapes=h_scratch + scratch(early),
    )(*near, *chosen(second_weights, early))
    kept = jax.ShapeDtypeStruct((frame_count, col_count, row_count, share), jnp.bfloat16)
    passed = jax.ShapeDtypeStruct((frame_count, INTERSECTION, row_count, share), jnp.bfloat16)
    parts = pl.pallas_call(
        functools.partial(second_end, late),
        out_shape=(kept, kept, passed, passed),
        in_specs=[smem] + [vmem] * 2 + [anywhere] * (tiles + len(late)),
        out_specs=(vmem,) * 4,
        scratch_shapes=[pltpu.VMEM(final.shape, jnp.bfloat16)]
        + acc_scratch
        + h_scratch
        + scratch(late),
    )(extents, source, begun, *near, *chosen(second_weights, late))

    owned, tails = [], []
    for turn in range(2):
        onward = [
            ((g * tiles + z) * 2 + c, (c * tiles + z + 1) * 2 + (g ^ turn))
            for g in range(2)
            for z in range(tiles - 1)
            for c in range(2)
        ]
        tails.append(
            lax.ppermute(parts[2 + turn], ("groups", "tile", "sub"), onward)
        )
    for turn in range(2):
        pairs = [(g * 2 + c, c * 2 + (g ^ turn)) for g in range(2) for c in range(2)]
        owned.append(lax.ppermute(parts[turn], ("groups", "sub"), pairs))

    def joined(pair):
        straight = jnp.concatenate(pair, axis=3)
        crossed = jnp.concatenate(pair[::-1], axis=3)
        return jnp.where(sub == 0, straight, crossed)

    own, tail = joined(owned), joined(tails)
    ramp = blend_ramp(prior)[None, :, None, None]
    head = jnp.repeat(own[:, :INTERSECTION].astype(jnp.float32), 2, axis=1) * ramp + jnp.repeat(
        tail.astype(jnp.float32), 2, axis=1
    ) * (1.0 - ramp)
    rest = jnp.repeat(own[:, INTERSECTION:], 2, axis=1)
    decoded = jnp.concatenate([head.astype(jnp.bfloat16), rest], axis=1)
    decoded = jnp.repeat(decoded, 2, axis=2)
    return jnp.transpose(decoded, (0, 2, 1, 3))


def solution(mesh):
    placed = (
        P(("groups", "sub"), None, "tile", "chan"),
        P(),
        P("chan"),
        P(None, None, None, "tile", "chan"),
        P("chan"),
        P(None, None, None, "tile", "chan"),
    )
    sizes = mesh.shape
    pairs_up = sizes["groups"] == 2 and sizes["sub"] == 2 and sizes["chan"] == 2
    few = pairs_up and CH // sizes["tile"] == LANES

    def body(*arrays):
        return (share_plan if few else gather_plan)(*arrays)

    return jax.shard_map(
        body,
        mesh=mesh,
        in_specs=placed,
        out_specs=P(("groups", "sub"), None, "tile", "chan"),
        check_vma=False,
    )
```

```python
import functools

import jax
import jax.numpy as jnp
from jax import lax
from jax.experimental import pallas as pl
from jax.experimental.pallas import tpu as pltpu
from jax.sharding import PartitionSpec as P


CH = 512
GROUPS = 32
INTERSECTION = 4
LANES = 128
GRANT = 14 * 2**20
FIRST_SPLIT = 3
SECOND_SPLIT = 5


eps = 1e-06


def shifted(array, axis, by):
    peers = lax.axis_size(axis)
    pairs = [(i, i + by) for i in range(peers) if 0 <= i + by < peers]
    return lax.ppermute(array, axis, pairs)


def blend_ramp(prior):
    positions = jnp.arange(2 * INTERSECTION).astype(jnp.float32) + 0.5
    limit = (2 * prior).astype(jnp.float32)[..., None]
    denom = (2 * jnp.maximum(prior, 1)).astype(jnp.float32)[..., None]
    return jnp.where(positions < limit, positions / denom, 1.0)


def convolve(inputs, kernel):
    result = lax.conv_general_dilated(
        inputs[None],
        kernel,
        (1, 1, 1),
        [(0, 0), (1, 1), (1, 1)],
        dimension_numbers=("NDHWC", "DHWIO", "NDHWC"),
        preferred_element_type=jnp.float32,
    )
    return result[0]


def group_norm(values, gain, count):
    group_size = CH // GROUPS
    grouped = values.reshape(values.shape[:-1] + (values.shape[-1] // group_size, group_size))
    totals, squares = lax.psum(
        (jnp.sum(grouped, axis=(0, 1, 2, 4)), jnp.sum(grouped * grouped, axis=(0, 1, 2, 4))), "sub"
    )
    size = count * group_size
    mean_val = totals / size
    variance = squares / size - mean_val * mean_val
    scaled = (grouped - mean_val[:, None]) * lax.rsqrt(variance + eps)[:, None]
    return scaled.reshape(values.shape) * gain


def causal_pad(values):
    earlier = shifted(values[-2:], "sub", 1)
    repeated = jnp.concatenate([values[:1], values[:1]], axis=0)
    leading = jnp.where(lax.axis_index("sub") == 0, repeated, earlier)
    return jnp.concatenate([leading, values], axis=0)


def channel_conv(padded_in, weight):
    full_in = lax.all_gather(padded_in, "chan", axis=3, tiled=True)
    out_count = weight.shape[4]
    share = weight.shape[3] // lax.axis_size("sub")
    portion = lax.dynamic_slice_in_dim(weight, lax.axis_index("sub") * share, share, 3)
    fetched = lax.all_gather(portion, "tile", axis=3, tiled=True)
    sectioned = fetched.reshape(3, 3, 3, lax.axis_size("tile"), 1, share, out_count)
    whole = lax.all_gather(sectioned, "sub", axis=4, tiled=True).reshape(3, 3, 3, -1, out_count)
    return convolve(full_in, whole)


def upscale(values):
    return jnp.repeat(jnp.repeat(values, 2, axis=1), 2, axis=2)


def reach_and_prior(extents):
    tile_count = lax.axis_size("tile")
    place = lax.axis_index("tile")
    tile_ids = jnp.arange(tile_count, dtype=jnp.int32)
    reaches = jnp.where(tile_ids == tile_count - 1, 0, extents)
    reach = jnp.sum(jnp.where(tile_ids == place, reaches, 0))
    prior = jnp.sum(jnp.where(tile_ids == place - 1, reaches, 0))
    return reach, prior


def gather_plan(latent, extents, gain_one, weight_one, gain_two, weight_two):
    frame_count, row_count, col_count, _ = latent.shape
    reach, prior = reach_and_prior(extents)
    incoming = shifted(latent[:, :, :INTERSECTION, :], "tile", -1)
    window = jnp.concatenate([latent, incoming], axis=2)
    valid = (jnp.arange(col_count + INTERSECTION, dtype=jnp.int32) < col_count + reach).astype(
        jnp.float32
    )
    mask = valid[None, None, :, None]
    window = jnp.where(mask > 0, window, jnp.zeros_like(window))
    count = (col_count + reach).astype(jnp.float32) * (
        frame_count * lax.axis_size("sub") * row_count
    )
    source = window.astype(jnp.float32)
    hidden = (jax.nn.silu(group_norm(source, gain_one, count)) * mask).astype(jnp.bfloat16)
    first = (channel_conv(causal_pad(hidden), weight_one) * mask).astype(jnp.bfloat16)
    first = lax.optimization_barrier(first)
    hidden_two = (
        jax.nn.silu(group_norm(first.astype(jnp.float32), gain_two, count)) * mask
    ).astype(jnp.bfloat16)
    second = channel_conv(causal_pad(hidden_two), weight_two)
    result = ((source + second) * mask).astype(jnp.bfloat16)
    larger = upscale(result)
    own = larger[:, :, : 2 * col_count]
    arrived = shifted(larger[:, :, 2 * col_count :], "tile", 1)
    ramp = blend_ramp(prior)[None, None, :, None]
    head = own[:, :, : 2 * INTERSECTION].astype(jnp.float32) * ramp + arrived.astype(
        jnp.float32
    ) * (1.0 - ramp)
    return jnp.concatenate([head.astype(jnp.bfloat16), own[:, :, 2 * INTERSECTION :]], axis=2)


def normalized(values, gain, count, mask):
    chans = values.shape[-1]
    group_size = CH // GROUPS
    rows = lax.broadcasted_iota(jnp.int32, (chans, chans), 0) // group_size
    cols = lax.broadcasted_iota(jnp.int32, (chans, chans), 1) // group_size
    same = (rows == cols).astype(jnp.float32)
    total = jnp.sum(values, axis=(0, 1, 2)).reshape(1, chans)
    square = jnp.sum(values * values, axis=(0, 1, 2)).reshape(1, chans)
    both = jnp.concatenate([jnp.broadcast_to(total, (8, chans)), jnp.broadcast_to(square, (8, chans))], 0)
    sums = jnp.dot(both, same, precision=lax.Precision.HIGHEST, preferred_element_type=jnp.float32)
    size = count * group_size
    mean = sums[0:1] / size
    variance = sums[8:9] / size - mean * mean
    rate = lax.rsqrt(variance + eps)
    shape = (1, 1, 1, chans)
    scaled = (values - mean.reshape(shape)) * rate.reshape(shape) * gain.reshape(shape)
    return (scaled / (1.0 + jnp.exp(-scaled))) * mask


def column_mask(cols, limit):
    ids = lax.broadcasted_iota(jnp.int32, (1, cols, 8, LANES), 1)
    return (ids < limit).astype(jnp.float32)


def window_limit(extents_ref, cols):
    place = lax.axis_index("tile")
    reach = jnp.where(place == lax.axis_size("tile") - 1, 0, extents_ref[place])
    return cols - INTERSECTION + reach


def owner_of(slot):
    step = (slot + 1) // 2
    ahead = (lax.axis_index("sub") == 0) == (slot % 2 == 0)
    return lax.axis_index("tile") + jnp.where(ahead, step, -step)


def prepare(limit, gain_refs, win_refs, h_ref, source_ref):
    clip, chan = lax.axis_index("groups"), lax.axis_index("chan")
    frames, cols, rows, width = win_refs[0].shape
    count = limit.astype(jnp.float32) * (2 * frames * rows)
    mask = column_mask(cols, limit)
    for away, gain_ref in enumerate(gain_refs):
        for piece in range(width // LANES):
            lanes = slice(piece * LANES, (piece + 1) * LANES)
            both = [win_refs[2 * turn + away][:, :, :, lanes] for turn in range(2)]
            values = jnp.concatenate(both, 0).astype(jnp.float32)
            values = jnp.where(mask > 0, values, 0.0)
            done = normalized(values, gain_ref[:, lanes], count, mask).astype(jnp.bfloat16)
            block = (chan ^ away) * (width // LANES) + piece
            for turn in range(2):
                rows_at = pl.ds((clip ^ turn) * frames, frames)
                h_ref[block, rows_at] = done[turn * frames : (turn + 1) * frames]
                if away == 0:

                    @pl.when(clip == piece)
                    def _(rows_at=rows_at, turn=turn, both=both):
                        source_ref[rows_at] = both[turn]


def fill_patches(h_ref, block, patch_ref):
    frames, cols, rows, width = h_ref.shape[1:]
    ids = lax.broadcasted_iota(jnp.int32, (cols, rows, width), 1)
    empty = jnp.zeros((rows, width), jnp.float32)
    for t in range(frames):
        here = h_ref[block, t].astype(jnp.float32)
        for b in range(3):
            if b == 1:
                moved = here
            else:
                moved = pltpu.roll(here, 1 if b == 0 else rows - 1, 1)
                moved = jnp.where(ids == (0 if b == 0 else rows - 1), 0.0, moved)
            flat = moved.reshape(cols * rows, width)
            for d in range(3):
                if d == 0:
                    piece = jnp.concatenate([empty, flat], 0)
                elif d == 1:
                    piece = jnp.concatenate([flat, empty], 0)
                else:
                    piece = jnp.concatenate([flat[rows:], empty, empty], 0)
                piece = piece.astype(jnp.bfloat16)
                lane = (b * 3 + d) * width
                patch_ref[t + 2, :, lane : lane + width] = piece
                if t == 0:
                    patch_ref[0, :, lane : lane + width] = piece
                    patch_ref[1, :, lane : lane + width] = piece


def add_block(h_ref, block, weight_ref, patch_ref, wide_ref, acc_ref):
    fill_patches(h_ref, block, patch_ref)
    frames = h_ref.shape[1]
    pitch, depth = patch_ref.shape[1:]
    both = jnp.concatenate([weight_ref[0], weight_ref[1]], axis=1)
    left = patch_ref[: frames + 1].reshape((frames + 1) * pitch, depth)
    wide_ref[...] += jnp.dot(left, both, preferred_element_type=jnp.float32)
    left = patch_ref[2:].reshape(frames * pitch, depth)
    acc_ref[...] += jnp.dot(left, weight_ref[2], preferred_element_type=jnp.float32)


def weight_copies(slots, weight_refs, held_ref, sem_ref):
    copies = []
    for i, (slot, weight_ref) in enumerate(zip(slots, weight_refs)):
        owner = owner_of(slot)
        there = (owner >= 0) & (owner < lax.axis_size("tile"))
        copy = pltpu.make_async_copy(weight_ref, held_ref.at[i], sem_ref.at[i])
        copies.append((owner, there, copy))
    return copies


def start_weights(copies):
    for _, there, copy in copies:

        @pl.when(there)
        def _(copy=copy):
            copy.start()


def add_blocks(copies, h_ref, held_ref, patch_ref, wide_ref, acc_ref):
    wide_ref[...] = jnp.zeros_like(wide_ref)
    for i, (owner, there, copy) in enumerate(copies):

        @pl.when(there)
        def _(i=i, owner=owner, copy=copy):
            copy.wait()
            add_block(h_ref, owner, held_ref.at[i], patch_ref, wide_ref, acc_ref)

    shift = patch_ref.shape[1]
    count = acc_ref.shape[0]
    acc_ref[...] += wide_ref[:count, :LANES] + wide_ref[shift : shift + count, LANES:]


def result_of(acc_ref, frames, cols, rows):
    pitch = acc_ref.shape[0] // frames
    whole = acc_ref[...].reshape(frames, pitch, LANES)
    return whole[:, : cols * rows].reshape(frames, cols, rows, LANES)


def fetch_blocks(near_refs, h_ref, sem_ref):
    own = lax.axis_index("chan") * 2 + lax.axis_index("groups")
    copies = [
        pltpu.make_async_copy(near_ref, h_ref.at[own ^ code], sem_ref.at[code])
        for code, near_ref in enumerate(near_refs)
    ]
    for copy in copies:
        copy.start()
    return copies


def first_begin(slots, extents_ref, gain_ref, far_gain_ref, *refs):
    win_refs, weight_refs = refs[:4], refs[4 : 4 + len(slots)]
    h_ref, source_ref, acc_ref, patch_ref, wide_ref, held_ref, sem_ref = refs[4 + len(slots) :]
    copies = weight_copies(slots, weight_refs, held_ref, sem_ref)
    start_weights(copies)
    limit = window_limit(extents_ref, h_ref.shape[2])
    prepare(limit, (gain_ref, far_gain_ref), win_refs, h_ref, source_ref)
    acc_ref[...] = jnp.zeros_like(acc_ref)
    add_blocks(copies, h_ref, held_ref, patch_ref, wide_ref, acc_ref)


def first_end(slots, extents_ref, gain_ref, h_ref, begun_ref, *refs):
    weight_refs = refs[: len(slots)]
    out_ref, acc_ref, patch_ref, wide_ref, held_ref, sem_ref = refs[len(slots) :]
    copies = weight_copies(slots, weight_refs, held_ref, sem_ref)
    start_weights(copies)
    acc_ref[...] = begun_ref[...]
    add_blocks(copies, h_ref, held_ref, patch_ref, wide_ref, acc_ref)
    frames, cols, rows = h_ref.shape[1:4]
    limit = window_limit(extents_ref, cols)
    mask = column_mask(cols, limit)
    count = limit.astype(jnp.float32) * (frames * rows)
    first = (result_of(acc_ref, frames, cols, rows) * mask).astype(jnp.bfloat16)
    share = pl.multiple_of(lax.axis_index("groups") * LANES, LANES)
    gain = gain_ref[:, pl.ds(share, LANES)]
    done = normalized(first.astype(jnp.float32), gain, count, mask)
    out_ref[...] = done.astype(jnp.bfloat16)


def second_begin(slots, *refs):
    near_refs, weight_refs = refs[:4], refs[4 : 4 + len(slots)]
    acc_ref, h_ref, h_sem_ref, patch_ref, wide_ref, held_ref, sem_ref = refs[4 + len(slots) :]
    fetched = fetch_blocks(near_refs, h_ref, h_sem_ref)
    copies = weight_copies(slots, weight_refs, held_ref, sem_ref)
    start_weights(copies)
    acc_ref[...] = jnp.zeros_like(acc_ref)
    for copy in fetched:
        copy.wait()
    add_blocks(copies, h_ref, held_ref, patch_ref, wide_ref, acc_ref)


def second_end(slots, extents_ref, source_ref, begun_ref, *refs):
    near_refs, weight_refs = refs[:4], refs[4 : 4 + len(slots)]
    out_refs, rest = refs[4 + len(slots) : 8 + len(slots)], refs[8 + len(slots) :]
    done_ref, acc_ref, h_ref, h_sem_ref, patch_ref, wide_ref, held_ref, sem_ref = rest
    fetched = fetch_blocks(near_refs, h_ref, h_sem_ref)
    copies = weight_copies(slots, weight_refs, held_ref, sem_ref)
    start_weights(copies)
    acc_ref[...] = begun_ref[...]
    for copy in fetched:
        copy.wait()
    add_blocks(copies, h_ref, held_ref, patch_ref, wide_ref, acc_ref)
    frames, cols, rows = h_ref.shape[1:4]
    mask = column_mask(cols, window_limit(extents_ref, cols))
    source = source_ref[...].astype(jnp.float32)
    done = (source + result_of(acc_ref, frames, cols, rows)) * mask
    done_ref[...] = done.astype(jnp.bfloat16)
    half, kept = frames // 2, cols - INTERSECTION
    for turn in range(2):
        rows_at = pl.ds((lax.axis_index("groups") ^ turn) * half, half)
        out_refs[turn][...] = done_ref[rows_at, :kept]
        out_refs[2 + turn][...] = done_ref[rows_at, kept:]


def relayed(weight):
    tiles, subs = lax.axis_size("tile"), lax.axis_size("sub")
    out_share = weight.shape[4] // lax.axis_size("groups")
    own = lax.dynamic_slice_in_dim(weight, lax.axis_index("groups") * out_share, out_share, 4)
    own = own.reshape(3, -1, out_share)
    held, pieces = own, [own]
    for step in range(1, tiles):
        pairs = [(z * subs, (z + 1) * subs) for z in range(step - 1, tiles - 1)]
        pairs += [(z * subs + 1, (z - 1) * subs + 1) for z in range(1, tiles - step + 1)]
        held = lax.ppermute(held, ("tile", "sub"), pairs)
        pieces += [held, lax.ppermute(held, "sub", [(0, 1), (1, 0)])]
    return pieces


def by_distance(array):
    got = [array]
    for code in range(1, 4):
        pairs = [(i, i ^ code) for i in range(4)]
        got.append(lax.ppermute(array, ("groups", "chan"), pairs))
    return got


def share_plan(latent, extents, gain_one, weight_one, gain_two, weight_two):
    frame_count, row_count, col_count, chan_count = latent.shape
    tiles, clips = lax.axis_size("tile"), lax.axis_size("groups")
    sub = lax.axis_index("sub")
    _, prior = reach_and_prior(extents)
    span = col_count + INTERSECTION
    share = chan_count // clips
    frames = clips * frame_count
    pitch = (span + 1) * row_count
    taps = weight_one.shape[1] * weight_one.shape[2]
    vmem, smem = pl.BlockSpec(memory_space=pltpu.VMEM), pl.BlockSpec(memory_space=pltpu.SMEM)
    anywhere = pl.BlockSpec(memory_space=pl.ANY)
    final = jax.ShapeDtypeStruct((frames, span, row_count, share), jnp.bfloat16)
    blocks = jax.ShapeDtypeStruct((tiles,) + final.shape, jnp.bfloat16)
    total = jax.ShapeDtypeStruct((frames * pitch, share), jnp.float32)

    def scratch(slots):
        return [
            pltpu.VMEM((frames + 2, pitch, taps * LANES), jnp.bfloat16),
            pltpu.VMEM(((frames + 1) * pitch, 2 * share), jnp.float32),
            pltpu.VMEM((len(slots), 3, taps * LANES, share), jnp.bfloat16),
            pltpu.SemaphoreType.DMA((len(slots),)),
        ]

    def chosen(weights, slots):
        return [weights[slot] for slot in slots]

    h_scratch = [pltpu.VMEM(blocks.shape, jnp.bfloat16), pltpu.SemaphoreType.DMA((tiles,))]
    acc_scratch = [pltpu.VMEM(total.shape, jnp.float32)]

    by_col = jnp.transpose(latent, (0, 2, 1, 3))
    incoming = shifted(by_col[:, :INTERSECTION], "tile", -1)
    window = jnp.concatenate([by_col, incoming], axis=1)
    windows = []
    for turn in range(2):
        for away in range(2):
            pairs = [
                ((c * 2 + (x ^ away)) * 2 + (g ^ turn), (g * 2 + x) * 2 + c)
                for g in range(2)
                for x in range(2)
                for c in range(2)
            ]
            windows.append(lax.ppermute(window, ("groups", "chan", "sub"), pairs))
    first_weights = relayed(weight_one)
    second_weights = relayed(weight_two)
    own_gain = gain_one.reshape(1, -1)
    other_gain = lax.ppermute(own_gain, "chan", [(0, 1), (1, 0)])
    slots = tuple(range(2 * tiles - 1))
    early, late = slots[:FIRST_SPLIT], slots[FIRST_SPLIT:]
    hidden, source, begun = pl.pallas_call(
        functools.partial(first_begin, early),
        out_shape=(blocks, final, total),
        in_specs=[smem] + [vmem] * 6 + [anywhere] * len(early),
        out_specs=(vmem,) * 3,
        scratch_shapes=scratch(early),
        compiler_params=pltpu.CompilerParams(vmem_limit_bytes=GRANT),
    )(extents, own_gain, other_gain, *windows, *chosen(first_weights, early))
    hidden_two = pl.pallas_call(
        functools.partial(first_end, late),
        out_shape=final,
        in_specs=[smem] + [vmem] * 3 + [anywhere] * len(late),
        out_specs=vmem,
        scratch_shapes=acc_scratch + scratch(late),
        compiler_params=pltpu.CompilerParams(vmem_limit_bytes=GRANT),
    )(extents, gain_two.reshape(1, -1), hidden, begun, *chosen(first_weights, late))
    near = by_distance(hidden_two)
    near = [near[0], near[2], near[1], near[3]]
    early, late = slots[:SECOND_SPLIT], slots[SECOND_SPLIT:]
    begun = pl.pallas_call(
        functools.partial(second_begin, early),
        out_shape=total,
        in_specs=[anywhere] * (tiles + len(early)),
        out_specs=vmem,
        scratch_shapes=h_scratch + scratch(early),
        compiler_params=pltpu.CompilerParams(vmem_limit_bytes=GRANT),
    )(*near, *chosen(second_weights, early))
    kept = jax.ShapeDtypeStruct((frame_count, col_count, row_count, share), jnp.bfloat16)
    passed = jax.ShapeDtypeStruct((frame_count, INTERSECTION, row_count, share), jnp.bfloat16)
    parts = pl.pallas_call(
        functools.partial(second_end, late),
        out_shape=(kept, kept, passed, passed),
        in_specs=[smem] + [vmem] * 2 + [anywhere] * (tiles + len(late)),
        out_specs=(vmem,) * 4,
        scratch_shapes=[pltpu.VMEM(final.shape, jnp.bfloat16)]
        + acc_scratch
        + h_scratch
        + scratch(late),
        compiler_params=pltpu.CompilerParams(vmem_limit_bytes=GRANT),
    )(extents, source, begun, *near, *chosen(second_weights, late))

    owned, tails = [], []
    for turn in range(2):
        onward = [
            ((g * tiles + z) * 2 + c, (c * tiles + z + 1) * 2 + (g ^ turn))
            for g in range(2)
            for z in range(tiles - 1)
            for c in range(2)
        ]
        tails.append(
            lax.ppermute(parts[2 + turn], ("groups", "tile", "sub"), onward)
        )
    for turn in range(2):
        pairs = [(g * 2 + c, c * 2 + (g ^ turn)) for g in range(2) for c in range(2)]
        owned.append(lax.ppermute(parts[turn], ("groups", "sub"), pairs))

    def joined(pair):
        straight = jnp.concatenate(pair, axis=3)
        crossed = jnp.concatenate(pair[::-1], axis=3)
        return jnp.where(sub == 0, straight, crossed)

    own, tail = joined(owned), joined(tails)
    ramp = blend_ramp(prior)[None, :, None, None]
    head = jnp.repeat(own[:, :INTERSECTION].astype(jnp.float32), 2, axis=1) * ramp + jnp.repeat(
        tail.astype(jnp.float32), 2, axis=1
    ) * (1.0 - ramp)
    rest = jnp.repeat(own[:, INTERSECTION:], 2, axis=1)
    decoded = jnp.concatenate([head.astype(jnp.bfloat16), rest], axis=1)
    decoded = jnp.repeat(decoded, 2, axis=2)
    return jnp.transpose(decoded, (0, 2, 1, 3))


def solution(mesh):
    placed = (
        P(("groups", "sub"), None, "tile", "chan"),
        P(),
        P("chan"),
        P(None, None, None, "tile", "chan"),
        P("chan"),
        P(None, None, None, "tile", "chan"),
    )
    sizes = mesh.shape
    pairs_up = sizes["groups"] == 2 and sizes["sub"] == 2 and sizes["chan"] == 2
    few = pairs_up and CH // sizes["tile"] == LANES

    def body(*arrays):
        return (share_plan if few else gather_plan)(*arrays)

    return jax.shard_map(
        body,
        mesh=mesh,
        in_specs=placed,
        out_specs=P(("groups", "sub"), None, "tile", "chan"),
        check_vma=False,
    )
```

```python
import functools

import jax
import jax.numpy as jnp
from jax import lax
from jax.experimental import pallas as pl
from jax.experimental.pallas import tpu as pltpu
from jax.sharding import PartitionSpec as P


CH = 512
GROUPS = 32
INTERSECTION = 4
LANES = 128
GRANT = 14 * 2**20
FIRST_SPLIT = 5
SECOND_SPLIT = 5


eps = 1e-06


def shifted(array, axis, by):
    peers = lax.axis_size(axis)
    pairs = [(i, i + by) for i in range(peers) if 0 <= i + by < peers]
    return lax.ppermute(array, axis, pairs)


def blend_ramp(prior):
    positions = jnp.arange(2 * INTERSECTION).astype(jnp.float32) + 0.5
    limit = (2 * prior).astype(jnp.float32)[..., None]
    denom = (2 * jnp.maximum(prior, 1)).astype(jnp.float32)[..., None]
    return jnp.where(positions < limit, positions / denom, 1.0)


def convolve(inputs, kernel):
    result = lax.conv_general_dilated(
        inputs[None],
        kernel,
        (1, 1, 1),
        [(0, 0), (1, 1), (1, 1)],
        dimension_numbers=("NDHWC", "DHWIO", "NDHWC"),
        preferred_element_type=jnp.float32,
    )
    return result[0]


def group_norm(values, gain, count):
    group_size = CH // GROUPS
    grouped = values.reshape(values.shape[:-1] + (values.shape[-1] // group_size, group_size))
    totals, squares = lax.psum(
        (jnp.sum(grouped, axis=(0, 1, 2, 4)), jnp.sum(grouped * grouped, axis=(0, 1, 2, 4))), "sub"
    )
    size = count * group_size
    mean_val = totals / size
    variance = squares / size - mean_val * mean_val
    scaled = (grouped - mean_val[:, None]) * lax.rsqrt(variance + eps)[:, None]
    return scaled.reshape(values.shape) * gain


def causal_pad(values):
    earlier = shifted(values[-2:], "sub", 1)
    repeated = jnp.concatenate([values[:1], values[:1]], axis=0)
    leading = jnp.where(lax.axis_index("sub") == 0, repeated, earlier)
    return jnp.concatenate([leading, values], axis=0)


def channel_conv(padded_in, weight):
    full_in = lax.all_gather(padded_in, "chan", axis=3, tiled=True)
    out_count = weight.shape[4]
    share = weight.shape[3] // lax.axis_size("sub")
    portion = lax.dynamic_slice_in_dim(weight, lax.axis_index("sub") * share, share, 3)
    fetched = lax.all_gather(portion, "tile", axis=3, tiled=True)
    sectioned = fetched.reshape(3, 3, 3, lax.axis_size("tile"), 1, share, out_count)
    whole = lax.all_gather(sectioned, "sub", axis=4, tiled=True).reshape(3, 3, 3, -1, out_count)
    return convolve(full_in, whole)


def upscale(values):
    return jnp.repeat(jnp.repeat(values, 2, axis=1), 2, axis=2)


def reach_and_prior(extents):
    tile_count = lax.axis_size("tile")
    place = lax.axis_index("tile")
    tile_ids = jnp.arange(tile_count, dtype=jnp.int32)
    reaches = jnp.where(tile_ids == tile_count - 1, 0, extents)
    reach = jnp.sum(jnp.where(tile_ids == place, reaches, 0))
    prior = jnp.sum(jnp.where(tile_ids == place - 1, reaches, 0))
    return reach, prior


def gather_plan(latent, extents, gain_one, weight_one, gain_two, weight_two):
    frame_count, row_count, col_count, _ = latent.shape
    reach, prior = reach_and_prior(extents)
    incoming = shifted(latent[:, :, :INTERSECTION, :], "tile", -1)
    window = jnp.concatenate([latent, incoming], axis=2)
    valid = (jnp.arange(col_count + INTERSECTION, dtype=jnp.int32) < col_count + reach).astype(
        jnp.float32
    )
    mask = valid[None, None, :, None]
    window = jnp.where(mask > 0, window, jnp.zeros_like(window))
    count = (col_count + reach).astype(jnp.float32) * (
        frame_count * lax.axis_size("sub") * row_count
    )
    source = window.astype(jnp.float32)
    hidden = (jax.nn.silu(group_norm(source, gain_one, count)) * mask).astype(jnp.bfloat16)
    first = (channel_conv(causal_pad(hidden), weight_one) * mask).astype(jnp.bfloat16)
    first = lax.optimization_barrier(first)
    hidden_two = (
        jax.nn.silu(group_norm(first.astype(jnp.float32), gain_two, count)) * mask
    ).astype(jnp.bfloat16)
    second = channel_conv(causal_pad(hidden_two), weight_two)
    result = ((source + second) * mask).astype(jnp.bfloat16)
    larger = upscale(result)
    own = larger[:, :, : 2 * col_count]
    arrived = shifted(larger[:, :, 2 * col_count :], "tile", 1)
    ramp = blend_ramp(prior)[None, None, :, None]
    head = own[:, :, : 2 * INTERSECTION].astype(jnp.float32) * ramp + arrived.astype(
        jnp.float32
    ) * (1.0 - ramp)
    return jnp.concatenate([head.astype(jnp.bfloat16), own[:, :, 2 * INTERSECTION :]], axis=2)


def normalized(values, gain, count, mask):
    chans = values.shape[-1]
    group_size = CH // GROUPS
    rows = lax.broadcasted_iota(jnp.int32, (chans, chans), 0) // group_size
    cols = lax.broadcasted_iota(jnp.int32, (chans, chans), 1) // group_size
    same = (rows == cols).astype(jnp.float32)
    total = jnp.sum(values, axis=(0, 1, 2)).reshape(1, chans)
    square = jnp.sum(values * values, axis=(0, 1, 2)).reshape(1, chans)
    both = jnp.concatenate([jnp.broadcast_to(total, (8, chans)), jnp.broadcast_to(square, (8, chans))], 0)
    sums = jnp.dot(both, same, precision=lax.Precision.HIGHEST, preferred_element_type=jnp.float32)
    size = count * group_size
    mean = sums[0:1] / size
    variance = sums[8:9] / size - mean * mean
    rate = lax.rsqrt(variance + eps)
    shape = (1, 1, 1, chans)
    scaled = (values - mean.reshape(shape)) * rate.reshape(shape) * gain.reshape(shape)
    return (scaled / (1.0 + jnp.exp(-scaled))) * mask


def column_mask(cols, limit):
    ids = lax.broadcasted_iota(jnp.int32, (1, cols, 8, LANES), 1)
    return (ids < limit).astype(jnp.float32)


def window_limit(extents_ref, cols):
    place = lax.axis_index("tile")
    reach = jnp.where(place == lax.axis_size("tile") - 1, 0, extents_ref[place])
    return cols - INTERSECTION + reach


def owner_of(slot):
    step = (slot + 1) // 2
    ahead = (lax.axis_index("sub") == 0) == (slot % 2 == 1)
    return lax.axis_index("tile") + jnp.where(ahead, step, -step)


def prepare(limit, gain_refs, win_refs, h_ref, source_ref):
    clip, chan = lax.axis_index("groups"), lax.axis_index("chan")
    frames, cols, rows, width = win_refs[0].shape
    count = limit.astype(jnp.float32) * (2 * frames * rows)
    mask = column_mask(cols, limit)
    for away, gain_ref in enumerate(gain_refs):
        for piece in range(width // LANES):
            lanes = slice(piece * LANES, (piece + 1) * LANES)
            both = [win_refs[2 * turn + away][:, :, :, lanes] for turn in range(2)]
            values = jnp.concatenate(both, 0).astype(jnp.float32)
            values = jnp.where(mask > 0, values, 0.0)
            done = normalized(values, gain_ref[:, lanes], count, mask).astype(jnp.bfloat16)
            block = (chan ^ away) * (width // LANES) + piece
            for turn in range(2):
                rows_at = pl.ds((clip ^ turn) * frames, frames)
                h_ref[block, rows_at] = done[turn * frames : (turn + 1) * frames]
                if away == 0:

                    @pl.when(clip == piece)
                    def _(rows_at=rows_at, turn=turn, both=both):
                        source_ref[rows_at] = both[turn]


def fill_patches(h_ref, block, patch_ref):
    frames, cols, rows, width = h_ref.shape[1:]
    ids = lax.broadcasted_iota(jnp.int32, (cols, rows, width), 1)
    empty = jnp.zeros((rows, width), jnp.float32)
    for t in range(frames):
        here = h_ref[block, t].astype(jnp.float32)
        for b in range(3):
            if b == 1:
                moved = here
            else:
                moved = pltpu.roll(here, 1 if b == 0 else rows - 1, 1)
                moved = jnp.where(ids == (0 if b == 0 else rows - 1), 0.0, moved)
            flat = moved.reshape(cols * rows, width)
            for d in range(3):
                if d == 0:
                    piece = jnp.concatenate([empty, flat], 0)
                elif d == 1:
                    piece = jnp.concatenate([flat, empty], 0)
                else:
                    piece = jnp.concatenate([flat[rows:], empty, empty], 0)
                piece = piece.astype(jnp.bfloat16)
                lane = (b * 3 + d) * width
                patch_ref[t + 2, :, lane : lane + width] = piece
                if t == 0:
                    patch_ref[0, :, lane : lane + width] = piece
                    patch_ref[1, :, lane : lane + width] = piece


def add_block(h_ref, block, weight_ref, patch_ref, wide_ref, acc_ref):
    fill_patches(h_ref, block, patch_ref)
    frames = h_ref.shape[1]
    pitch, depth = patch_ref.shape[1:]
    both = jnp.concatenate([weight_ref[0], weight_ref[1]], axis=1)
    left = patch_ref[: frames + 1].reshape((frames + 1) * pitch, depth)
    wide_ref[...] += jnp.dot(left, both, preferred_element_type=jnp.float32)
    left = patch_ref[2:].reshape(frames * pitch, depth)
    acc_ref[...] += jnp.dot(left, weight_ref[2], preferred_element_type=jnp.float32)


def weight_copies(slots, weight_refs, held_ref, sem_ref):
    copies = []
    for i, slot in enumerate(slots):
        owner = owner_of(slot)
        there = (owner >= 0) & (owner < lax.axis_size("tile"))
        early_ref, late_ref = weight_refs[2 * i : 2 * i + 2]
        part = early_ref.shape[0]
        pair = (
            pltpu.make_async_copy(early_ref, held_ref.at[i, :part], sem_ref.at[i, 0]),
            pltpu.make_async_copy(late_ref, held_ref.at[i, part:], sem_ref.at[i, 1]),
        )
        copies.append((owner, there, pair))
    return copies


def start_weights(copies):
    for _, there, pair in copies:

        @pl.when(there)
        def _(pair=pair):
            for copy in pair:
                copy.start()


def add_blocks(copies, h_ref, held_ref, patch_ref, wide_ref, acc_ref):
    wide_ref[...] = jnp.zeros_like(wide_ref)
    for i, (owner, there, pair) in enumerate(copies):

        @pl.when(there)
        def _(i=i, owner=owner, pair=pair):
            for copy in pair:
                copy.wait()
            add_block(h_ref, owner, held_ref.at[i], patch_ref, wide_ref, acc_ref)

    shift = patch_ref.shape[1]
    count = acc_ref.shape[0]
    acc_ref[...] += wide_ref[:count, :LANES] + wide_ref[shift : shift + count, LANES:]


def result_of(acc_ref, frames, cols, rows):
    pitch = acc_ref.shape[0] // frames
    whole = acc_ref[...].reshape(frames, pitch, LANES)
    return whole[:, : cols * rows].reshape(frames, cols, rows, LANES)


def fetch_blocks(near_refs, h_ref, sem_ref):
    own = lax.axis_index("chan") * 2 + lax.axis_index("groups")
    copies = [
        pltpu.make_async_copy(near_ref, h_ref.at[own ^ code], sem_ref.at[code])
        for code, near_ref in enumerate(near_refs)
    ]
    for copy in copies:
        copy.start()
    return copies


def first_begin(slots, extents_ref, gain_ref, far_gain_ref, *refs):
    used = 4 + 2 * len(slots)
    win_refs, weight_refs = refs[:4], refs[4:used]
    h_ref, source_ref, acc_ref, patch_ref, wide_ref, held_ref, sem_ref = refs[used:]
    copies = weight_copies(slots, weight_refs, held_ref, sem_ref)
    start_weights(copies)
    limit = window_limit(extents_ref, h_ref.shape[2])
    prepare(limit, (gain_ref, far_gain_ref), win_refs, h_ref, source_ref)
    acc_ref[...] = jnp.zeros_like(acc_ref)
    add_blocks(copies, h_ref, held_ref, patch_ref, wide_ref, acc_ref)


def first_end(slots, extents_ref, gain_ref, h_ref, begun_ref, *refs):
    weight_refs = refs[: 2 * len(slots)]
    out_ref, acc_ref, patch_ref, wide_ref, held_ref, sem_ref = refs[2 * len(slots) :]
    copies = weight_copies(slots, weight_refs, held_ref, sem_ref)
    start_weights(copies)
    acc_ref[...] = begun_ref[...]
    add_blocks(copies, h_ref, held_ref, patch_ref, wide_ref, acc_ref)
    frames, cols, rows = h_ref.shape[1:4]
    limit = window_limit(extents_ref, cols)
    mask = column_mask(cols, limit)
    count = limit.astype(jnp.float32) * (frames * rows)
    first = (result_of(acc_ref, frames, cols, rows) * mask).astype(jnp.bfloat16)
    share = pl.multiple_of(lax.axis_index("groups") * LANES, LANES)
    gain = gain_ref[:, pl.ds(share, LANES)]
    done = normalized(first.astype(jnp.float32), gain, count, mask)
    out_ref[...] = done.astype(jnp.bfloat16)


def second_begin(slots, *refs):
    used = 4 + 2 * len(slots)
    near_refs, weight_refs = refs[:4], refs[4:used]
    h_ref, acc_ref, h_sem_ref, patch_ref, wide_ref, held_ref, sem_ref = refs[used:]
    fetched = fetch_blocks(near_refs, h_ref, h_sem_ref)
    copies = weight_copies(slots, weight_refs, held_ref, sem_ref)
    start_weights(copies)
    acc_ref[...] = jnp.zeros_like(acc_ref)
    for copy in fetched:
        copy.wait()
    add_blocks(copies, h_ref, held_ref, patch_ref, wide_ref, acc_ref)


def second_end(slots, extents_ref, h_ref, begun_ref, source_hbm_ref, *refs):
    used = 2 * len(slots)
    weight_refs, out_refs, rest = refs[:used], refs[used : used + 4], refs[used + 4 :]
    source_ref, source_sem, done_ref, acc_ref, patch_ref, wide_ref, held_ref, sem_ref = rest
    source_copy = pltpu.make_async_copy(source_hbm_ref, source_ref, source_sem)
    source_copy.start()
    copies = weight_copies(slots, weight_refs, held_ref, sem_ref)
    start_weights(copies)
    acc_ref[...] = begun_ref[...]
    add_blocks(copies, h_ref, held_ref, patch_ref, wide_ref, acc_ref)
    frames, cols, rows = h_ref.shape[1:4]
    mask = column_mask(cols, window_limit(extents_ref, cols))
    source_copy.wait()
    source = source_ref[...].astype(jnp.float32)
    done = (source + result_of(acc_ref, frames, cols, rows)) * mask
    done_ref[...] = done.astype(jnp.bfloat16)
    half, kept = frames // 2, cols - INTERSECTION
    for turn in range(2):
        rows_at = pl.ds((lax.axis_index("groups") ^ turn) * half, half)
        out_refs[turn][...] = done_ref[rows_at, :kept]
        out_refs[2 + turn][...] = done_ref[rows_at, kept:]


def relayed(weight):
    tiles, subs = lax.axis_size("tile"), lax.axis_size("sub")
    out_share = weight.shape[4] // lax.axis_size("groups")
    own = lax.dynamic_slice_in_dim(weight, lax.axis_index("groups") * out_share, out_share, 4)
    own = own.reshape(3, -1, out_share)
    held = [own[:2], own[2:]]
    pieces = [tuple(held)]
    for step in range(1, tiles):
        pairs = [(z * subs, (z + 1) * subs + 1) for z in range(step - 1, tiles - 1)]
        pairs += [(z * subs + 1, (z - 1) * subs) for z in range(1, tiles - step + 1)]
        arrived = []
        for i in range(2):
            arrived.append(lax.ppermute(held[i], ("tile", "sub"), pairs))
            held[i] = lax.ppermute(arrived[i], "sub", [(0, 1), (1, 0)])
        pieces += [tuple(arrived), tuple(held)]
    return pieces


def by_distance(array):
    got = [array]
    for code in range(1, 4):
        pairs = [(i, i ^ code) for i in range(4)]
        got.append(lax.ppermute(array, ("groups", "chan"), pairs))
    return got


def share_plan(latent, extents, gain_one, weight_one, gain_two, weight_two):
    frame_count, row_count, col_count, chan_count = latent.shape
    tiles, clips = lax.axis_size("tile"), lax.axis_size("groups")
    sub = lax.axis_index("sub")
    _, prior = reach_and_prior(extents)
    span = col_count + INTERSECTION
    share = chan_count // clips
    frames = clips * frame_count
    pitch = (span + 1) * row_count
    taps = weight_one.shape[1] * weight_one.shape[2]
    vmem, smem = pl.BlockSpec(memory_space=pltpu.VMEM), pl.BlockSpec(memory_space=pltpu.SMEM)
    anywhere = pl.BlockSpec(memory_space=pl.ANY)
    in_hbm = pl.BlockSpec(memory_space=pltpu.HBM)
    final = jax.ShapeDtypeStruct((frames, span, row_count, share), jnp.bfloat16)
    blocks = jax.ShapeDtypeStruct((tiles,) + final.shape, jnp.bfloat16)
    total = jax.ShapeDtypeStruct((frames * pitch, share), jnp.float32)

    def scratch(slots):
        return [
            pltpu.VMEM((frames + 2, pitch, taps * LANES), jnp.bfloat16),
            pltpu.VMEM(((frames + 1) * pitch, 2 * share), jnp.float32),
            pltpu.VMEM((len(slots), 3, taps * LANES, share), jnp.bfloat16),
            pltpu.SemaphoreType.DMA((len(slots), 2)),
        ]

    def chosen(weights, slots):
        return [chunk for slot in slots for chunk in weights[slot]]

    acc_scratch = [pltpu.VMEM(total.shape, jnp.float32)]

    by_col = jnp.transpose(latent, (0, 2, 1, 3))
    incoming = shifted(by_col[:, :INTERSECTION], "tile", -1)
    window = jnp.concatenate([by_col, incoming], axis=1)
    windows = []
    for turn in range(2):
        for away in range(2):
            pairs = [
                ((c * 2 + (x ^ away)) * 2 + (g ^ turn), (g * 2 + x) * 2 + c)
                for g in range(2)
                for x in range(2)
                for c in range(2)
            ]
            windows.append(lax.ppermute(window, ("groups", "chan", "sub"), pairs))
    first_weights = relayed(weight_one)
    second_weights = relayed(weight_two)
    own_gain = gain_one.reshape(1, -1)
    other_gain = lax.ppermute(own_gain, "chan", [(0, 1), (1, 0)])
    slots = tuple(range(2 * tiles - 1))
    early, late = slots[:FIRST_SPLIT], slots[FIRST_SPLIT:]
    hidden, source, begun = pl.pallas_call(
        functools.partial(first_begin, early),
        out_shape=(blocks, final, total),
        in_specs=[smem] + [vmem] * 6 + [anywhere] * (2 * len(early)),
        out_specs=(vmem,) * 3,
        scratch_shapes=scratch(early),
        compiler_params=pltpu.CompilerParams(vmem_limit_bytes=GRANT),
    )(extents, own_gain, other_gain, *windows, *chosen(first_weights, early))
    hidden_two = pl.pallas_call(
        functools.partial(first_end, late),
        out_shape=final,
        in_specs=[smem] + [vmem] * 3 + [anywhere] * (2 * len(late)),
        out_specs=vmem,
        scratch_shapes=acc_scratch + scratch(late),
        compiler_params=pltpu.CompilerParams(vmem_limit_bytes=GRANT),
    )(extents, gain_two.reshape(1, -1), hidden, begun, *chosen(first_weights, late))
    near = by_distance(hidden_two)
    near = [near[0], near[2], near[1], near[3]]
    early, late = slots[:SECOND_SPLIT], slots[SECOND_SPLIT:]
    gathered, begun = pl.pallas_call(
        functools.partial(second_begin, early),
        out_shape=(blocks, total),
        in_specs=[anywhere] * (tiles + 2 * len(early)),
        out_specs=(vmem, vmem),
        scratch_shapes=[pltpu.SemaphoreType.DMA((tiles,))] + scratch(early),
        compiler_params=pltpu.CompilerParams(vmem_limit_bytes=GRANT),
    )(*near, *chosen(second_weights, early))
    kept = jax.ShapeDtypeStruct((frame_count, col_count, row_count, share), jnp.bfloat16)
    passed = jax.ShapeDtypeStruct((frame_count, INTERSECTION, row_count, share), jnp.bfloat16)
    parts = pl.pallas_call(
        functools.partial(second_end, late),
        out_shape=(kept, kept, passed, passed),
        in_specs=[smem, vmem, vmem, in_hbm] + [anywhere] * (2 * len(late)),
        out_specs=(vmem,) * 4,
        scratch_shapes=[
            pltpu.VMEM(final.shape, jnp.bfloat16),
            pltpu.SemaphoreType.DMA,
            pltpu.VMEM(final.shape, jnp.bfloat16),
        ]
        + acc_scratch
        + scratch(late),
        compiler_params=pltpu.CompilerParams(vmem_limit_bytes=GRANT),
    )(extents, gathered, begun, source, *chosen(second_weights, late))

    owned, tails = [], []
    for turn in range(2):
        onward = [
            ((g * tiles + z) * 2 + c, (c * tiles + z + 1) * 2 + (g ^ turn))
            for g in range(2)
            for z in range(tiles - 1)
            for c in range(2)
        ]
        tails.append(
            lax.ppermute(parts[2 + turn], ("groups", "tile", "sub"), onward)
        )
    for turn in range(2):
        pairs = [(g * 2 + c, c * 2 + (g ^ turn)) for g in range(2) for c in range(2)]
        owned.append(lax.ppermute(parts[turn], ("groups", "sub"), pairs))

    def joined(pair):
        straight = jnp.concatenate(pair, axis=3)
        crossed = jnp.concatenate(pair[::-1], axis=3)
        return jnp.where(sub == 0, straight, crossed)

    own, tail = joined(owned), joined(tails)
    ramp = blend_ramp(prior)[None, :, None, None]
    head = jnp.repeat(own[:, :INTERSECTION].astype(jnp.float32), 2, axis=1) * ramp + jnp.repeat(
        tail.astype(jnp.float32), 2, axis=1
    ) * (1.0 - ramp)
    rest = jnp.repeat(own[:, INTERSECTION:], 2, axis=1)
    decoded = jnp.concatenate([head.astype(jnp.bfloat16), rest], axis=1)
    decoded = jnp.repeat(decoded, 2, axis=2)
    return jnp.transpose(decoded, (0, 2, 1, 3))


def solution(mesh):
    placed = (
        P(("groups", "sub"), None, "tile", "chan"),
        P(),
        P("chan"),
        P(None, None, None, "tile", "chan"),
        P("chan"),
        P(None, None, None, "tile", "chan"),
    )
    sizes = mesh.shape
    pairs_up = sizes["groups"] == 2 and sizes["sub"] == 2 and sizes["chan"] == 2
    few = pairs_up and CH // sizes["tile"] == LANES

    def body(*arrays):
        return (share_plan if few else gather_plan)(*arrays)

    return jax.shard_map(
        body,
        mesh=mesh,
        in_specs=placed,
        out_specs=P(("groups", "sub"), None, "tile", "chan"),
        check_vma=False,
    )
```

```python
import functools

import jax
import jax.numpy as jnp
from jax import lax
from jax.experimental import pallas as pl
from jax.experimental.pallas import tpu as pltpu
from jax.sharding import PartitionSpec as P


CH = 512
GROUPS = 32
INTERSECTION = 4
LANES = 128
GRANT = 12 * 2**20
LAST_GRANT = 60 * 2**20
FIRST_SPLIT = 3


eps = 1e-06


def shifted(array, axis, by):
    peers = lax.axis_size(axis)
    pairs = [(i, i + by) for i in range(peers) if 0 <= i + by < peers]
    return lax.ppermute(array, axis, pairs)


def blend_ramp(prior):
    positions = jnp.arange(2 * INTERSECTION).astype(jnp.float32) + 0.5
    limit = (2 * prior).astype(jnp.float32)[..., None]
    denom = (2 * jnp.maximum(prior, 1)).astype(jnp.float32)[..., None]
    return jnp.where(positions < limit, positions / denom, 1.0)


def convolve(inputs, kernel):
    result = lax.conv_general_dilated(
        inputs[None],
        kernel,
        (1, 1, 1),
        [(0, 0), (1, 1), (1, 1)],
        dimension_numbers=("NDHWC", "DHWIO", "NDHWC"),
        preferred_element_type=jnp.float32,
    )
    return result[0]


def group_norm(values, gain, count):
    group_size = CH // GROUPS
    grouped = values.reshape(values.shape[:-1] + (values.shape[-1] // group_size, group_size))
    totals, squares = lax.psum(
        (jnp.sum(grouped, axis=(0, 1, 2, 4)), jnp.sum(grouped * grouped, axis=(0, 1, 2, 4))), "sub"
    )
    size = count * group_size
    mean_val = totals / size
    variance = squares / size - mean_val * mean_val
    scaled = (grouped - mean_val[:, None]) * lax.rsqrt(variance + eps)[:, None]
    return scaled.reshape(values.shape) * gain


def causal_pad(values):
    earlier = shifted(values[-2:], "sub", 1)
    repeated = jnp.concatenate([values[:1], values[:1]], axis=0)
    leading = jnp.where(lax.axis_index("sub") == 0, repeated, earlier)
    return jnp.concatenate([leading, values], axis=0)


def channel_conv(padded_in, weight):
    full_in = lax.all_gather(padded_in, "chan", axis=3, tiled=True)
    out_count = weight.shape[4]
    share = weight.shape[3] // lax.axis_size("sub")
    portion = lax.dynamic_slice_in_dim(weight, lax.axis_index("sub") * share, share, 3)
    fetched = lax.all_gather(portion, "tile", axis=3, tiled=True)
    sectioned = fetched.reshape(3, 3, 3, lax.axis_size("tile"), 1, share, out_count)
    whole = lax.all_gather(sectioned, "sub", axis=4, tiled=True).reshape(3, 3, 3, -1, out_count)
    return convolve(full_in, whole)


def upscale(values):
    return jnp.repeat(jnp.repeat(values, 2, axis=1), 2, axis=2)


def reach_and_prior(extents):
    tile_count = lax.axis_size("tile")
    place = lax.axis_index("tile")
    tile_ids = jnp.arange(tile_count, dtype=jnp.int32)
    reaches = jnp.where(tile_ids == tile_count - 1, 0, extents)
    reach = jnp.sum(jnp.where(tile_ids == place, reaches, 0))
    prior = jnp.sum(jnp.where(tile_ids == place - 1, reaches, 0))
    return reach, prior


def gather_plan(latent, extents, gain_one, weight_one, gain_two, weight_two):
    frame_count, row_count, col_count, _ = latent.shape
    reach, prior = reach_and_prior(extents)
    incoming = shifted(latent[:, :, :INTERSECTION, :], "tile", -1)
    window = jnp.concatenate([latent, incoming], axis=2)
    valid = (jnp.arange(col_count + INTERSECTION, dtype=jnp.int32) < col_count + reach).astype(
        jnp.float32
    )
    mask = valid[None, None, :, None]
    window = jnp.where(mask > 0, window, jnp.zeros_like(window))
    count = (col_count + reach).astype(jnp.float32) * (
        frame_count * lax.axis_size("sub") * row_count
    )
    source = window.astype(jnp.float32)
    hidden = (jax.nn.silu(group_norm(source, gain_one, count)) * mask).astype(jnp.bfloat16)
    first = (channel_conv(causal_pad(hidden), weight_one) * mask).astype(jnp.bfloat16)
    first = lax.optimization_barrier(first)
    hidden_two = (
        jax.nn.silu(group_norm(first.astype(jnp.float32), gain_two, count)) * mask
    ).astype(jnp.bfloat16)
    second = channel_conv(causal_pad(hidden_two), weight_two)
    result = ((source + second) * mask).astype(jnp.bfloat16)
    larger = upscale(result)
    own = larger[:, :, : 2 * col_count]
    arrived = shifted(larger[:, :, 2 * col_count :], "tile", 1)
    ramp = blend_ramp(prior)[None, None, :, None]
    head = own[:, :, : 2 * INTERSECTION].astype(jnp.float32) * ramp + arrived.astype(
        jnp.float32
    ) * (1.0 - ramp)
    return jnp.concatenate([head.astype(jnp.bfloat16), own[:, :, 2 * INTERSECTION :]], axis=2)


def normalized(values, gain, count, mask):
    chans = values.shape[-1]
    group_size = CH // GROUPS
    rows = lax.broadcasted_iota(jnp.int32, (chans, chans), 0) // group_size
    cols = lax.broadcasted_iota(jnp.int32, (chans, chans), 1) // group_size
    same = (rows == cols).astype(jnp.float32)
    total = jnp.sum(values, axis=(0, 1, 2)).reshape(1, chans)
    square = jnp.sum(values * values, axis=(0, 1, 2)).reshape(1, chans)
    both = jnp.concatenate([jnp.broadcast_to(total, (8, chans)), jnp.broadcast_to(square, (8, chans))], 0)
    sums = jnp.dot(both, same, precision=lax.Precision.HIGHEST, preferred_element_type=jnp.float32)
    size = count * group_size
    mean = sums[0:1] / size
    variance = sums[8:9] / size - mean * mean
    rate = lax.rsqrt(variance + eps)
    shape = (1, 1, 1, chans)
    scaled = (values - mean.reshape(shape)) * rate.reshape(shape) * gain.reshape(shape)
    return (scaled / (1.0 + jnp.exp(-scaled))) * mask


def column_mask(cols, limit):
    ids = lax.broadcasted_iota(jnp.int32, (1, cols, 8, LANES), 1)
    return (ids < limit).astype(jnp.float32)


def window_limit(extents_ref, cols):
    place = lax.axis_index("tile")
    reach = jnp.where(place == lax.axis_size("tile") - 1, 0, extents_ref[place])
    return cols - INTERSECTION + reach


def owner_of(slot):
    step = (slot + 1) // 2
    ahead = (lax.axis_index("sub") == 0) == (slot % 2 == 1)
    return lax.axis_index("tile") + jnp.where(ahead, step, -step)


def prepare(limit, gain_refs, win_refs, h_ref, source_ref):
    clip, chan = lax.axis_index("groups"), lax.axis_index("chan")
    frames, cols, rows, width = win_refs[0].shape
    count = limit.astype(jnp.float32) * (2 * frames * rows)
    mask = column_mask(cols, limit)
    for away, gain_ref in enumerate(gain_refs):
        for piece in range(width // LANES):
            lanes = slice(piece * LANES, (piece + 1) * LANES)
            both = [win_refs[2 * turn + away][:, :, :, lanes] for turn in range(2)]
            values = jnp.concatenate(both, 0).astype(jnp.float32)
            values = jnp.where(mask > 0, values, 0.0)
            done = normalized(values, gain_ref[:, lanes], count, mask).astype(jnp.bfloat16)
            block = (chan ^ away) * (width // LANES) + piece
            for turn in range(2):
                rows_at = pl.ds((clip ^ turn) * frames, frames)
                h_ref[block, rows_at] = done[turn * frames : (turn + 1) * frames]
                if away == 0:

                    @pl.when(clip == piece)
                    def _(rows_at=rows_at, turn=turn, both=both):
                        source_ref[rows_at] = both[turn]


def fill_patches(h_ref, block, patch_ref):
    frames, cols, rows, width = h_ref.shape[1:]
    ids = lax.broadcasted_iota(jnp.int32, (cols, rows, width), 1)
    empty = jnp.zeros((rows, width), jnp.float32)
    for t in range(frames):
        here = h_ref[block, t].astype(jnp.float32)
        for b in range(3):
            if b == 1:
                moved = here
            else:
                moved = pltpu.roll(here, 1 if b == 0 else rows - 1, 1)
                moved = jnp.where(ids == (0 if b == 0 else rows - 1), 0.0, moved)
            flat = moved.reshape(cols * rows, width)
            for d in range(3):
                if d == 0:
                    piece = jnp.concatenate([empty, flat], 0)
                elif d == 1:
                    piece = jnp.concatenate([flat, empty], 0)
                else:
                    piece = jnp.concatenate([flat[rows:], empty, empty], 0)
                piece = piece.astype(jnp.bfloat16)
                lane = (b * 3 + d) * width
                patch_ref[t + 2, :, lane : lane + width] = piece
                if t == 0:
                    patch_ref[0, :, lane : lane + width] = piece
                    patch_ref[1, :, lane : lane + width] = piece


def add_block(h_ref, block, weight_ref, patch_ref, wide_ref, acc_ref):
    fill_patches(h_ref, block, patch_ref)
    frames = h_ref.shape[1]
    pitch, depth = patch_ref.shape[1:]
    both = jnp.concatenate([weight_ref[0], weight_ref[1]], axis=1)
    left = patch_ref[: frames + 1].reshape((frames + 1) * pitch, depth)
    wide_ref[...] += jnp.dot(left, both, preferred_element_type=jnp.float32)
    left = patch_ref[2:].reshape(frames * pitch, depth)
    acc_ref[...] += jnp.dot(left, weight_ref[2], preferred_element_type=jnp.float32)


def weight_copies(slots, weight_refs, held_ref, sem_ref):
    copies = []
    for i, (slot, weight_ref) in enumerate(zip(slots, weight_refs)):
        owner = owner_of(slot)
        there = (owner >= 0) & (owner < lax.axis_size("tile"))
        copy = pltpu.make_async_copy(weight_ref, held_ref.at[i], sem_ref.at[i])
        copies.append((owner, there, copy))
    return copies


def start_weights(copies):
    for _, there, copy in copies:

        @pl.when(there)
        def _(copy=copy):
            copy.start()


def add_blocks(copies, h_ref, held_ref, patch_ref, wide_ref, acc_ref):
    wide_ref[...] = jnp.zeros_like(wide_ref)
    for i, (owner, there, copy) in enumerate(copies):

        @pl.when(there)
        def _(i=i, owner=owner, copy=copy):
            copy.wait()
            add_block(h_ref, owner, held_ref.at[i], patch_ref, wide_ref, acc_ref)

    shift = patch_ref.shape[1]
    count = acc_ref.shape[0]
    acc_ref[...] += wide_ref[:count, :LANES] + wide_ref[shift : shift + count, LANES:]


def result_of(acc_ref, frames, cols, rows):
    pitch = acc_ref.shape[0] // frames
    whole = acc_ref[...].reshape(frames, pitch, LANES)
    return whole[:, : cols * rows].reshape(frames, cols, rows, LANES)


def fetch_blocks(near_refs, h_ref, sem_ref):
    own = lax.axis_index("chan") * 2 + lax.axis_index("groups")
    copies = [
        pltpu.make_async_copy(near_ref, h_ref.at[own ^ code], sem_ref.at[code])
        for code, near_ref in enumerate(near_refs)
    ]
    for copy in copies:
        copy.start()
    return copies


def first_begin(slots, extents_ref, gain_ref, far_gain_ref, *refs):
    used = 4 + len(slots)
    win_refs, weight_refs = refs[:4], refs[4:used]
    h_ref, source_ref, acc_ref, patch_ref, wide_ref, held_ref, sem_ref = refs[used:]
    copies = weight_copies(slots, weight_refs, held_ref, sem_ref)
    start_weights(copies)
    limit = window_limit(extents_ref, h_ref.shape[2])
    prepare(limit, (gain_ref, far_gain_ref), win_refs, h_ref, source_ref)
    acc_ref[...] = jnp.zeros_like(acc_ref)
    add_blocks(copies, h_ref, held_ref, patch_ref, wide_ref, acc_ref)


def first_end(slots, extents_ref, gain_ref, h_ref, begun_ref, *refs):
    weight_refs = refs[: len(slots)]
    out_ref, acc_ref, patch_ref, wide_ref, held_ref, sem_ref = refs[len(slots) :]
    copies = weight_copies(slots, weight_refs, held_ref, sem_ref)
    start_weights(copies)
    acc_ref[...] = begun_ref[...]
    add_blocks(copies, h_ref, held_ref, patch_ref, wide_ref, acc_ref)
    frames, cols, rows = h_ref.shape[1:4]
    limit = window_limit(extents_ref, cols)
    mask = column_mask(cols, limit)
    count = limit.astype(jnp.float32) * (frames * rows)
    first = (result_of(acc_ref, frames, cols, rows) * mask).astype(jnp.bfloat16)
    share = pl.multiple_of(lax.axis_index("groups") * LANES, LANES)
    gain = gain_ref[:, pl.ds(share, LANES)]
    done = normalized(first.astype(jnp.float32), gain, count, mask)
    out_ref[...] = done.astype(jnp.bfloat16)


def second_kernel(slots, extents_ref, source_hbm_ref, *refs):
    used = 4 + len(slots)
    near_refs, weight_refs, out_refs = refs[:4], refs[4:used], refs[used : used + 2]
    source_ref, source_sem, h_ref, h_sem_ref, acc_ref = refs[used + 2 : used + 7]
    patch_ref, wide_ref, held_ref, sem_ref = refs[used + 7 :]
    fetched = fetch_blocks(near_refs, h_ref, h_sem_ref)
    copies = weight_copies(slots, weight_refs, held_ref, sem_ref)
    start_weights(copies)
    source_copy = pltpu.make_async_copy(source_hbm_ref, source_ref, source_sem)
    source_copy.start()
    acc_ref[...] = jnp.zeros_like(acc_ref)
    for copy in fetched:
        copy.wait()
    add_blocks(copies, h_ref, held_ref, patch_ref, wide_ref, acc_ref)
    frames, cols, rows = h_ref.shape[1:4]
    mask = column_mask(cols, window_limit(extents_ref, cols))
    source_copy.wait()
    source = source_ref[...].astype(jnp.float32)
    done = (source + result_of(acc_ref, frames, cols, rows)) * mask
    done = done.astype(jnp.bfloat16)
    out_refs[0][...] = done[:, : cols - INTERSECTION]
    out_refs[1][...] = done[:, cols - INTERSECTION :]


def relayed(weight):
    tiles, subs = lax.axis_size("tile"), lax.axis_size("sub")
    out_share = weight.shape[4] // lax.axis_size("groups")
    own = lax.dynamic_slice_in_dim(weight, lax.axis_index("groups") * out_share, out_share, 4)
    own = own.reshape(3, -1, out_share)
    held, pieces = own, [own]
    for step in range(1, tiles):
        pairs = [(z * subs, (z + 1) * subs + 1) for z in range(step - 1, tiles - 1)]
        pairs += [(z * subs + 1, (z - 1) * subs) for z in range(1, tiles - step + 1)]
        arrived = lax.ppermute(held, ("tile", "sub"), pairs)
        held = lax.ppermute(arrived, "sub", [(0, 1), (1, 0)])
        pieces += [arrived, held]
    return pieces


def by_distance(array):
    got = [array]
    for code in range(1, 4):
        pairs = [(i, i ^ code) for i in range(4)]
        got.append(lax.ppermute(array, ("groups", "chan"), pairs))
    return got


def share_plan(latent, extents, gain_one, weight_one, gain_two, weight_two):
    frame_count, row_count, col_count, chan_count = latent.shape
    tiles, clips = lax.axis_size("tile"), lax.axis_size("groups")
    sub = lax.axis_index("sub")
    _, prior = reach_and_prior(extents)
    span = col_count + INTERSECTION
    share = chan_count // clips
    frames = clips * frame_count
    pitch = (span + 1) * row_count
    taps = weight_one.shape[1] * weight_one.shape[2]
    vmem, smem = pl.BlockSpec(memory_space=pltpu.VMEM), pl.BlockSpec(memory_space=pltpu.SMEM)
    anywhere = pl.BlockSpec(memory_space=pl.ANY)
    final = jax.ShapeDtypeStruct((frames, span, row_count, share), jnp.bfloat16)
    blocks = jax.ShapeDtypeStruct((tiles,) + final.shape, jnp.bfloat16)
    total = jax.ShapeDtypeStruct((frames * pitch, share), jnp.float32)

    def scratch(slots):
        return [
            pltpu.VMEM((frames + 2, pitch, taps * LANES), jnp.bfloat16),
            pltpu.VMEM(((frames + 1) * pitch, 2 * share), jnp.float32),
            pltpu.VMEM((len(slots), 3, taps * LANES, share), jnp.bfloat16),
            pltpu.SemaphoreType.DMA((len(slots),)),
        ]

    def chosen(weights, slots):
        return [weights[slot] for slot in slots]

    acc_scratch = [pltpu.VMEM(total.shape, jnp.float32)]

    by_col = jnp.transpose(latent, (0, 2, 1, 3))
    incoming = shifted(by_col[:, :INTERSECTION], "tile", -1)
    window = jnp.concatenate([by_col, incoming], axis=1)
    windows = []
    for turn in range(2):
        for away in range(2):
            pairs = [
                ((c * 2 + (x ^ away)) * 2 + (g ^ turn), (g * 2 + x) * 2 + c)
                for g in range(2)
                for x in range(2)
                for c in range(2)
            ]
            windows.append(lax.ppermute(window, ("groups", "chan", "sub"), pairs))
    first_weights = relayed(weight_one)
    second_weights = relayed(weight_two)
    own_gain = gain_one.reshape(1, -1)
    other_gain = lax.ppermute(own_gain, "chan", [(0, 1), (1, 0)])
    slots = tuple(range(2 * tiles - 1))
    early, late = slots[:FIRST_SPLIT], slots[FIRST_SPLIT:]
    hidden, source, begun = pl.pallas_call(
        functools.partial(first_begin, early),
        out_shape=(blocks, final, total),
        in_specs=[smem] + [vmem] * 6 + [anywhere] * len(early),
        out_specs=(vmem,) * 3,
        scratch_shapes=scratch(early),
        compiler_params=pltpu.CompilerParams(vmem_limit_bytes=GRANT),
    )(extents, own_gain, other_gain, *windows, *chosen(first_weights, early))
    hidden_two = pl.pallas_call(
        functools.partial(first_end, late),
        out_shape=final,
        in_specs=[smem] + [vmem] * 3 + [anywhere] * len(late),
        out_specs=vmem,
        scratch_shapes=acc_scratch + scratch(late),
        compiler_params=pltpu.CompilerParams(vmem_limit_bytes=GRANT),
    )(extents, gain_two.reshape(1, -1), hidden, begun, *chosen(first_weights, late))
    near = by_distance(hidden_two)
    near = [near[0], near[2], near[1], near[3]]
    kept = jax.ShapeDtypeStruct((frames, col_count, row_count, share), jnp.bfloat16)
    passed = jax.ShapeDtypeStruct((frames, INTERSECTION, row_count, share), jnp.bfloat16)
    own, tail = pl.pallas_call(
        functools.partial(second_kernel, slots),
        out_shape=(kept, passed),
        in_specs=[smem] + [anywhere] * (1 + tiles + len(slots)),
        out_specs=(vmem, vmem),
        scratch_shapes=[
            pltpu.VMEM(final.shape, jnp.bfloat16),
            pltpu.SemaphoreType.DMA,
            pltpu.VMEM(blocks.shape, jnp.bfloat16),
            pltpu.SemaphoreType.DMA((tiles,)),
        ]
        + acc_scratch
        + scratch(slots),
        compiler_params=pltpu.CompilerParams(vmem_limit_bytes=LAST_GRANT),
    )(extents, source, *near, *chosen(second_weights, slots))

    onward = [
        ((g * tiles + z) * 2 + c, (c * tiles + z + 1) * 2 + g)
        for g in range(2)
        for z in range(tiles - 1)
        for c in range(2)
    ]
    tail = lax.ppermute(tail, ("groups", "tile", "sub"), onward)
    own = lax.ppermute(own, ("groups", "sub"), [(0, 0), (1, 2), (2, 1), (3, 3)])

    def frames_here(array):
        halves = array.reshape((2, frame_count) + array.shape[1:])
        mine = lax.dynamic_index_in_dim(halves, sub, 0, keepdims=False)
        other = lax.dynamic_index_in_dim(halves, 1 - sub, 0, keepdims=False)
        other = lax.ppermute(other, "sub", [(0, 1), (1, 0)])
        straight = jnp.concatenate([mine, other], axis=3)
        crossed = jnp.concatenate([other, mine], axis=3)
        return jnp.where(sub == 0, straight, crossed)

    own, tail = frames_here(own), frames_here(tail)
    ramp = blend_ramp(prior)[None, :, None, None]
    head = jnp.repeat(own[:, :INTERSECTION].astype(jnp.float32), 2, axis=1) * ramp + jnp.repeat(
        tail.astype(jnp.float32), 2, axis=1
    ) * (1.0 - ramp)
    rest = jnp.repeat(own[:, INTERSECTION:], 2, axis=1)
    decoded = jnp.concatenate([head.astype(jnp.bfloat16), rest], axis=1)
    decoded = jnp.repeat(decoded, 2, axis=2)
    return jnp.transpose(decoded, (0, 2, 1, 3))


def solution(mesh):
    placed = (
        P(("groups", "sub"), None, "tile", "chan"),
        P(),
        P("chan"),
        P(None, None, None, "tile", "chan"),
        P("chan"),
        P(None, None, None, "tile", "chan"),
    )
    sizes = mesh.shape
    pairs_up = sizes["groups"] == 2 and sizes["sub"] == 2 and sizes["chan"] == 2
    few = pairs_up and CH // sizes["tile"] == LANES

    def body(*arrays):
        return (share_plan if few else gather_plan)(*arrays)

    return jax.shard_map(
        body,
        mesh=mesh,
        in_specs=placed,
        out_specs=P(("groups", "sub"), None, "tile", "chan"),
        check_vma=False,
    )
```

```python
import functools

import jax
import jax.numpy as jnp
from jax import lax
from jax.experimental import pallas as pl
from jax.experimental.pallas import tpu as pltpu
from jax.sharding import PartitionSpec as P


CH = 512
GROUPS = 32
INTERSECTION = 4
LANES = 128
GRANT = 12 * 2**20
LAST_GRANT = 60 * 2**20


eps = 1e-06


def shifted(array, axis, by):
    peers = lax.axis_size(axis)
    pairs = [(i, i + by) for i in range(peers) if 0 <= i + by < peers]
    return lax.ppermute(array, axis, pairs)


def ramp_after(prior):
    positions = jnp.arange(2 * INTERSECTION).astype(jnp.float32) + 0.5
    limit = (2 * prior).astype(jnp.float32)[..., None]
    denom = (2 * jnp.maximum(prior, 1)).astype(jnp.float32)[..., None]
    return jnp.where(positions < limit, positions / denom, 1.0)


def convolve(inputs, kernel):
    result = lax.conv_general_dilated(
        inputs[None],
        kernel,
        (1, 1, 1),
        [(0, 0), (1, 1), (1, 1)],
        dimension_numbers=("NDHWC", "DHWIO", "NDHWC"),
        preferred_element_type=jnp.float32,
    )
    return result[0]


def group_norm(values, gain, count):
    group_size = CH // GROUPS
    grouped = values.reshape(values.shape[:-1] + (values.shape[-1] // group_size, group_size))
    totals, squares = lax.psum(
        (jnp.sum(grouped, axis=(0, 1, 2, 4)), jnp.sum(grouped * grouped, axis=(0, 1, 2, 4))), "sub"
    )
    size = count * group_size
    mean_val = totals / size
    variance = squares / size - mean_val * mean_val
    scaled = (grouped - mean_val[:, None]) * lax.rsqrt(variance + eps)[:, None]
    return scaled.reshape(values.shape) * gain


def causal_pad(values):
    earlier = shifted(values[-2:], "sub", 1)
    repeated = jnp.concatenate([values[:1], values[:1]], axis=0)
    leading = jnp.where(lax.axis_index("sub") == 0, repeated, earlier)
    return jnp.concatenate([leading, values], axis=0)


def channel_conv(padded_in, weight):
    full_in = lax.all_gather(padded_in, "chan", axis=3, tiled=True)
    out_count = weight.shape[4]
    share = weight.shape[3] // lax.axis_size("sub")
    portion = lax.dynamic_slice_in_dim(weight, lax.axis_index("sub") * share, share, 3)
    fetched = lax.all_gather(portion, "tile", axis=3, tiled=True)
    sectioned = fetched.reshape(3, 3, 3, lax.axis_size("tile"), 1, share, out_count)
    whole = lax.all_gather(sectioned, "sub", axis=4, tiled=True).reshape(3, 3, 3, -1, out_count)
    return convolve(full_in, whole)


def upscale(values):
    return jnp.repeat(jnp.repeat(values, 2, axis=1), 2, axis=2)


def reach_and_prior(extents):
    tile_count = lax.axis_size("tile")
    place = lax.axis_index("tile")
    tile_ids = jnp.arange(tile_count, dtype=jnp.int32)
    reaches = jnp.where(tile_ids == tile_count - 1, 0, extents)
    reach = jnp.sum(jnp.where(tile_ids == place, reaches, 0))
    prior = jnp.sum(jnp.where(tile_ids == place - 1, reaches, 0))
    return reach, prior


def gather_plan(latent, extents, gain_one, weight_one, gain_two, weight_two):
    frame_count, row_count, col_count, _ = latent.shape
    reach, prior = reach_and_prior(extents)
    incoming = shifted(latent[:, :, :INTERSECTION, :], "tile", -1)
    window = jnp.concatenate([latent, incoming], axis=2)
    valid = (jnp.arange(col_count + INTERSECTION, dtype=jnp.int32) < col_count + reach).astype(
        jnp.float32
    )
    mask = valid[None, None, :, None]
    window = jnp.where(mask > 0, window, jnp.zeros_like(window))
    count = (col_count + reach).astype(jnp.float32) * (
        frame_count * lax.axis_size("sub") * row_count
    )
    source = window.astype(jnp.float32)
    hidden = (jax.nn.silu(group_norm(source, gain_one, count)) * mask).astype(jnp.bfloat16)
    first = (channel_conv(causal_pad(hidden), weight_one) * mask).astype(jnp.bfloat16)
    first = lax.optimization_barrier(first)
    hidden_two = (
        jax.nn.silu(group_norm(first.astype(jnp.float32), gain_two, count)) * mask
    ).astype(jnp.bfloat16)
    second = channel_conv(causal_pad(hidden_two), weight_two)
    result = ((source + second) * mask).astype(jnp.bfloat16)
    larger = upscale(result)
    own = larger[:, :, : 2 * col_count]
    arrived = shifted(larger[:, :, 2 * col_count :], "tile", 1)
    ramp = ramp_after(prior)[None, None, :, None]
    head = own[:, :, : 2 * INTERSECTION].astype(jnp.float32) * ramp + arrived.astype(
        jnp.float32
    ) * (1.0 - ramp)
    return jnp.concatenate([head.astype(jnp.bfloat16), own[:, :, 2 * INTERSECTION :]], axis=2)


def normalized(values, gain, count, mask):
    chans = values.shape[-1]
    group_size = CH // GROUPS
    rows = lax.broadcasted_iota(jnp.int32, (chans, chans), 0) // group_size
    cols = lax.broadcasted_iota(jnp.int32, (chans, chans), 1) // group_size
    same = (rows == cols).astype(jnp.float32)
    total = jnp.sum(values, axis=(0, 1, 2)).reshape(1, chans)
    square = jnp.sum(values * values, axis=(0, 1, 2)).reshape(1, chans)
    both = jnp.concatenate([jnp.broadcast_to(total, (8, chans)), jnp.broadcast_to(square, (8, chans))], 0)
    sums = jnp.dot(both, same, precision=lax.Precision.HIGHEST, preferred_element_type=jnp.float32)
    size = count * group_size
    mean = sums[0:1] / size
    variance = sums[8:9] / size - mean * mean
    rate = lax.rsqrt(variance + eps)
    shape = (1, 1, 1, chans)
    scaled = (values - mean.reshape(shape)) * rate.reshape(shape) * gain.reshape(shape)
    return (scaled / (1.0 + jnp.exp(-scaled))) * mask


def column_mask(cols, limit):
    ids = lax.broadcasted_iota(jnp.int32, (1, cols, 8, LANES), 1)
    return (ids < limit).astype(jnp.float32)


def window_limit(extents_ref, cols):
    place = lax.axis_index("tile")
    reach = jnp.where(place == lax.axis_size("tile") - 1, 0, extents_ref[place])
    return cols - INTERSECTION + reach


def blend_ramp(extents_ref, shape):
    place = lax.axis_index("tile")
    prior = jnp.where(place == 0, 0, extents_ref[jnp.maximum(place - 1, 0)])
    positions = lax.broadcasted_iota(jnp.int32, shape, 0).astype(jnp.float32) + 0.5
    limit = jnp.broadcast_to((2 * prior).astype(jnp.float32), shape)
    denom = jnp.broadcast_to((2 * jnp.maximum(prior, 1)).astype(jnp.float32), shape)
    return jnp.where(positions < limit, positions / denom, 1.0)


def owner_of(slot):
    step = (slot + 1) // 2
    ahead = (lax.axis_index("sub") == 0) == (slot % 2 == 1)
    return lax.axis_index("tile") + jnp.where(ahead, step, -step)


def prepare(limit, gain_refs, win_refs, h_ref, source_ref):
    clip, chan = lax.axis_index("groups"), lax.axis_index("chan")
    frames, cols, rows, width = win_refs[0].shape
    count = limit.astype(jnp.float32) * (2 * frames * rows)
    mask = column_mask(cols, limit)
    for away, gain_ref in enumerate(gain_refs):
        for piece in range(width // LANES):
            lanes = slice(piece * LANES, (piece + 1) * LANES)
            both = [win_refs[2 * turn + away][:, :, :, lanes] for turn in range(2)]
            values = jnp.concatenate(both, 0).astype(jnp.float32)
            values = jnp.where(mask > 0, values, 0.0)
            done = normalized(values, gain_ref[:, lanes], count, mask).astype(jnp.bfloat16)
            block = (chan ^ away) * (width // LANES) + piece
            for turn in range(2):
                rows_at = pl.ds((clip ^ turn) * frames, frames)
                h_ref[block, rows_at] = done[turn * frames : (turn + 1) * frames]
                if away == 0:

                    @pl.when(clip == piece)
                    def _(rows_at=rows_at, turn=turn, both=both):
                        source_ref[rows_at] = both[turn]


def fill_patches(h_ref, block, patch_ref):
    frames, cols, rows, width = h_ref.shape[1:]
    ids = lax.broadcasted_iota(jnp.int32, (cols, rows, width), 1)
    empty = jnp.zeros((rows, width), jnp.float32)
    for t in range(frames):
        here = h_ref[block, t].astype(jnp.float32)
        for b in range(3):
            if b == 1:
                moved = here
            else:
                moved = pltpu.roll(here, 1 if b == 0 else rows - 1, 1)
                moved = jnp.where(ids == (0 if b == 0 else rows - 1), 0.0, moved)
            flat = moved.reshape(cols * rows, width)
            for d in range(3):
                if d == 0:
                    piece = jnp.concatenate([empty, flat], 0)
                elif d == 1:
                    piece = jnp.concatenate([flat, empty], 0)
                else:
                    piece = jnp.concatenate([flat[rows:], empty, empty], 0)
                piece = piece.astype(jnp.bfloat16)
                lane = (b * 3 + d) * width
                patch_ref[t + 2, :, lane : lane + width] = piece
                if t == 0:
                    patch_ref[0, :, lane : lane + width] = piece
                    patch_ref[1, :, lane : lane + width] = piece


def add_block(h_ref, block, weight_ref, patch_ref, wide_ref, acc_ref):
    fill_patches(h_ref, block, patch_ref)
    frames = h_ref.shape[1]
    pitch, depth = patch_ref.shape[1:]
    both = jnp.concatenate([weight_ref[0], weight_ref[1]], axis=1)
    left = patch_ref[: frames + 1].reshape((frames + 1) * pitch, depth)
    wide_ref[...] += jnp.dot(left, both, preferred_element_type=jnp.float32)
    left = patch_ref[2:].reshape(frames * pitch, depth)
    acc_ref[...] += jnp.dot(left, weight_ref[2], preferred_element_type=jnp.float32)


def weight_copies(slots, weight_refs, held_ref, sem_ref):
    copies = []
    for i, (slot, weight_ref) in enumerate(zip(slots, weight_refs)):
        owner = owner_of(slot)
        there = (owner >= 0) & (owner < lax.axis_size("tile"))
        copy = pltpu.make_async_copy(weight_ref, held_ref.at[i], sem_ref.at[i])
        copies.append((owner, there, copy))
    return copies


def start_weights(copies):
    for _, there, copy in copies:

        @pl.when(there)
        def _(copy=copy):
            copy.start()


def add_blocks(copies, h_ref, held_ref, patch_ref, wide_ref, acc_ref):
    wide_ref[...] = jnp.zeros_like(wide_ref)
    for i, (owner, there, copy) in enumerate(copies):

        @pl.when(there)
        def _(i=i, owner=owner, copy=copy):
            copy.wait()
            add_block(h_ref, owner, held_ref.at[i], patch_ref, wide_ref, acc_ref)

    shift = patch_ref.shape[1]
    count = acc_ref.shape[0]
    acc_ref[...] += wide_ref[:count, :LANES] + wide_ref[shift : shift + count, LANES:]


def result_of(acc_ref, frames, cols, rows):
    pitch = acc_ref.shape[0] // frames
    whole = acc_ref[...].reshape(frames, pitch, LANES)
    return whole[:, : cols * rows].reshape(frames, cols, rows, LANES)


def fetch_blocks(near_refs, h_ref, sem_ref):
    own = lax.axis_index("chan") * 2 + lax.axis_index("groups")
    copies = [
        pltpu.make_async_copy(near_ref, h_ref.at[own ^ code], sem_ref.at[code])
        for code, near_ref in enumerate(near_refs)
    ]
    for copy in copies:
        copy.start()
    return copies


def first_begin(slots, extents_ref, gain_ref, far_gain_ref, *refs):
    used = 4 + len(slots)
    win_refs, weight_refs = refs[:4], refs[4:used]
    h_ref, source_ref, acc_ref, patch_ref, wide_ref, held_ref, sem_ref = refs[used:]
    copies = weight_copies(slots, weight_refs, held_ref, sem_ref)
    start_weights(copies)
    limit = window_limit(extents_ref, h_ref.shape[2])
    prepare(limit, (gain_ref, far_gain_ref), win_refs, h_ref, source_ref)
    acc_ref[...] = jnp.zeros_like(acc_ref)
    add_blocks(copies, h_ref, held_ref, patch_ref, wide_ref, acc_ref)


def first_more(slots, h_ref, begun_ref, *refs):
    weight_refs = refs[: len(slots)]
    acc_ref, patch_ref, wide_ref, held_ref, sem_ref = refs[len(slots) :]
    copies = weight_copies(slots, weight_refs, held_ref, sem_ref)
    start_weights(copies)
    acc_ref[...] = begun_ref[...]
    add_blocks(copies, h_ref, held_ref, patch_ref, wide_ref, acc_ref)


def first_end(slots, extents_ref, gain_ref, h_ref, begun_ref, *refs):
    weight_refs = refs[: len(slots)]
    out_ref, acc_ref, patch_ref, wide_ref, held_ref, sem_ref = refs[len(slots) :]
    copies = weight_copies(slots, weight_refs, held_ref, sem_ref)
    start_weights(copies)
    acc_ref[...] = begun_ref[...]
    add_blocks(copies, h_ref, held_ref, patch_ref, wide_ref, acc_ref)
    frames, cols, rows = h_ref.shape[1:4]
    limit = window_limit(extents_ref, cols)
    mask = column_mask(cols, limit)
    count = limit.astype(jnp.float32) * (frames * rows)
    first = (result_of(acc_ref, frames, cols, rows) * mask).astype(jnp.bfloat16)
    share = pl.multiple_of(lax.axis_index("groups") * LANES, LANES)
    gain = gain_ref[:, pl.ds(share, LANES)]
    done = normalized(first.astype(jnp.float32), gain, count, mask)
    out_ref[...] = done.astype(jnp.bfloat16)


def second_kernel(slots, extents_ref, source_hbm_ref, *refs):
    used = 4 + len(slots)
    near_refs, weight_refs, out_refs = refs[:4], refs[4:used], refs[used : used + 3]
    source_ref, source_sem, h_ref, h_sem_ref, acc_ref = refs[used + 3 : used + 8]
    patch_ref, wide_ref, held_ref, sem_ref = refs[used + 8 :]
    fetched = fetch_blocks(near_refs, h_ref, h_sem_ref)
    copies = weight_copies(slots, weight_refs, held_ref, sem_ref)
    start_weights(copies)
    source_copy = pltpu.make_async_copy(source_hbm_ref, source_ref, source_sem)
    source_copy.start()
    acc_ref[...] = jnp.zeros_like(acc_ref)
    for copy in fetched:
        copy.wait()
    add_blocks(copies, h_ref, held_ref, patch_ref, wide_ref, acc_ref)
    frames, cols, rows = h_ref.shape[1:4]
    mask = column_mask(cols, window_limit(extents_ref, cols))
    source_copy.wait()
    source = source_ref[...].astype(jnp.float32)
    done = (source + result_of(acc_ref, frames, cols, rows)) * mask
    done = done.astype(jnp.bfloat16)
    out_refs[0][...] = done[:, : cols - INTERSECTION]
    out_refs[1][...] = done[:, cols - INTERSECTION :]
    out_refs[2][...] = blend_ramp(extents_ref, out_refs[2].shape)


def relayed(weight):
    tiles, subs = lax.axis_size("tile"), lax.axis_size("sub")
    out_share = weight.shape[4] // lax.axis_size("groups")
    own = lax.dynamic_slice_in_dim(weight, lax.axis_index("groups") * out_share, out_share, 4)
    own = own.reshape(3, -1, out_share)
    held, pieces = own, [own]
    for step in range(1, tiles):
        pairs = [(z * subs, (z + 1) * subs + 1) for z in range(step - 1, tiles - 1)]
        pairs += [(z * subs + 1, (z - 1) * subs) for z in range(1, tiles - step + 1)]
        arrived = lax.ppermute(held, ("tile", "sub"), pairs)
        held = lax.ppermute(arrived, "sub", [(0, 1), (1, 0)])
        pieces += [arrived, held]
    return pieces


def by_distance(array):
    got = [array]
    for code in range(1, 4):
        pairs = [(i, i ^ code) for i in range(4)]
        got.append(lax.ppermute(array, ("groups", "chan"), pairs))
    return got


def share_plan(latent, extents, gain_one, weight_one, gain_two, weight_two):
    frame_count, row_count, col_count, chan_count = latent.shape
    tiles, clips = lax.axis_size("tile"), lax.axis_size("groups")
    sub = lax.axis_index("sub")
    span = col_count + INTERSECTION
    share = chan_count // clips
    frames = clips * frame_count
    pitch = (span + 1) * row_count
    taps = weight_one.shape[1] * weight_one.shape[2]
    vmem, smem = pl.BlockSpec(memory_space=pltpu.VMEM), pl.BlockSpec(memory_space=pltpu.SMEM)
    anywhere = pl.BlockSpec(memory_space=pl.ANY)
    final = jax.ShapeDtypeStruct((frames, span, row_count, share), jnp.bfloat16)
    blocks = jax.ShapeDtypeStruct((tiles,) + final.shape, jnp.bfloat16)
    total = jax.ShapeDtypeStruct((frames * pitch, share), jnp.float32)

    def scratch(slots):
        return [
            pltpu.VMEM((frames + 2, pitch, taps * LANES), jnp.bfloat16),
            pltpu.VMEM(((frames + 1) * pitch, 2 * share), jnp.float32),
            pltpu.VMEM((len(slots), 3, taps * LANES, share), jnp.bfloat16),
            pltpu.SemaphoreType.DMA((len(slots),)),
        ]

    def chosen(weights, slots):
        return [weights[slot] for slot in slots]

    acc_scratch = [pltpu.VMEM(total.shape, jnp.float32)]

    by_col = jnp.transpose(latent, (0, 2, 1, 3))
    incoming = shifted(by_col[:, :INTERSECTION], "tile", -1)
    window = jnp.concatenate([by_col, incoming], axis=1)
    windows = []
    for turn in range(2):
        for away in range(2):
            pairs = [
                ((c * 2 + (x ^ away)) * 2 + (g ^ turn), (g * 2 + x) * 2 + c)
                for g in range(2)
                for x in range(2)
                for c in range(2)
            ]
            windows.append(lax.ppermute(window, ("groups", "chan", "sub"), pairs))
    first_weights = relayed(weight_one)
    second_weights = relayed(weight_two)
    own_gain = gain_one.reshape(1, -1)
    other_gain = lax.ppermute(own_gain, "chan", [(0, 1), (1, 0)])
    slots = tuple(range(2 * tiles - 1))
    early, middle, late = slots[:3], slots[3:-2], slots[-2:]
    hidden, source, begun = pl.pallas_call(
        functools.partial(first_begin, early),
        out_shape=(blocks, final, total),
        in_specs=[smem] + [vmem] * 6 + [anywhere] * len(early),
        out_specs=(vmem,) * 3,
        scratch_shapes=scratch(early),
        compiler_params=pltpu.CompilerParams(vmem_limit_bytes=GRANT),
    )(extents, own_gain, other_gain, *windows, *chosen(first_weights, early))
    begun = pl.pallas_call(
        functools.partial(first_more, middle),
        out_shape=total,
        in_specs=[vmem] * 2 + [anywhere] * len(middle),
        out_specs=vmem,
        scratch_shapes=scratch(middle),
        compiler_params=pltpu.CompilerParams(vmem_limit_bytes=GRANT),
    )(hidden, begun, *chosen(first_weights, middle))
    hidden_two = pl.pallas_call(
        functools.partial(first_end, late),
        out_shape=final,
        in_specs=[smem] + [vmem] * 3 + [anywhere] * len(late),
        out_specs=vmem,
        scratch_shapes=acc_scratch + scratch(late),
        compiler_params=pltpu.CompilerParams(vmem_limit_bytes=GRANT),
    )(extents, gain_two.reshape(1, -1), hidden, begun, *chosen(first_weights, late))
    near = by_distance(hidden_two)
    near = [near[0], near[2], near[1], near[3]]
    kept = jax.ShapeDtypeStruct((frames, col_count, row_count, share), jnp.bfloat16)
    ramps = jax.ShapeDtypeStruct((2 * INTERSECTION, share), jnp.float32)
    passed = jax.ShapeDtypeStruct((frames, INTERSECTION, row_count, share), jnp.bfloat16)
    own, tail, ramp = pl.pallas_call(
        functools.partial(second_kernel, slots),
        out_shape=(kept, passed, ramps),
        in_specs=[smem] + [anywhere] * (1 + tiles + len(slots)),
        out_specs=(vmem,) * 3,
        scratch_shapes=[
            pltpu.VMEM(final.shape, jnp.bfloat16),
            pltpu.SemaphoreType.DMA,
            pltpu.VMEM(blocks.shape, jnp.bfloat16),
            pltpu.SemaphoreType.DMA((tiles,)),
        ]
        + acc_scratch
        + scratch(slots),
        compiler_params=pltpu.CompilerParams(vmem_limit_bytes=LAST_GRANT),
    )(extents, source, *near, *chosen(second_weights, slots))

    onward = [
        ((g * tiles + z) * 2 + c, (c * tiles + z + 1) * 2 + g)
        for g in range(2)
        for z in range(tiles - 1)
        for c in range(2)
    ]
    tail = lax.ppermute(tail, ("groups", "tile", "sub"), onward)
    own = lax.ppermute(own, ("groups", "sub"), [(0, 0), (1, 2), (2, 1), (3, 3)])

    def frames_here(array):
        halves = array.reshape((2, frame_count) + array.shape[1:])
        mine = lax.dynamic_index_in_dim(halves, sub, 0, keepdims=False)
        other = lax.dynamic_index_in_dim(halves, 1 - sub, 0, keepdims=False)
        other = lax.ppermute(other, "sub", [(0, 1), (1, 0)])
        straight = jnp.concatenate([mine, other], axis=3)
        crossed = jnp.concatenate([other, mine], axis=3)
        return jnp.where(sub == 0, straight, crossed)

    own, tail = frames_here(own), frames_here(tail)
    ramp = ramp[None, :, None, :1]
    head = jnp.repeat(own[:, :INTERSECTION].astype(jnp.float32), 2, axis=1) * ramp + jnp.repeat(
        tail.astype(jnp.float32), 2, axis=1
    ) * (1.0 - ramp)
    rest = jnp.repeat(own[:, INTERSECTION:], 2, axis=1)
    decoded = jnp.concatenate([head.astype(jnp.bfloat16), rest], axis=1)
    decoded = jnp.repeat(decoded, 2, axis=2)
    return jnp.transpose(decoded, (0, 2, 1, 3))


def solution(mesh):
    placed = (
        P(("groups", "sub"), None, "tile", "chan"),
        P(),
        P("chan"),
        P(None, None, None, "tile", "chan"),
        P("chan"),
        P(None, None, None, "tile", "chan"),
    )
    sizes = mesh.shape
    pairs_up = sizes["groups"] == 2 and sizes["sub"] == 2 and sizes["chan"] == 2
    few = pairs_up and CH // sizes["tile"] == LANES

    def body(*arrays):
        return (share_plan if few else gather_plan)(*arrays)

    return jax.shard_map(
        body,
        mesh=mesh,
        in_specs=placed,
        out_specs=P(("groups", "sub"), None, "tile", "chan"),
        check_vma=False,
    )
```

```python
import functools

import jax
import jax.numpy as jnp
from jax import lax
from jax.experimental import pallas as pl
from jax.experimental.pallas import tpu as pltpu
from jax.sharding import PartitionSpec as P


CH = 512
GROUPS = 32
INTERSECTION = 4
LANES = 128
GRANT = 12 * 2**20
LAST_GRANT = 60 * 2**20


eps = 1e-06


def shifted(array, axis, by):
    peers = lax.axis_size(axis)
    pairs = [(i, i + by) for i in range(peers) if 0 <= i + by < peers]
    return lax.ppermute(array, axis, pairs)


def ramp_after(prior):
    positions = jnp.arange(2 * INTERSECTION).astype(jnp.float32) + 0.5
    limit = (2 * prior).astype(jnp.float32)[..., None]
    denom = (2 * jnp.maximum(prior, 1)).astype(jnp.float32)[..., None]
    return jnp.where(positions < limit, positions / denom, 1.0)


def convolve(inputs, kernel):
    result = lax.conv_general_dilated(
        inputs[None],
        kernel,
        (1, 1, 1),
        [(0, 0), (1, 1), (1, 1)],
        dimension_numbers=("NDHWC", "DHWIO", "NDHWC"),
        preferred_element_type=jnp.float32,
    )
    return result[0]


def group_norm(values, gain, count):
    group_size = CH // GROUPS
    grouped = values.reshape(values.shape[:-1] + (values.shape[-1] // group_size, group_size))
    totals, squares = lax.psum(
        (jnp.sum(grouped, axis=(0, 1, 2, 4)), jnp.sum(grouped * grouped, axis=(0, 1, 2, 4))), "sub"
    )
    size = count * group_size
    mean_val = totals / size
    variance = squares / size - mean_val * mean_val
    scaled = (grouped - mean_val[:, None]) * lax.rsqrt(variance + eps)[:, None]
    return scaled.reshape(values.shape) * gain


def causal_pad(values):
    earlier = shifted(values[-2:], "sub", 1)
    repeated = jnp.concatenate([values[:1], values[:1]], axis=0)
    leading = jnp.where(lax.axis_index("sub") == 0, repeated, earlier)
    return jnp.concatenate([leading, values], axis=0)


def channel_conv(padded_in, weight):
    full_in = lax.all_gather(padded_in, "chan", axis=3, tiled=True)
    out_count = weight.shape[4]
    share = weight.shape[3] // lax.axis_size("sub")
    portion = lax.dynamic_slice_in_dim(weight, lax.axis_index("sub") * share, share, 3)
    fetched = lax.all_gather(portion, "tile", axis=3, tiled=True)
    sectioned = fetched.reshape(3, 3, 3, lax.axis_size("tile"), 1, share, out_count)
    whole = lax.all_gather(sectioned, "sub", axis=4, tiled=True).reshape(3, 3, 3, -1, out_count)
    return convolve(full_in, whole)


def upscale(values):
    return jnp.repeat(jnp.repeat(values, 2, axis=1), 2, axis=2)


def reach_and_prior(extents):
    tile_count = lax.axis_size("tile")
    place = lax.axis_index("tile")
    tile_ids = jnp.arange(tile_count, dtype=jnp.int32)
    reaches = jnp.where(tile_ids == tile_count - 1, 0, extents)
    reach = jnp.sum(jnp.where(tile_ids == place, reaches, 0))
    prior = jnp.sum(jnp.where(tile_ids == place - 1, reaches, 0))
    return reach, prior


def gather_plan(latent, extents, gain_one, weight_one, gain_two, weight_two):
    frame_count, row_count, col_count, _ = latent.shape
    reach, prior = reach_and_prior(extents)
    incoming = shifted(latent[:, :, :INTERSECTION, :], "tile", -1)
    window = jnp.concatenate([latent, incoming], axis=2)
    valid = (jnp.arange(col_count + INTERSECTION, dtype=jnp.int32) < col_count + reach).astype(
        jnp.float32
    )
    mask = valid[None, None, :, None]
    window = jnp.where(mask > 0, window, jnp.zeros_like(window))
    count = (col_count + reach).astype(jnp.float32) * (
        frame_count * lax.axis_size("sub") * row_count
    )
    source = window.astype(jnp.float32)
    hidden = (jax.nn.silu(group_norm(source, gain_one, count)) * mask).astype(jnp.bfloat16)
    first = (channel_conv(causal_pad(hidden), weight_one) * mask).astype(jnp.bfloat16)
    first = lax.optimization_barrier(first)
    hidden_two = (
        jax.nn.silu(group_norm(first.astype(jnp.float32), gain_two, count)) * mask
    ).astype(jnp.bfloat16)
    second = channel_conv(causal_pad(hidden_two), weight_two)
    result = ((source + second) * mask).astype(jnp.bfloat16)
    larger = upscale(result)
    own = larger[:, :, : 2 * col_count]
    arrived = shifted(larger[:, :, 2 * col_count :], "tile", 1)
    ramp = ramp_after(prior)[None, None, :, None]
    head = own[:, :, : 2 * INTERSECTION].astype(jnp.float32) * ramp + arrived.astype(
        jnp.float32
    ) * (1.0 - ramp)
    return jnp.concatenate([head.astype(jnp.bfloat16), own[:, :, 2 * INTERSECTION :]], axis=2)


def normalized(values, gain, count, mask):
    chans = values.shape[-1]
    group_size = CH // GROUPS
    rows = lax.broadcasted_iota(jnp.int32, (chans, chans), 0) // group_size
    cols = lax.broadcasted_iota(jnp.int32, (chans, chans), 1) // group_size
    same = (rows == cols).astype(jnp.float32)
    total = jnp.sum(values, axis=(0, 1, 2)).reshape(1, chans)
    square = jnp.sum(values * values, axis=(0, 1, 2)).reshape(1, chans)
    both = jnp.concatenate([jnp.broadcast_to(total, (8, chans)), jnp.broadcast_to(square, (8, chans))], 0)
    sums = jnp.dot(both, same, precision=lax.Precision.HIGHEST, preferred_element_type=jnp.float32)
    size = count * group_size
    mean = sums[0:1] / size
    variance = sums[8:9] / size - mean * mean
    rate = lax.rsqrt(variance + eps)
    shape = (1, 1, 1, chans)
    scaled = (values - mean.reshape(shape)) * rate.reshape(shape) * gain.reshape(shape)
    return (scaled / (1.0 + jnp.exp(-scaled))) * mask


def column_mask(cols, limit):
    ids = lax.broadcasted_iota(jnp.int32, (1, cols, 8, LANES), 1)
    return (ids < limit).astype(jnp.float32)


def window_limit(extents_ref, cols):
    place = lax.axis_index("tile")
    reach = jnp.where(place == lax.axis_size("tile") - 1, 0, extents_ref[place])
    return cols - INTERSECTION + reach


def blend_ramp(extents_ref, shape):
    place = lax.axis_index("tile")
    prior = jnp.where(place == 0, 0, extents_ref[jnp.maximum(place - 1, 0)])
    positions = lax.broadcasted_iota(jnp.int32, shape, 0).astype(jnp.float32) + 0.5
    limit = jnp.broadcast_to((2 * prior).astype(jnp.float32), shape)
    denom = jnp.broadcast_to((2 * jnp.maximum(prior, 1)).astype(jnp.float32), shape)
    return jnp.where(positions < limit, positions / denom, 1.0)


def owner_of(slot):
    step = (slot + 1) // 2
    ahead = (lax.axis_index("sub") == 0) == (slot % 2 == 1)
    return lax.axis_index("tile") + jnp.where(ahead, step, -step)


def prepare(limit, gain_refs, win_refs, h_ref, source_ref):
    clip, chan = lax.axis_index("groups"), lax.axis_index("chan")
    frames, cols, rows, width = win_refs[0].shape
    count = limit.astype(jnp.float32) * (2 * frames * rows)
    mask = column_mask(cols, limit)
    for away, gain_ref in enumerate(gain_refs):
        for piece in range(width // LANES):
            lanes = slice(piece * LANES, (piece + 1) * LANES)
            both = [win_refs[2 * turn + away][:, :, :, lanes] for turn in range(2)]
            values = jnp.concatenate(both, 0).astype(jnp.float32)
            values = jnp.where(mask > 0, values, 0.0)
            done = normalized(values, gain_ref[:, lanes], count, mask).astype(jnp.bfloat16)
            block = (chan ^ away) * (width // LANES) + piece
            for turn in range(2):
                rows_at = pl.ds((clip ^ turn) * frames, frames)
                h_ref[block, rows_at] = done[turn * frames : (turn + 1) * frames]
                if away == 0:

                    @pl.when(clip == piece)
                    def _(rows_at=rows_at, turn=turn, both=both):
                        source_ref[rows_at] = both[turn]


def fill_patches(h_ref, block, patch_ref):
    frames, cols, rows, width = h_ref.shape[1:]
    ids = lax.broadcasted_iota(jnp.int32, (cols, rows, width), 1)
    empty = jnp.zeros((rows, width), jnp.float32)
    for t in range(frames):
        here = h_ref[block, t].astype(jnp.float32)
        for b in range(3):
            if b == 1:
                moved = here
            else:
                moved = pltpu.roll(here, 1 if b == 0 else rows - 1, 1)
                moved = jnp.where(ids == (0 if b == 0 else rows - 1), 0.0, moved)
            flat = moved.reshape(cols * rows, width)
            for d in range(3):
                if d == 0:
                    piece = jnp.concatenate([empty, flat], 0)
                elif d == 1:
                    piece = jnp.concatenate([flat, empty], 0)
                else:
                    piece = jnp.concatenate([flat[rows:], empty, empty], 0)
                piece = piece.astype(jnp.bfloat16)
                lane = (b * 3 + d) * width
                patch_ref[t + 2, :, lane : lane + width] = piece
                if t == 0:
                    patch_ref[0, :, lane : lane + width] = piece
                    patch_ref[1, :, lane : lane + width] = piece


def add_block(h_ref, block, weight_ref, patch_ref, wide_ref, acc_ref):
    fill_patches(h_ref, block, patch_ref)
    frames = h_ref.shape[1]
    pitch, depth = patch_ref.shape[1:]
    both = jnp.concatenate([weight_ref[0], weight_ref[1]], axis=1)
    left = patch_ref[: frames + 1].reshape((frames + 1) * pitch, depth)
    wide_ref[...] += jnp.dot(left, both, preferred_element_type=jnp.float32)
    left = patch_ref[2:].reshape(frames * pitch, depth)
    acc_ref[...] += jnp.dot(left, weight_ref[2], preferred_element_type=jnp.float32)


def weight_copies(slots, weight_refs, held_ref, sem_ref):
    copies = []
    for i, (slot, weight_ref) in enumerate(zip(slots, weight_refs)):
        owner = owner_of(slot)
        there = (owner >= 0) & (owner < lax.axis_size("tile"))
        copy = pltpu.make_async_copy(weight_ref, held_ref.at[i], sem_ref.at[i])
        copies.append((owner, there, copy))
    return copies


def start_weights(copies):
    for _, there, copy in copies:

        @pl.when(there)
        def _(copy=copy):
            copy.start()


def add_blocks(copies, h_ref, held_ref, patch_ref, wide_ref, acc_ref):
    wide_ref[...] = jnp.zeros_like(wide_ref)
    for i, (owner, there, copy) in enumerate(copies):

        @pl.when(there)
        def _(i=i, owner=owner, copy=copy):
            copy.wait()
            add_block(h_ref, owner, held_ref.at[i], patch_ref, wide_ref, acc_ref)

    join_wide(patch_ref, wide_ref, acc_ref)


def join_wide(patch_ref, wide_ref, acc_ref):
    shift = patch_ref.shape[1]
    count = acc_ref.shape[0]
    acc_ref[...] += wide_ref[:count, :LANES] + wide_ref[shift : shift + count, LANES:]


def result_of(acc_ref, frames, cols, rows):
    pitch = acc_ref.shape[0] // frames
    whole = acc_ref[...].reshape(frames, pitch, LANES)
    return whole[:, : cols * rows].reshape(frames, cols, rows, LANES)


def fetch_blocks(near_refs, h_ref, sem_ref):
    own = lax.axis_index("chan") * 2 + lax.axis_index("groups")
    copies = [
        pltpu.make_async_copy(near_ref, h_ref.at[own ^ code], sem_ref.at[code])
        for code, near_ref in enumerate(near_refs)
    ]
    for copy in copies:
        copy.start()
    return copies


def first_begin(slots, extents_ref, gain_ref, far_gain_ref, *refs):
    used = 4 + len(slots)
    win_refs, weight_refs = refs[:4], refs[4:used]
    h_ref, source_ref, acc_ref, patch_ref, wide_ref, held_ref, sem_ref = refs[used:]
    copies = weight_copies(slots, weight_refs, held_ref, sem_ref)
    start_weights(copies)
    limit = window_limit(extents_ref, h_ref.shape[2])
    prepare(limit, (gain_ref, far_gain_ref), win_refs, h_ref, source_ref)
    acc_ref[...] = jnp.zeros_like(acc_ref)
    add_blocks(copies, h_ref, held_ref, patch_ref, wide_ref, acc_ref)


def first_more(slots, h_ref, begun_ref, *refs):
    weight_refs = refs[: len(slots)]
    acc_ref, patch_ref, wide_ref, held_ref, sem_ref = refs[len(slots) :]
    copies = weight_copies(slots, weight_refs, held_ref, sem_ref)
    start_weights(copies)
    acc_ref[...] = begun_ref[...]
    add_blocks(copies, h_ref, held_ref, patch_ref, wide_ref, acc_ref)


def first_end(slots, extents_ref, gain_ref, h_ref, begun_ref, *refs):
    weight_refs = refs[: len(slots)]
    out_ref, acc_ref, patch_ref, wide_ref, held_ref, sem_ref = refs[len(slots) :]
    copies = weight_copies(slots, weight_refs, held_ref, sem_ref)
    start_weights(copies)
    acc_ref[...] = begun_ref[...]
    add_blocks(copies, h_ref, held_ref, patch_ref, wide_ref, acc_ref)
    frames, cols, rows = h_ref.shape[1:4]
    limit = window_limit(extents_ref, cols)
    mask = column_mask(cols, limit)
    count = limit.astype(jnp.float32) * (frames * rows)
    first = (result_of(acc_ref, frames, cols, rows) * mask).astype(jnp.bfloat16)
    share = pl.multiple_of(lax.axis_index("groups") * LANES, LANES)
    gain = gain_ref[:, pl.ds(share, LANES)]
    done = normalized(first.astype(jnp.float32), gain, count, mask)
    out_ref[...] = done.astype(jnp.bfloat16)


def second_kernel(slots, extents_ref, source_hbm_ref, *refs):
    used = 4 + len(slots)
    near_refs, weight_refs, out_refs = refs[:4], refs[4:used], refs[used : used + 3]
    source_ref, source_sem, h_ref, h_sem_ref, acc_ref, spare_ref = refs[used + 3 : used + 9]
    patch_ref, wide_ref, held_ref, sem_ref = refs[used + 9 :]
    fetched = fetch_blocks(near_refs, h_ref, h_sem_ref)
    for slot, weight_ref in zip(slots, weight_refs):
        owner = owner_of(slot)

        @pl.when((owner >= 0) & (owner < lax.axis_size("tile")))
        def _(owner=owner, weight_ref=weight_ref):
            pltpu.make_async_copy(weight_ref, held_ref.at[owner], sem_ref.at[owner]).start()

    source_copy = pltpu.make_async_copy(source_hbm_ref, source_ref, source_sem)
    source_copy.start()
    acc_ref[...] = jnp.zeros_like(acc_ref)
    wide_ref[...] = jnp.zeros_like(wide_ref)
    for copy in fetched:
        copy.wait()
    for block in range(h_ref.shape[0]):
        pltpu.make_async_copy(weight_refs[0], held_ref.at[block], sem_ref.at[block]).wait()
        buffer_ref = (patch_ref, spare_ref)[block % 2]
        add_block(h_ref, block, held_ref.at[block], buffer_ref, wide_ref, acc_ref)
    join_wide(patch_ref, wide_ref, acc_ref)
    frames, cols, rows = h_ref.shape[1:4]
    mask = column_mask(cols, window_limit(extents_ref, cols))
    source_copy.wait()
    source = source_ref[...].astype(jnp.float32)
    done = (source + result_of(acc_ref, frames, cols, rows)) * mask
    done = done.astype(jnp.bfloat16)
    out_refs[0][...] = done[:, : cols - INTERSECTION]
    out_refs[1][...] = done[:, cols - INTERSECTION :]
    out_refs[2][...] = blend_ramp(extents_ref, out_refs[2].shape)


def relayed(weight):
    tiles, subs = lax.axis_size("tile"), lax.axis_size("sub")
    out_share = weight.shape[4] // lax.axis_size("groups")
    own = lax.dynamic_slice_in_dim(weight, lax.axis_index("groups") * out_share, out_share, 4)
    own = own.reshape(3, -1, out_share)
    held, pieces = own, [own]
    for step in range(1, tiles):
        pairs = [(z * subs, (z + 1) * subs + 1) for z in range(step - 1, tiles - 1)]
        pairs += [(z * subs + 1, (z - 1) * subs) for z in range(1, tiles - step + 1)]
        arrived = lax.ppermute(held, ("tile", "sub"), pairs)
        held = lax.ppermute(arrived, "sub", [(0, 1), (1, 0)])
        pieces += [arrived, held]
    return pieces


def by_distance(array):
    got = [array]
    for code in range(1, 4):
        pairs = [(i, i ^ code) for i in range(4)]
        got.append(lax.ppermute(array, ("groups", "chan"), pairs))
    return got


def share_plan(latent, extents, gain_one, weight_one, gain_two, weight_two):
    frame_count, row_count, col_count, chan_count = latent.shape
    tiles, clips = lax.axis_size("tile"), lax.axis_size("groups")
    sub = lax.axis_index("sub")
    span = col_count + INTERSECTION
    share = chan_count // clips
    frames = clips * frame_count
    pitch = (span + 1) * row_count
    taps = weight_one.shape[1] * weight_one.shape[2]
    vmem, smem = pl.BlockSpec(memory_space=pltpu.VMEM), pl.BlockSpec(memory_space=pltpu.SMEM)
    anywhere = pl.BlockSpec(memory_space=pl.ANY)
    final = jax.ShapeDtypeStruct((frames, span, row_count, share), jnp.bfloat16)
    blocks = jax.ShapeDtypeStruct((tiles,) + final.shape, jnp.bfloat16)
    total = jax.ShapeDtypeStruct((frames * pitch, share), jnp.float32)

    def scratch(slots):
        return [
            pltpu.VMEM((frames + 2, pitch, taps * LANES), jnp.bfloat16),
            pltpu.VMEM(((frames + 1) * pitch, 2 * share), jnp.float32),
            pltpu.VMEM((len(slots), 3, taps * LANES, share), jnp.bfloat16),
            pltpu.SemaphoreType.DMA((len(slots),)),
        ]

    def chosen(weights, slots):
        return [weights[slot] for slot in slots]

    acc_scratch = [pltpu.VMEM(total.shape, jnp.float32)]

    by_col = jnp.transpose(latent, (0, 2, 1, 3))
    incoming = shifted(by_col[:, :INTERSECTION], "tile", -1)
    window = jnp.concatenate([by_col, incoming], axis=1)
    windows = []
    for turn in range(2):
        for away in range(2):
            pairs = [
                ((c * 2 + (x ^ away)) * 2 + (g ^ turn), (g * 2 + x) * 2 + c)
                for g in range(2)
                for x in range(2)
                for c in range(2)
            ]
            windows.append(lax.ppermute(window, ("groups", "chan", "sub"), pairs))
    first_weights = relayed(weight_one)
    second_weights = relayed(weight_two)
    own_gain = gain_one.reshape(1, -1)
    other_gain = lax.ppermute(own_gain, "chan", [(0, 1), (1, 0)])
    slots = tuple(range(2 * tiles - 1))
    early, middle, late = slots[:3], slots[3:-2], slots[-2:]
    hidden, source, begun = pl.pallas_call(
        functools.partial(first_begin, early),
        out_shape=(blocks, final, total),
        in_specs=[smem] + [vmem] * 6 + [anywhere] * len(early),
        out_specs=(vmem,) * 3,
        scratch_shapes=scratch(early),
        compiler_params=pltpu.CompilerParams(vmem_limit_bytes=GRANT),
    )(extents, own_gain, other_gain, *windows, *chosen(first_weights, early))
    begun = pl.pallas_call(
        functools.partial(first_more, middle),
        out_shape=total,
        in_specs=[vmem] * 2 + [anywhere] * len(middle),
        out_specs=vmem,
        scratch_shapes=scratch(middle),
        compiler_params=pltpu.CompilerParams(vmem_limit_bytes=GRANT),
    )(hidden, begun, *chosen(first_weights, middle))
    hidden_two = pl.pallas_call(
        functools.partial(first_end, late),
        out_shape=final,
        in_specs=[smem] + [vmem] * 3 + [anywhere] * len(late),
        out_specs=vmem,
        scratch_shapes=acc_scratch + scratch(late),
        compiler_params=pltpu.CompilerParams(vmem_limit_bytes=GRANT),
    )(extents, gain_two.reshape(1, -1), hidden, begun, *chosen(first_weights, late))
    near = by_distance(hidden_two)
    near = [near[0], near[2], near[1], near[3]]
    kept = jax.ShapeDtypeStruct((frames, col_count, row_count, share), jnp.bfloat16)
    ramps = jax.ShapeDtypeStruct((2 * INTERSECTION, share), jnp.float32)
    passed = jax.ShapeDtypeStruct((frames, INTERSECTION, row_count, share), jnp.bfloat16)
    own, tail, ramp = pl.pallas_call(
        functools.partial(second_kernel, slots),
        out_shape=(kept, passed, ramps),
        in_specs=[smem] + [anywhere] * (1 + tiles + len(slots)),
        out_specs=(vmem,) * 3,
        scratch_shapes=[
            pltpu.VMEM(final.shape, jnp.bfloat16),
            pltpu.SemaphoreType.DMA,
            pltpu.VMEM(blocks.shape, jnp.bfloat16),
            pltpu.SemaphoreType.DMA((tiles,)),
        ]
        + acc_scratch
        + scratch(slots[:tiles])[:1]
        + scratch(slots[:tiles]),
        compiler_params=pltpu.CompilerParams(vmem_limit_bytes=LAST_GRANT),
    )(extents, source, *near, *chosen(second_weights, slots))

    onward = [
        ((g * tiles + z) * 2 + c, (c * tiles + z + 1) * 2 + g)
        for g in range(2)
        for z in range(tiles - 1)
        for c in range(2)
    ]
    tail = lax.ppermute(tail, ("groups", "tile", "sub"), onward)
    own = lax.ppermute(own, ("groups", "sub"), [(0, 0), (1, 2), (2, 1), (3, 3)])

    def frames_here(array):
        halves = array.reshape((2, frame_count) + array.shape[1:])
        mine = lax.dynamic_index_in_dim(halves, sub, 0, keepdims=False)
        other = lax.dynamic_index_in_dim(halves, 1 - sub, 0, keepdims=False)
        other = lax.ppermute(other, "sub", [(0, 1), (1, 0)])
        straight = jnp.concatenate([mine, other], axis=3)
        crossed = jnp.concatenate([other, mine], axis=3)
        return jnp.where(sub == 0, straight, crossed)

    own, tail = frames_here(own), frames_here(tail)
    ramp = ramp[None, :, None, :1]
    head = jnp.repeat(own[:, :INTERSECTION].astype(jnp.float32), 2, axis=1) * ramp + jnp.repeat(
        tail.astype(jnp.float32), 2, axis=1
    ) * (1.0 - ramp)
    rest = jnp.repeat(own[:, INTERSECTION:], 2, axis=1)
    decoded = jnp.concatenate([head.astype(jnp.bfloat16), rest], axis=1)
    decoded = jnp.repeat(decoded, 2, axis=2)
    return jnp.transpose(decoded, (0, 2, 1, 3))


def solution(mesh):
    placed = (
        P(("groups", "sub"), None, "tile", "chan"),
        P(),
        P("chan"),
        P(None, None, None, "tile", "chan"),
        P("chan"),
        P(None, None, None, "tile", "chan"),
    )
    sizes = mesh.shape
    pairs_up = sizes["groups"] == 2 and sizes["sub"] == 2 and sizes["chan"] == 2
    few = pairs_up and CH // sizes["tile"] == LANES

    def body(*arrays):
        return (share_plan if few else gather_plan)(*arrays)

    return jax.shard_map(
        body,
        mesh=mesh,
        in_specs=placed,
        out_specs=P(("groups", "sub"), None, "tile", "chan"),
        check_vma=False,
    )
```

```python
import functools

import jax
import jax.numpy as jnp
from jax import lax
from jax.experimental import pallas as pl
from jax.experimental.pallas import tpu as pltpu
from jax.sharding import PartitionSpec as P


CH = 512
GROUPS = 32
INTERSECTION = 4
LANES = 128
GRANT = 12 * 2**20
LAST_GRANT = 60 * 2**20


eps = 1e-06


def shifted(array, axis, by):
    peers = lax.axis_size(axis)
    pairs = [(i, i + by) for i in range(peers) if 0 <= i + by < peers]
    return lax.ppermute(array, axis, pairs)


def ramp_after(prior):
    positions = jnp.arange(2 * INTERSECTION).astype(jnp.float32) + 0.5
    limit = (2 * prior).astype(jnp.float32)[..., None]
    denom = (2 * jnp.maximum(prior, 1)).astype(jnp.float32)[..., None]
    return jnp.where(positions < limit, positions / denom, 1.0)


def convolve(inputs, kernel):
    result = lax.conv_general_dilated(
        inputs[None],
        kernel,
        (1, 1, 1),
        [(0, 0), (1, 1), (1, 1)],
        dimension_numbers=("NDHWC", "DHWIO", "NDHWC"),
        preferred_element_type=jnp.float32,
    )
    return result[0]


def group_norm(values, gain, count):
    group_size = CH // GROUPS
    grouped = values.reshape(values.shape[:-1] + (values.shape[-1] // group_size, group_size))
    totals, squares = lax.psum(
        (jnp.sum(grouped, axis=(0, 1, 2, 4)), jnp.sum(grouped * grouped, axis=(0, 1, 2, 4))), "sub"
    )
    size = count * group_size
    mean_val = totals / size
    variance = squares / size - mean_val * mean_val
    scaled = (grouped - mean_val[:, None]) * lax.rsqrt(variance + eps)[:, None]
    return scaled.reshape(values.shape) * gain


def causal_pad(values):
    earlier = shifted(values[-2:], "sub", 1)
    repeated = jnp.concatenate([values[:1], values[:1]], axis=0)
    leading = jnp.where(lax.axis_index("sub") == 0, repeated, earlier)
    return jnp.concatenate([leading, values], axis=0)


def channel_conv(padded_in, weight):
    full_in = lax.all_gather(padded_in, "chan", axis=3, tiled=True)
    out_count = weight.shape[4]
    share = weight.shape[3] // lax.axis_size("sub")
    portion = lax.dynamic_slice_in_dim(weight, lax.axis_index("sub") * share, share, 3)
    fetched = lax.all_gather(portion, "tile", axis=3, tiled=True)
    sectioned = fetched.reshape(3, 3, 3, lax.axis_size("tile"), 1, share, out_count)
    whole = lax.all_gather(sectioned, "sub", axis=4, tiled=True).reshape(3, 3, 3, -1, out_count)
    return convolve(full_in, whole)


def upscale(values):
    return jnp.repeat(jnp.repeat(values, 2, axis=1), 2, axis=2)


def reach_and_prior(extents):
    tile_count = lax.axis_size("tile")
    place = lax.axis_index("tile")
    tile_ids = jnp.arange(tile_count, dtype=jnp.int32)
    reaches = jnp.where(tile_ids == tile_count - 1, 0, extents)
    reach = jnp.sum(jnp.where(tile_ids == place, reaches, 0))
    prior = jnp.sum(jnp.where(tile_ids == place - 1, reaches, 0))
    return reach, prior


def gather_plan(latent, extents, gain_one, weight_one, gain_two, weight_two):
    frame_count, row_count, col_count, _ = latent.shape
    reach, prior = reach_and_prior(extents)
    incoming = shifted(latent[:, :, :INTERSECTION, :], "tile", -1)
    window = jnp.concatenate([latent, incoming], axis=2)
    valid = (jnp.arange(col_count + INTERSECTION, dtype=jnp.int32) < col_count + reach).astype(
        jnp.float32
    )
    mask = valid[None, None, :, None]
    window = jnp.where(mask > 0, window, jnp.zeros_like(window))
    count = (col_count + reach).astype(jnp.float32) * (
        frame_count * lax.axis_size("sub") * row_count
    )
    source = window.astype(jnp.float32)
    hidden = (jax.nn.silu(group_norm(source, gain_one, count)) * mask).astype(jnp.bfloat16)
    first = (channel_conv(causal_pad(hidden), weight_one) * mask).astype(jnp.bfloat16)
    first = lax.optimization_barrier(first)
    hidden_two = (
        jax.nn.silu(group_norm(first.astype(jnp.float32), gain_two, count)) * mask
    ).astype(jnp.bfloat16)
    second = channel_conv(causal_pad(hidden_two), weight_two)
    result = ((source + second) * mask).astype(jnp.bfloat16)
    larger = upscale(result)
    own = larger[:, :, : 2 * col_count]
    arrived = shifted(larger[:, :, 2 * col_count :], "tile", 1)
    ramp = ramp_after(prior)[None, None, :, None]
    head = own[:, :, : 2 * INTERSECTION].astype(jnp.float32) * ramp + arrived.astype(
        jnp.float32
    ) * (1.0 - ramp)
    return jnp.concatenate([head.astype(jnp.bfloat16), own[:, :, 2 * INTERSECTION :]], axis=2)


def normalized(values, gain, count, mask):
    chans = values.shape[-1]
    group_size = CH // GROUPS
    rows = lax.broadcasted_iota(jnp.int32, (chans, chans), 0) // group_size
    cols = lax.broadcasted_iota(jnp.int32, (chans, chans), 1) // group_size
    same = (rows == cols).astype(jnp.float32)
    total = jnp.sum(values, axis=(0, 1, 2)).reshape(1, chans)
    square = jnp.sum(values * values, axis=(0, 1, 2)).reshape(1, chans)
    both = jnp.concatenate([jnp.broadcast_to(total, (8, chans)), jnp.broadcast_to(square, (8, chans))], 0)
    sums = jnp.dot(both, same, precision=lax.Precision.HIGHEST, preferred_element_type=jnp.float32)
    size = count * group_size
    mean = sums[0:1] / size
    variance = sums[8:9] / size - mean * mean
    rate = lax.rsqrt(variance + eps)
    shape = (1, 1, 1, chans)
    scaled = (values - mean.reshape(shape)) * rate.reshape(shape) * gain.reshape(shape)
    return (scaled / (1.0 + jnp.exp(-scaled))) * mask


def column_mask(cols, limit):
    ids = lax.broadcasted_iota(jnp.int32, (1, cols, 8, LANES), 1)
    return (ids < limit).astype(jnp.float32)


def window_limit(extents_ref, cols):
    place = lax.axis_index("tile")
    reach = jnp.where(place == lax.axis_size("tile") - 1, 0, extents_ref[place])
    return cols - INTERSECTION + reach


def blend_ramp(extents_ref, shape):
    place = lax.axis_index("tile")
    prior = jnp.where(place == 0, 0, extents_ref[jnp.maximum(place - 1, 0)])
    positions = lax.broadcasted_iota(jnp.int32, shape, 0).astype(jnp.float32) + 0.5
    limit = jnp.broadcast_to((2 * prior).astype(jnp.float32), shape)
    denom = jnp.broadcast_to((2 * jnp.maximum(prior, 1)).astype(jnp.float32), shape)
    return jnp.where(positions < limit, positions / denom, 1.0)


def owner_of(slot):
    step = (slot + 1) // 2
    ahead = (lax.axis_index("sub") == 0) == (slot % 2 == 1)
    return lax.axis_index("tile") + jnp.where(ahead, step, -step)


def prepare(limit, gain_refs, win_refs, h_ref, source_ref):
    clip, chan = lax.axis_index("groups"), lax.axis_index("chan")
    frames, cols, rows, width = win_refs[0].shape
    count = limit.astype(jnp.float32) * (2 * frames * rows)
    mask = column_mask(cols, limit)
    for away, gain_ref in enumerate(gain_refs):
        for piece in range(width // LANES):
            lanes = slice(piece * LANES, (piece + 1) * LANES)
            both = [win_refs[2 * turn + away][:, :, :, lanes] for turn in range(2)]
            values = jnp.concatenate(both, 0).astype(jnp.float32)
            values = jnp.where(mask > 0, values, 0.0)
            done = normalized(values, gain_ref[:, lanes], count, mask).astype(jnp.bfloat16)
            block = (chan ^ away) * (width // LANES) + piece
            for turn in range(2):
                rows_at = pl.ds((clip ^ turn) * frames, frames)
                h_ref[block, rows_at] = done[turn * frames : (turn + 1) * frames]
                if away == 0:

                    @pl.when(clip == piece)
                    def _(rows_at=rows_at, turn=turn, both=both):
                        source_ref[rows_at] = both[turn]


def fill_patches(h_ref, block, patch_ref):
    frames, cols, rows, width = h_ref.shape[1:]
    ids = lax.broadcasted_iota(jnp.int32, (cols, rows, width), 1)
    empty = jnp.zeros((rows, width), jnp.float32)
    for t in range(frames):
        here = h_ref[block, t].astype(jnp.float32)
        for b in range(3):
            if b == 1:
                moved = here
            else:
                moved = pltpu.roll(here, 1 if b == 0 else rows - 1, 1)
                moved = jnp.where(ids == (0 if b == 0 else rows - 1), 0.0, moved)
            flat = moved.reshape(cols * rows, width)
            for d in range(3):
                if d == 0:
                    piece = jnp.concatenate([empty, flat], 0)
                elif d == 1:
                    piece = jnp.concatenate([flat, empty], 0)
                else:
                    piece = jnp.concatenate([flat[rows:], empty, empty], 0)
                piece = piece.astype(jnp.bfloat16)
                lane = (b * 3 + d) * width
                patch_ref[t + 2, :, lane : lane + width] = piece
                if t == 0:
                    patch_ref[0, :, lane : lane + width] = piece
                    patch_ref[1, :, lane : lane + width] = piece


def add_block(h_ref, block, weight_ref, patch_ref, wide_ref, acc_ref):
    fill_patches(h_ref, block, patch_ref)
    frames = h_ref.shape[1]
    pitch, depth = patch_ref.shape[1:]
    both = jnp.concatenate([weight_ref[0], weight_ref[1]], axis=1)
    left = patch_ref[: frames + 1].reshape((frames + 1) * pitch, depth)
    wide_ref[...] += jnp.dot(left, both, preferred_element_type=jnp.float32)
    left = patch_ref[2:].reshape(frames * pitch, depth)
    acc_ref[...] += jnp.dot(left, weight_ref[2], preferred_element_type=jnp.float32)


def weight_copies(slots, weight_refs, held_ref, sem_ref):
    copies = []
    for i, (slot, weight_ref) in enumerate(zip(slots, weight_refs)):
        owner = owner_of(slot)
        there = (owner >= 0) & (owner < lax.axis_size("tile"))
        copy = pltpu.make_async_copy(weight_ref, held_ref.at[i], sem_ref.at[i])
        copies.append((owner, there, copy))
    return copies


def start_weights(copies):
    for _, there, copy in copies:

        @pl.when(there)
        def _(copy=copy):
            copy.start()


def add_blocks(copies, h_ref, held_ref, patch_ref, wide_ref, acc_ref):
    wide_ref[...] = jnp.zeros_like(wide_ref)
    for i, (owner, there, copy) in enumerate(copies):

        @pl.when(there)
        def _(i=i, owner=owner, copy=copy):
            copy.wait()
            add_block(h_ref, owner, held_ref.at[i], patch_ref, wide_ref, acc_ref)

    join_wide(patch_ref, wide_ref, acc_ref)


def join_wide(patch_ref, wide_ref, acc_ref):
    shift = patch_ref.shape[1]
    count = acc_ref.shape[0]
    acc_ref[...] += wide_ref[:count, :LANES] + wide_ref[shift : shift + count, LANES:]


def result_of(acc_ref, frames, cols, rows):
    pitch = acc_ref.shape[0] // frames
    whole = acc_ref[...].reshape(frames, pitch, LANES)
    return whole[:, : cols * rows].reshape(frames, cols, rows, LANES)


def fetch_blocks(near_refs, h_ref, sem_ref):
    own = lax.axis_index("chan") * 2 + lax.axis_index("groups")
    copies = [
        pltpu.make_async_copy(near_ref, h_ref.at[own ^ code], sem_ref.at[code])
        for code, near_ref in enumerate(near_refs)
    ]
    for copy in copies:
        copy.start()
    return copies


def first_begin(slots, extents_ref, gain_ref, far_gain_ref, *refs):
    used = 4 + len(slots)
    win_refs, weight_refs = refs[:4], refs[4:used]
    h_ref, source_ref, acc_ref, patch_ref, wide_ref, held_ref, sem_ref = refs[used:]
    copies = weight_copies(slots, weight_refs, held_ref, sem_ref)
    start_weights(copies)
    limit = window_limit(extents_ref, h_ref.shape[2])
    prepare(limit, (gain_ref, far_gain_ref), win_refs, h_ref, source_ref)
    acc_ref[...] = jnp.zeros_like(acc_ref)
    add_blocks(copies, h_ref, held_ref, patch_ref, wide_ref, acc_ref)


def first_more(slots, h_ref, begun_ref, *refs):
    weight_refs = refs[: len(slots)]
    acc_ref, patch_ref, wide_ref, held_ref, sem_ref = refs[len(slots) :]
    copies = weight_copies(slots, weight_refs, held_ref, sem_ref)
    start_weights(copies)
    acc_ref[...] = begun_ref[...]
    add_blocks(copies, h_ref, held_ref, patch_ref, wide_ref, acc_ref)


def first_end(slots, extents_ref, gain_ref, h_ref, begun_ref, *refs):
    weight_refs = refs[: len(slots)]
    out_ref, acc_ref, patch_ref, wide_ref, held_ref, sem_ref = refs[len(slots) :]
    copies = weight_copies(slots, weight_refs, held_ref, sem_ref)
    start_weights(copies)
    acc_ref[...] = begun_ref[...]
    add_blocks(copies, h_ref, held_ref, patch_ref, wide_ref, acc_ref)
    frames, cols, rows = h_ref.shape[1:4]
    limit = window_limit(extents_ref, cols)
    mask = column_mask(cols, limit)
    count = limit.astype(jnp.float32) * (frames * rows)
    first = (result_of(acc_ref, frames, cols, rows) * mask).astype(jnp.bfloat16)
    share = pl.multiple_of(lax.axis_index("groups") * LANES, LANES)
    gain = gain_ref[:, pl.ds(share, LANES)]
    done = normalized(first.astype(jnp.float32), gain, count, mask)
    out_ref[...] = done.astype(jnp.bfloat16)


def second_kernel(slots, extents_ref, source_hbm_ref, *refs):
    used = 4 + 2 * len(slots)
    near_refs, weight_refs, out_refs = refs[:4], refs[4:used], refs[used : used + 3]
    source_ref, source_sem, h_ref, h_sem_ref, acc_ref, spare_ref = refs[used + 3 : used + 9]
    patch_ref, wide_ref, held_ref, sem_ref = refs[used + 9 :]
    fetched = fetch_blocks(near_refs, h_ref, h_sem_ref)

    def chunk_copy(owner, chunk, weight_ref):
        rows_at = slice(0, 2) if chunk == 0 else slice(2, 3)
        target = held_ref.at[owner, rows_at]
        return pltpu.make_async_copy(weight_ref, target, sem_ref.at[owner, chunk])

    for i, slot in enumerate(slots):
        owner = owner_of(slot)

        @pl.when((owner >= 0) & (owner < lax.axis_size("tile")))
        def _(owner=owner, i=i):
            for chunk in range(2):
                chunk_copy(owner, chunk, weight_refs[2 * i + chunk]).start()

    source_copy = pltpu.make_async_copy(source_hbm_ref, source_ref, source_sem)
    source_copy.start()
    acc_ref[...] = jnp.zeros_like(acc_ref)
    wide_ref[...] = jnp.zeros_like(wide_ref)
    for copy in fetched:
        copy.wait()
    for block in range(h_ref.shape[0]):
        for chunk in range(2):
            chunk_copy(block, chunk, weight_refs[chunk]).wait()
        buffer_ref = (patch_ref, spare_ref)[block % 2]
        add_block(h_ref, block, held_ref.at[block], buffer_ref, wide_ref, acc_ref)
    join_wide(patch_ref, wide_ref, acc_ref)
    frames, cols, rows = h_ref.shape[1:4]
    mask = column_mask(cols, window_limit(extents_ref, cols))
    source_copy.wait()
    source = source_ref[...].astype(jnp.float32)
    done = (source + result_of(acc_ref, frames, cols, rows)) * mask
    done = done.astype(jnp.bfloat16)
    out_refs[0][...] = done[:, : cols - INTERSECTION]
    out_refs[1][...] = done[:, cols - INTERSECTION :]
    out_refs[2][...] = blend_ramp(extents_ref, out_refs[2].shape)


def relayed(weight, cuts):
    tiles, subs = lax.axis_size("tile"), lax.axis_size("sub")
    out_share = weight.shape[4] // lax.axis_size("groups")
    own = lax.dynamic_slice_in_dim(weight, lax.axis_index("groups") * out_share, out_share, 4)
    own = own.reshape(3, -1, out_share)
    held = [own[first:last] for first, last in zip(cuts, cuts[1:])]
    pieces = [held]
    for step in range(1, tiles):
        pairs = [(z * subs, (z + 1) * subs + 1) for z in range(step - 1, tiles - 1)]
        pairs += [(z * subs + 1, (z - 1) * subs) for z in range(1, tiles - step + 1)]
        arrived, swapped = [], []
        for i, chunk in enumerate(held):
            arrived.append(lax.ppermute(chunk, ("tile", "sub"), pairs))
            swapped.append(lax.ppermute(arrived[i], "sub", [(0, 1), (1, 0)]))
        held = swapped
        pieces += [arrived, held]
    return pieces


def by_distance(array):
    got = [array]
    for code in range(1, 4):
        pairs = [(i, i ^ code) for i in range(4)]
        got.append(lax.ppermute(array, ("groups", "chan"), pairs))
    return got


def share_plan(latent, extents, gain_one, weight_one, gain_two, weight_two):
    frame_count, row_count, col_count, chan_count = latent.shape
    tiles, clips = lax.axis_size("tile"), lax.axis_size("groups")
    sub = lax.axis_index("sub")
    span = col_count + INTERSECTION
    share = chan_count // clips
    frames = clips * frame_count
    pitch = (span + 1) * row_count
    taps = weight_one.shape[1] * weight_one.shape[2]
    vmem, smem = pl.BlockSpec(memory_space=pltpu.VMEM), pl.BlockSpec(memory_space=pltpu.SMEM)
    anywhere = pl.BlockSpec(memory_space=pl.ANY)
    final = jax.ShapeDtypeStruct((frames, span, row_count, share), jnp.bfloat16)
    blocks = jax.ShapeDtypeStruct((tiles,) + final.shape, jnp.bfloat16)
    total = jax.ShapeDtypeStruct((frames * pitch, share), jnp.float32)

    def scratch(slots):
        return [
            pltpu.VMEM((frames + 2, pitch, taps * LANES), jnp.bfloat16),
            pltpu.VMEM(((frames + 1) * pitch, 2 * share), jnp.float32),
            pltpu.VMEM((len(slots), 3, taps * LANES, share), jnp.bfloat16),
            pltpu.SemaphoreType.DMA((len(slots),)),
        ]

    def chosen(weights, slots):
        return [chunk for slot in slots for chunk in weights[slot]]

    acc_scratch = [pltpu.VMEM(total.shape, jnp.float32)]

    by_col = jnp.transpose(latent, (0, 2, 1, 3))
    incoming = shifted(by_col[:, :INTERSECTION], "tile", -1)
    window = jnp.concatenate([by_col, incoming], axis=1)
    windows = []
    for turn in range(2):
        for away in range(2):
            pairs = [
                ((c * 2 + (x ^ away)) * 2 + (g ^ turn), (g * 2 + x) * 2 + c)
                for g in range(2)
                for x in range(2)
                for c in range(2)
            ]
            windows.append(lax.ppermute(window, ("groups", "chan", "sub"), pairs))
    first_weights = relayed(weight_one, (0, 3))
    second_weights = relayed(weight_two, (0, 2, 3))
    own_gain = gain_one.reshape(1, -1)
    other_gain = lax.ppermute(own_gain, "chan", [(0, 1), (1, 0)])
    slots = tuple(range(2 * tiles - 1))
    early, middle, late = slots[:3], slots[3:-2], slots[-2:]
    hidden, source, begun = pl.pallas_call(
        functools.partial(first_begin, early),
        out_shape=(blocks, final, total),
        in_specs=[smem] + [vmem] * 6 + [anywhere] * len(early),
        out_specs=(vmem,) * 3,
        scratch_shapes=scratch(early),
        compiler_params=pltpu.CompilerParams(vmem_limit_bytes=GRANT),
    )(extents, own_gain, other_gain, *windows, *chosen(first_weights, early))
    begun = pl.pallas_call(
        functools.partial(first_more, middle),
        out_shape=total,
        in_specs=[vmem] * 2 + [anywhere] * len(middle),
        out_specs=vmem,
        scratch_shapes=scratch(middle),
        compiler_params=pltpu.CompilerParams(vmem_limit_bytes=GRANT),
    )(hidden, begun, *chosen(first_weights, middle))
    hidden_two = pl.pallas_call(
        functools.partial(first_end, late),
        out_shape=final,
        in_specs=[smem] + [vmem] * 3 + [anywhere] * len(late),
        out_specs=vmem,
        scratch_shapes=acc_scratch + scratch(late),
        compiler_params=pltpu.CompilerParams(vmem_limit_bytes=GRANT),
    )(extents, gain_two.reshape(1, -1), hidden, begun, *chosen(first_weights, late))
    near = by_distance(hidden_two)
    near = [near[0], near[2], near[1], near[3]]
    kept = jax.ShapeDtypeStruct((frames, col_count, row_count, share), jnp.bfloat16)
    ramps = jax.ShapeDtypeStruct((2 * INTERSECTION, share), jnp.float32)
    passed = jax.ShapeDtypeStruct((frames, INTERSECTION, row_count, share), jnp.bfloat16)
    own, tail, ramp = pl.pallas_call(
        functools.partial(second_kernel, slots),
        out_shape=(kept, passed, ramps),
        in_specs=[smem] + [anywhere] * (1 + tiles + 2 * len(slots)),
        out_specs=(vmem,) * 3,
        scratch_shapes=[
            pltpu.VMEM(final.shape, jnp.bfloat16),
            pltpu.SemaphoreType.DMA,
            pltpu.VMEM(blocks.shape, jnp.bfloat16),
            pltpu.SemaphoreType.DMA((tiles,)),
        ]
        + acc_scratch
        + scratch(slots[:tiles])[:1]
        + scratch(slots[:tiles])[:3]
        + [pltpu.SemaphoreType.DMA((tiles, 2))],
        compiler_params=pltpu.CompilerParams(vmem_limit_bytes=LAST_GRANT),
    )(extents, source, *near, *chosen(second_weights, slots))

    onward = [
        ((g * tiles + z) * 2 + c, (c * tiles + z + 1) * 2 + g)
        for g in range(2)
        for z in range(tiles - 1)
        for c in range(2)
    ]
    tail = lax.ppermute(tail, ("groups", "tile", "sub"), onward)
    own = lax.ppermute(own, ("groups", "sub"), [(0, 0), (1, 2), (2, 1), (3, 3)])

    def frames_here(array):
        halves = array.reshape((2, frame_count) + array.shape[1:])
        mine = lax.dynamic_index_in_dim(halves, sub, 0, keepdims=False)
        other = lax.dynamic_index_in_dim(halves, 1 - sub, 0, keepdims=False)
        other = lax.ppermute(other, "sub", [(0, 1), (1, 0)])
        straight = jnp.concatenate([mine, other], axis=3)
        crossed = jnp.concatenate([other, mine], axis=3)
        return jnp.where(sub == 0, straight, crossed)

    own, tail = frames_here(own), frames_here(tail)
    ramp = ramp[None, :, None, :1]
    head = jnp.repeat(own[:, :INTERSECTION].astype(jnp.float32), 2, axis=1) * ramp + jnp.repeat(
        tail.astype(jnp.float32), 2, axis=1
    ) * (1.0 - ramp)
    rest = jnp.repeat(own[:, INTERSECTION:], 2, axis=1)
    decoded = jnp.concatenate([head.astype(jnp.bfloat16), rest], axis=1)
    decoded = jnp.repeat(decoded, 2, axis=2)
    return jnp.transpose(decoded, (0, 2, 1, 3))


def solution(mesh):
    placed = (
        P(("groups", "sub"), None, "tile", "chan"),
        P(),
        P("chan"),
        P(None, None, None, "tile", "chan"),
        P("chan"),
        P(None, None, None, "tile", "chan"),
    )
    sizes = mesh.shape
    pairs_up = sizes["groups"] == 2 and sizes["sub"] == 2 and sizes["chan"] == 2
    few = pairs_up and CH // sizes["tile"] == LANES

    def body(*arrays):
        return (share_plan if few else gather_plan)(*arrays)

    return jax.shard_map(
        body,
        mesh=mesh,
        in_specs=placed,
        out_specs=P(("groups", "sub"), None, "tile", "chan"),
        check_vma=False,
    )
```

```python
import functools

import jax
import jax.numpy as jnp
from jax import lax
from jax.experimental import pallas as pl
from jax.experimental.pallas import tpu as pltpu
from jax.sharding import PartitionSpec as P


CH = 512
GROUPS = 32
INTERSECTION = 4
LANES = 128
GRANT = 12 * 2**20
LAST_GRANT = 60 * 2**20


eps = 1e-06


def shifted(array, axis, by):
    peers = lax.axis_size(axis)
    pairs = [(i, i + by) for i in range(peers) if 0 <= i + by < peers]
    return lax.ppermute(array, axis, pairs)


def ramp_after(prior):
    positions = jnp.arange(2 * INTERSECTION).astype(jnp.float32) + 0.5
    limit = (2 * prior).astype(jnp.float32)[..., None]
    denom = (2 * jnp.maximum(prior, 1)).astype(jnp.float32)[..., None]
    return jnp.where(positions < limit, positions / denom, 1.0)


def convolve(inputs, kernel):
    result = lax.conv_general_dilated(
        inputs[None],
        kernel,
        (1, 1, 1),
        [(0, 0), (1, 1), (1, 1)],
        dimension_numbers=("NDHWC", "DHWIO", "NDHWC"),
        preferred_element_type=jnp.float32,
    )
    return result[0]


def group_norm(values, gain, count):
    group_size = CH // GROUPS
    grouped = values.reshape(values.shape[:-1] + (values.shape[-1] // group_size, group_size))
    totals, squares = lax.psum(
        (jnp.sum(grouped, axis=(0, 1, 2, 4)), jnp.sum(grouped * grouped, axis=(0, 1, 2, 4))), "sub"
    )
    size = count * group_size
    mean_val = totals / size
    variance = squares / size - mean_val * mean_val
    scaled = (grouped - mean_val[:, None]) * lax.rsqrt(variance + eps)[:, None]
    return scaled.reshape(values.shape) * gain


def causal_pad(values):
    earlier = shifted(values[-2:], "sub", 1)
    repeated = jnp.concatenate([values[:1], values[:1]], axis=0)
    leading = jnp.where(lax.axis_index("sub") == 0, repeated, earlier)
    return jnp.concatenate([leading, values], axis=0)


def channel_conv(padded_in, weight):
    full_in = lax.all_gather(padded_in, "chan", axis=3, tiled=True)
    out_count = weight.shape[4]
    share = weight.shape[3] // lax.axis_size("sub")
    portion = lax.dynamic_slice_in_dim(weight, lax.axis_index("sub") * share, share, 3)
    fetched = lax.all_gather(portion, "tile", axis=3, tiled=True)
    sectioned = fetched.reshape(3, 3, 3, lax.axis_size("tile"), 1, share, out_count)
    whole = lax.all_gather(sectioned, "sub", axis=4, tiled=True).reshape(3, 3, 3, -1, out_count)
    return convolve(full_in, whole)


def upscale(values):
    return jnp.repeat(jnp.repeat(values, 2, axis=1), 2, axis=2)


def reach_and_prior(extents):
    tile_count = lax.axis_size("tile")
    place = lax.axis_index("tile")
    tile_ids = jnp.arange(tile_count, dtype=jnp.int32)
    reaches = jnp.where(tile_ids == tile_count - 1, 0, extents)
    reach = jnp.sum(jnp.where(tile_ids == place, reaches, 0))
    prior = jnp.sum(jnp.where(tile_ids == place - 1, reaches, 0))
    return reach, prior


def gather_plan(latent, extents, gain_one, weight_one, gain_two, weight_two):
    frame_count, row_count, col_count, _ = latent.shape
    reach, prior = reach_and_prior(extents)
    incoming = shifted(latent[:, :, :INTERSECTION, :], "tile", -1)
    window = jnp.concatenate([latent, incoming], axis=2)
    valid = (jnp.arange(col_count + INTERSECTION, dtype=jnp.int32) < col_count + reach).astype(
        jnp.float32
    )
    mask = valid[None, None, :, None]
    window = jnp.where(mask > 0, window, jnp.zeros_like(window))
    count = (col_count + reach).astype(jnp.float32) * (
        frame_count * lax.axis_size("sub") * row_count
    )
    source = window.astype(jnp.float32)
    hidden = (jax.nn.silu(group_norm(source, gain_one, count)) * mask).astype(jnp.bfloat16)
    first = (channel_conv(causal_pad(hidden), weight_one) * mask).astype(jnp.bfloat16)
    first = lax.optimization_barrier(first)
    hidden_two = (
        jax.nn.silu(group_norm(first.astype(jnp.float32), gain_two, count)) * mask
    ).astype(jnp.bfloat16)
    second = channel_conv(causal_pad(hidden_two), weight_two)
    result = ((source + second) * mask).astype(jnp.bfloat16)
    larger = upscale(result)
    own = larger[:, :, : 2 * col_count]
    arrived = shifted(larger[:, :, 2 * col_count :], "tile", 1)
    ramp = ramp_after(prior)[None, None, :, None]
    head = own[:, :, : 2 * INTERSECTION].astype(jnp.float32) * ramp + arrived.astype(
        jnp.float32
    ) * (1.0 - ramp)
    return jnp.concatenate([head.astype(jnp.bfloat16), own[:, :, 2 * INTERSECTION :]], axis=2)


def normalized(values, gain, count, mask):
    chans = values.shape[-1]
    group_size = CH // GROUPS
    rows = lax.broadcasted_iota(jnp.int32, (chans, chans), 0) // group_size
    cols = lax.broadcasted_iota(jnp.int32, (chans, chans), 1) // group_size
    same = (rows == cols).astype(jnp.float32)
    total = jnp.sum(values, axis=(0, 1, 2)).reshape(1, chans)
    square = jnp.sum(values * values, axis=(0, 1, 2)).reshape(1, chans)
    both = jnp.concatenate([jnp.broadcast_to(total, (8, chans)), jnp.broadcast_to(square, (8, chans))], 0)
    sums = jnp.dot(both, same, precision=lax.Precision.HIGHEST, preferred_element_type=jnp.float32)
    size = count * group_size
    mean = sums[0:1] / size
    variance = sums[8:9] / size - mean * mean
    rate = lax.rsqrt(variance + eps)
    shape = (1, 1, 1, chans)
    scaled = (values - mean.reshape(shape)) * rate.reshape(shape) * gain.reshape(shape)
    return (scaled / (1.0 + jnp.exp(-scaled))) * mask


def column_mask(cols, limit):
    ids = lax.broadcasted_iota(jnp.int32, (1, cols, 8, LANES), 1)
    return (ids < limit).astype(jnp.float32)


def window_limit(extents_ref, cols):
    place = lax.axis_index("tile")
    reach = jnp.where(place == lax.axis_size("tile") - 1, 0, extents_ref[place])
    return cols - INTERSECTION + reach


def blend_ramp(extents_ref, shape):
    place = lax.axis_index("tile")
    prior = jnp.where(place == 0, 0, extents_ref[jnp.maximum(place - 1, 0)])
    positions = lax.broadcasted_iota(jnp.int32, shape, 0).astype(jnp.float32) + 0.5
    limit = jnp.broadcast_to((2 * prior).astype(jnp.float32), shape)
    denom = jnp.broadcast_to((2 * jnp.maximum(prior, 1)).astype(jnp.float32), shape)
    return jnp.where(positions < limit, positions / denom, 1.0)


def owner_of(slot):
    step = (slot + 1) // 2
    ahead = (lax.axis_index("sub") == 0) == (slot % 2 == 1)
    return lax.axis_index("tile") + jnp.where(ahead, step, -step)


def prepare(limit, gain_refs, win_refs, h_ref, source_ref):
    clip, chan = lax.axis_index("groups"), lax.axis_index("chan")
    frames, cols, rows, width = win_refs[0].shape
    count = limit.astype(jnp.float32) * (2 * frames * rows)
    mask = column_mask(cols, limit)
    for away, gain_ref in enumerate(gain_refs):
        for piece in range(width // LANES):
            lanes = slice(piece * LANES, (piece + 1) * LANES)
            both = [win_refs[2 * turn + away][:, :, :, lanes] for turn in range(2)]
            values = jnp.concatenate(both, 0).astype(jnp.float32)
            values = jnp.where(mask > 0, values, 0.0)
            done = normalized(values, gain_ref[:, lanes], count, mask).astype(jnp.bfloat16)
            block = (chan ^ away) * (width // LANES) + piece
            for turn in range(2):
                rows_at = pl.ds((clip ^ turn) * frames, frames)
                h_ref[block, rows_at] = done[turn * frames : (turn + 1) * frames]
                if away == 0:

                    @pl.when(clip == piece)
                    def _(rows_at=rows_at, turn=turn, both=both):
                        source_ref[rows_at] = both[turn]


def fill_patches(h_ref, block, patch_ref):
    frames, cols, rows, width = h_ref.shape[1:]
    ids = lax.broadcasted_iota(jnp.int32, (cols, rows, width), 1)
    empty = jnp.zeros((rows, width), jnp.float32)
    for t in range(frames):
        here = h_ref[block, t].astype(jnp.float32)
        for b in range(3):
            if b == 1:
                moved = here
            else:
                moved = pltpu.roll(here, 1 if b == 0 else rows - 1, 1)
                moved = jnp.where(ids == (0 if b == 0 else rows - 1), 0.0, moved)
            flat = moved.reshape(cols * rows, width)
            for d in range(3):
                if d == 0:
                    piece = jnp.concatenate([empty, flat], 0)
                elif d == 1:
                    piece = jnp.concatenate([flat, empty], 0)
                else:
                    piece = jnp.concatenate([flat[rows:], empty, empty], 0)
                piece = piece.astype(jnp.bfloat16)
                lane = (b * 3 + d) * width
                patch_ref[t + 2, :, lane : lane + width] = piece
                if t == 0:
                    patch_ref[0, :, lane : lane + width] = piece
                    patch_ref[1, :, lane : lane + width] = piece


def add_block(h_ref, block, weight_ref, patch_ref, wide_ref, acc_ref):
    fill_patches(h_ref, block, patch_ref)
    frames = h_ref.shape[1]
    pitch, depth = patch_ref.shape[1:]
    both = jnp.concatenate([weight_ref[0], weight_ref[1]], axis=1)
    left = patch_ref[: frames + 1].reshape((frames + 1) * pitch, depth)
    wide_ref[...] += jnp.dot(left, both, preferred_element_type=jnp.float32)
    left = patch_ref[2:].reshape(frames * pitch, depth)
    acc_ref[...] += jnp.dot(left, weight_ref[2], preferred_element_type=jnp.float32)


def weight_copies(slots, weight_refs, held_ref, sem_ref):
    copies = []
    for i, (slot, weight_ref) in enumerate(zip(slots, weight_refs)):
        owner = owner_of(slot)
        there = (owner >= 0) & (owner < lax.axis_size("tile"))
        copy = pltpu.make_async_copy(weight_ref, held_ref.at[i], sem_ref.at[i])
        copies.append((owner, there, copy))
    return copies


def start_weights(copies):
    for _, there, copy in copies:

        @pl.when(there)
        def _(copy=copy):
            copy.start()


def add_blocks(copies, h_ref, held_ref, patch_ref, wide_ref, acc_ref):
    wide_ref[...] = jnp.zeros_like(wide_ref)
    for i, (owner, there, copy) in enumerate(copies):

        @pl.when(there)
        def _(i=i, owner=owner, copy=copy):
            copy.wait()
            add_block(h_ref, owner, held_ref.at[i], patch_ref, wide_ref, acc_ref)

    join_wide(patch_ref, wide_ref, acc_ref)


def join_wide(patch_ref, wide_ref, acc_ref):
    shift = patch_ref.shape[1]
    count = acc_ref.shape[0]
    acc_ref[...] += wide_ref[:count, :LANES] + wide_ref[shift : shift + count, LANES:]


def result_of(acc_ref, frames, cols, rows):
    pitch = acc_ref.shape[0] // frames
    whole = acc_ref[...].reshape(frames, pitch, LANES)
    return whole[:, : cols * rows].reshape(frames, cols, rows, LANES)


def fetch_blocks(near_refs, h_ref, sem_ref):
    own = lax.axis_index("chan") * 2 + lax.axis_index("groups")
    copies = [
        pltpu.make_async_copy(near_ref, h_ref.at[own ^ code], sem_ref.at[code])
        for code, near_ref in enumerate(near_refs)
    ]
    for copy in copies:
        copy.start()
    return copies


def first_begin(slots, extents_ref, gain_ref, far_gain_ref, *refs):
    used = 4 + len(slots)
    win_refs, weight_refs = refs[:4], refs[4:used]
    h_ref, source_ref, acc_ref, patch_ref, wide_ref, held_ref, sem_ref = refs[used:]
    copies = weight_copies(slots, weight_refs, held_ref, sem_ref)
    start_weights(copies)
    limit = window_limit(extents_ref, h_ref.shape[2])
    prepare(limit, (gain_ref, far_gain_ref), win_refs, h_ref, source_ref)
    acc_ref[...] = jnp.zeros_like(acc_ref)
    add_blocks(copies, h_ref, held_ref, patch_ref, wide_ref, acc_ref)


def first_end(slots, extents_ref, gain_ref, h_ref, begun_ref, *refs):
    weight_refs = refs[: len(slots)]
    out_ref, acc_ref, patch_ref, wide_ref, held_ref, sem_ref = refs[len(slots) :]
    copies = weight_copies(slots, weight_refs, held_ref, sem_ref)
    start_weights(copies)
    acc_ref[...] = begun_ref[...]
    add_blocks(copies, h_ref, held_ref, patch_ref, wide_ref, acc_ref)
    frames, cols, rows = h_ref.shape[1:4]
    limit = window_limit(extents_ref, cols)
    mask = column_mask(cols, limit)
    count = limit.astype(jnp.float32) * (frames * rows)
    first = (result_of(acc_ref, frames, cols, rows) * mask).astype(jnp.bfloat16)
    share = pl.multiple_of(lax.axis_index("groups") * LANES, LANES)
    gain = gain_ref[:, pl.ds(share, LANES)]
    done = normalized(first.astype(jnp.float32), gain, count, mask)
    out_ref[...] = done.astype(jnp.bfloat16)


def second_kernel(slots, extents_ref, source_hbm_ref, *refs):
    used = 4 + len(slots)
    near_refs, weight_refs, out_refs = refs[:4], refs[4:used], refs[used : used + 3]
    source_ref, source_sem, h_ref, h_sem_ref, acc_ref, spare_ref = refs[used + 3 : used + 9]
    patch_ref, wide_ref, held_ref, sem_ref = refs[used + 9 :]
    fetched = fetch_blocks(near_refs, h_ref, h_sem_ref)
    for slot, weight_ref in zip(slots, weight_refs):
        owner = owner_of(slot)

        @pl.when((owner >= 0) & (owner < lax.axis_size("tile")))
        def _(owner=owner, weight_ref=weight_ref):
            pltpu.make_async_copy(weight_ref, held_ref.at[owner], sem_ref.at[owner]).start()

    source_copy = pltpu.make_async_copy(source_hbm_ref, source_ref, source_sem)
    source_copy.start()
    acc_ref[...] = jnp.zeros_like(acc_ref)
    wide_ref[...] = jnp.zeros_like(wide_ref)
    for copy in fetched:
        copy.wait()
    for block in range(h_ref.shape[0]):
        pltpu.make_async_copy(weight_refs[0], held_ref.at[block], sem_ref.at[block]).wait()
        buffer_ref = (patch_ref, spare_ref)[block % 2]
        add_block(h_ref, block, held_ref.at[block], buffer_ref, wide_ref, acc_ref)
    join_wide(patch_ref, wide_ref, acc_ref)
    frames, cols, rows = h_ref.shape[1:4]
    mask = column_mask(cols, window_limit(extents_ref, cols))
    source_copy.wait()
    source = source_ref[...].astype(jnp.float32)
    done = (source + result_of(acc_ref, frames, cols, rows)) * mask
    done = done.astype(jnp.bfloat16)
    out_refs[0][...] = done[:, : cols - INTERSECTION]
    out_refs[1][...] = done[:, cols - INTERSECTION :]
    out_refs[2][...] = blend_ramp(extents_ref, out_refs[2].shape)


def relayed(weight):
    tiles, subs = lax.axis_size("tile"), lax.axis_size("sub")
    out_share = weight.shape[4] // lax.axis_size("groups")
    own = lax.dynamic_slice_in_dim(weight, lax.axis_index("groups") * out_share, out_share, 4)
    own = own.reshape(3, -1, out_share)
    held, pieces = own, [own]
    for step in range(1, tiles):
        pairs = [(z * subs, (z + 1) * subs + 1) for z in range(step - 1, tiles - 1)]
        pairs += [(z * subs + 1, (z - 1) * subs) for z in range(1, tiles - step + 1)]
        arrived = lax.ppermute(held, ("tile", "sub"), pairs)
        held = lax.ppermute(arrived, "sub", [(0, 1), (1, 0)])
        pieces += [arrived, held]
    return pieces


def by_distance(array):
    got = [array]
    for code in range(1, 4):
        pairs = [(i, i ^ code) for i in range(4)]
        got.append(lax.ppermute(array, ("groups", "chan"), pairs))
    return got


def share_plan(latent, extents, gain_one, weight_one, gain_two, weight_two):
    frame_count, row_count, col_count, chan_count = latent.shape
    tiles, clips = lax.axis_size("tile"), lax.axis_size("groups")
    sub = lax.axis_index("sub")
    span = col_count + INTERSECTION
    share = chan_count // clips
    frames = clips * frame_count
    pitch = (span + 1) * row_count
    taps = weight_one.shape[1] * weight_one.shape[2]
    vmem, smem = pl.BlockSpec(memory_space=pltpu.VMEM), pl.BlockSpec(memory_space=pltpu.SMEM)
    anywhere = pl.BlockSpec(memory_space=pl.ANY)
    final = jax.ShapeDtypeStruct((frames, span, row_count, share), jnp.bfloat16)
    blocks = jax.ShapeDtypeStruct((tiles,) + final.shape, jnp.bfloat16)
    total = jax.ShapeDtypeStruct((frames * pitch, share), jnp.float32)

    def scratch(slots):
        return [
            pltpu.VMEM((frames + 2, pitch, taps * LANES), jnp.bfloat16),
            pltpu.VMEM(((frames + 1) * pitch, 2 * share), jnp.float32),
            pltpu.VMEM((len(slots), 3, taps * LANES, share), jnp.bfloat16),
            pltpu.SemaphoreType.DMA((len(slots),)),
        ]

    def chosen(weights, slots):
        return [weights[slot] for slot in slots]

    acc_scratch = [pltpu.VMEM(total.shape, jnp.float32)]

    by_col = jnp.transpose(latent, (0, 2, 1, 3))
    incoming = shifted(by_col[:, :INTERSECTION], "tile", -1)
    window = jnp.concatenate([by_col, incoming], axis=1)
    windows = []
    for turn in range(2):
        for away in range(2):
            pairs = [
                ((c * 2 + (x ^ away)) * 2 + (g ^ turn), (g * 2 + x) * 2 + c)
                for g in range(2)
                for x in range(2)
                for c in range(2)
            ]
            windows.append(lax.ppermute(window, ("groups", "chan", "sub"), pairs))
    first_weights = relayed(weight_one)
    second_weights = relayed(weight_two)
    own_gain = gain_one.reshape(1, -1)
    other_gain = lax.ppermute(own_gain, "chan", [(0, 1), (1, 0)])
    slots = tuple(range(2 * tiles - 1))
    early, late = slots[:-2], slots[-2:]
    hidden, source, begun = pl.pallas_call(
        functools.partial(first_begin, early),
        out_shape=(blocks, final, total),
        in_specs=[smem] + [vmem] * 6 + [anywhere] * len(early),
        out_specs=(vmem,) * 3,
        scratch_shapes=scratch(early),
        compiler_params=pltpu.CompilerParams(vmem_limit_bytes=GRANT),
    )(extents, own_gain, other_gain, *windows, *chosen(first_weights, early))
    hidden_two = pl.pallas_call(
        functools.partial(first_end, late),
        out_shape=final,
        in_specs=[smem] + [vmem] * 3 + [anywhere] * len(late),
        out_specs=vmem,
        scratch_shapes=acc_scratch + scratch(late),
        compiler_params=pltpu.CompilerParams(vmem_limit_bytes=GRANT),
    )(extents, gain_two.reshape(1, -1), hidden, begun, *chosen(first_weights, late))
    near = by_distance(hidden_two)
    near = [near[0], near[2], near[1], near[3]]
    kept = jax.ShapeDtypeStruct((frames, col_count, row_count, share), jnp.bfloat16)
    ramps = jax.ShapeDtypeStruct((2 * INTERSECTION, row_count, chan_count), jnp.float32)
    passed = jax.ShapeDtypeStruct((frames, INTERSECTION, row_count, share), jnp.bfloat16)
    own, tail, ramp = pl.pallas_call(
        functools.partial(second_kernel, slots),
        out_shape=(kept, passed, ramps),
        in_specs=[smem] + [anywhere] * (1 + tiles + len(slots)),
        out_specs=(vmem,) * 3,
        scratch_shapes=[
            pltpu.VMEM(final.shape, jnp.bfloat16),
            pltpu.SemaphoreType.DMA,
            pltpu.VMEM(blocks.shape, jnp.bfloat16),
            pltpu.SemaphoreType.DMA((tiles,)),
        ]
        + acc_scratch
        + scratch(slots[:tiles])[:1]
        + scratch(slots[:tiles]),
        compiler_params=pltpu.CompilerParams(vmem_limit_bytes=LAST_GRANT),
    )(extents, source, *near, *chosen(second_weights, slots))

    onward = [
        ((g * tiles + z) * 2 + c, (c * tiles + z + 1) * 2 + g)
        for g in range(2)
        for z in range(tiles - 1)
        for c in range(2)
    ]
    tail = lax.ppermute(tail, ("groups", "tile", "sub"), onward)
    own = lax.ppermute(own, ("groups", "sub"), [(0, 0), (1, 2), (2, 1), (3, 3)])

    def frames_here(array):
        halves = array.reshape((2, frame_count) + array.shape[1:])
        mine = lax.dynamic_index_in_dim(halves, sub, 0, keepdims=False)
        other = lax.dynamic_index_in_dim(halves, 1 - sub, 0, keepdims=False)
        other = lax.ppermute(other, "sub", [(0, 1), (1, 0)])
        straight = jnp.concatenate([mine, other], axis=3)
        crossed = jnp.concatenate([other, mine], axis=3)
        return jnp.where(sub == 0, straight, crossed)

    own, tail = frames_here(own), frames_here(tail)
    ramp = ramp[None]
    head = jnp.repeat(own[:, :INTERSECTION].astype(jnp.float32), 2, axis=1) * ramp + jnp.repeat(
        tail.astype(jnp.float32), 2, axis=1
    ) * (1.0 - ramp)
    rest = jnp.repeat(own[:, INTERSECTION:], 2, axis=1)
    decoded = jnp.concatenate([head.astype(jnp.bfloat16), rest], axis=1)
    decoded = jnp.repeat(decoded, 2, axis=2)
    return jnp.transpose(decoded, (0, 2, 1, 3))


def solution(mesh):
    placed = (
        P(("groups", "sub"), None, "tile", "chan"),
        P(),
        P("chan"),
        P(None, None, None, "tile", "chan"),
        P("chan"),
        P(None, None, None, "tile", "chan"),
    )
    sizes = mesh.shape
    pairs_up = sizes["groups"] == 2 and sizes["sub"] == 2 and sizes["chan"] == 2
    few = pairs_up and CH // sizes["tile"] == LANES

    def body(*arrays):
        return (share_plan if few else gather_plan)(*arrays)

    return jax.shard_map(
        body,
        mesh=mesh,
        in_specs=placed,
        out_specs=P(("groups", "sub"), None, "tile", "chan"),
        check_vma=False,
    )
```

```python
import functools

import jax
import jax.numpy as jnp
from jax import lax
from jax.experimental import pallas as pl
from jax.experimental.pallas import tpu as pltpu
from jax.sharding import PartitionSpec as P


CH = 512
GROUPS = 32
INTERSECTION = 4
LANES = 128
GRANT = 12 * 2**20
LAST_GRANT = 44 * 2**20


eps = 1e-06


def shifted(array, axis, by):
    peers = lax.axis_size(axis)
    pairs = [(i, i + by) for i in range(peers) if 0 <= i + by < peers]
    return lax.ppermute(array, axis, pairs)


def ramp_after(prior):
    positions = jnp.arange(2 * INTERSECTION).astype(jnp.float32) + 0.5
    limit = (2 * prior).astype(jnp.float32)[..., None]
    denom = (2 * jnp.maximum(prior, 1)).astype(jnp.float32)[..., None]
    return jnp.where(positions < limit, positions / denom, 1.0)


def convolve(inputs, kernel):
    result = lax.conv_general_dilated(
        inputs[None],
        kernel,
        (1, 1, 1),
        [(0, 0), (1, 1), (1, 1)],
        dimension_numbers=("NDHWC", "DHWIO", "NDHWC"),
        preferred_element_type=jnp.float32,
    )
    return result[0]


def group_norm(values, gain, count):
    group_size = CH // GROUPS
    grouped = values.reshape(values.shape[:-1] + (values.shape[-1] // group_size, group_size))
    totals, squares = lax.psum(
        (jnp.sum(grouped, axis=(0, 1, 2, 4)), jnp.sum(grouped * grouped, axis=(0, 1, 2, 4))), "sub"
    )
    size = count * group_size
    mean_val = totals / size
    variance = squares / size - mean_val * mean_val
    scaled = (grouped - mean_val[:, None]) * lax.rsqrt(variance + eps)[:, None]
    return scaled.reshape(values.shape) * gain


def causal_pad(values):
    earlier = shifted(values[-2:], "sub", 1)
    repeated = jnp.concatenate([values[:1], values[:1]], axis=0)
    leading = jnp.where(lax.axis_index("sub") == 0, repeated, earlier)
    return jnp.concatenate([leading, values], axis=0)


def channel_conv(padded_in, weight):
    full_in = lax.all_gather(padded_in, "chan", axis=3, tiled=True)
    out_count = weight.shape[4]
    share = weight.shape[3] // lax.axis_size("sub")
    portion = lax.dynamic_slice_in_dim(weight, lax.axis_index("sub") * share, share, 3)
    fetched = lax.all_gather(portion, "tile", axis=3, tiled=True)
    sectioned = fetched.reshape(3, 3, 3, lax.axis_size("tile"), 1, share, out_count)
    whole = lax.all_gather(sectioned, "sub", axis=4, tiled=True).reshape(3, 3, 3, -1, out_count)
    return convolve(full_in, whole)


def upscale(values):
    return jnp.repeat(jnp.repeat(values, 2, axis=1), 2, axis=2)


def reach_and_prior(extents):
    tile_count = lax.axis_size("tile")
    place = lax.axis_index("tile")
    tile_ids = jnp.arange(tile_count, dtype=jnp.int32)
    reaches = jnp.where(tile_ids == tile_count - 1, 0, extents)
    reach = jnp.sum(jnp.where(tile_ids == place, reaches, 0))
    prior = jnp.sum(jnp.where(tile_ids == place - 1, reaches, 0))
    return reach, prior


def gather_plan(latent, extents, gain_one, weight_one, gain_two, weight_two):
    frame_count, row_count, col_count, _ = latent.shape
    reach, prior = reach_and_prior(extents)
    incoming = shifted(latent[:, :, :INTERSECTION, :], "tile", -1)
    window = jnp.concatenate([latent, incoming], axis=2)
    valid = (jnp.arange(col_count + INTERSECTION, dtype=jnp.int32) < col_count + reach).astype(
        jnp.float32
    )
    mask = valid[None, None, :, None]
    window = jnp.where(mask > 0, window, jnp.zeros_like(window))
    count = (col_count + reach).astype(jnp.float32) * (
        frame_count * lax.axis_size("sub") * row_count
    )
    source = window.astype(jnp.float32)
    hidden = (jax.nn.silu(group_norm(source, gain_one, count)) * mask).astype(jnp.bfloat16)
    first = (channel_conv(causal_pad(hidden), weight_one) * mask).astype(jnp.bfloat16)
    first = lax.optimization_barrier(first)
    hidden_two = (
        jax.nn.silu(group_norm(first.astype(jnp.float32), gain_two, count)) * mask
    ).astype(jnp.bfloat16)
    second = channel_conv(causal_pad(hidden_two), weight_two)
    result = ((source + second) * mask).astype(jnp.bfloat16)
    larger = upscale(result)
    own = larger[:, :, : 2 * col_count]
    arrived = shifted(larger[:, :, 2 * col_count :], "tile", 1)
    ramp = ramp_after(prior)[None, None, :, None]
    head = own[:, :, : 2 * INTERSECTION].astype(jnp.float32) * ramp + arrived.astype(
        jnp.float32
    ) * (1.0 - ramp)
    return jnp.concatenate([head.astype(jnp.bfloat16), own[:, :, 2 * INTERSECTION :]], axis=2)


def normalized(values, gain, count, mask):
    chans = values.shape[-1]
    group_size = CH // GROUPS
    rows = lax.broadcasted_iota(jnp.int32, (chans, chans), 0) // group_size
    cols = lax.broadcasted_iota(jnp.int32, (chans, chans), 1) // group_size
    same = (rows == cols).astype(jnp.float32)
    total = jnp.sum(values, axis=(0, 1, 2)).reshape(1, chans)
    square = jnp.sum(values * values, axis=(0, 1, 2)).reshape(1, chans)
    both = jnp.concatenate([jnp.broadcast_to(total, (8, chans)), jnp.broadcast_to(square, (8, chans))], 0)
    sums = jnp.dot(both, same, precision=lax.Precision.HIGHEST, preferred_element_type=jnp.float32)
    size = count * group_size
    mean = sums[0:1] / size
    variance = sums[8:9] / size - mean * mean
    rate = lax.rsqrt(variance + eps)
    shape = (1, 1, 1, chans)
    scaled = (values - mean.reshape(shape)) * rate.reshape(shape) * gain.reshape(shape)
    return (scaled / (1.0 + jnp.exp(-scaled))) * mask


def column_mask(cols, limit):
    ids = lax.broadcasted_iota(jnp.int32, (1, cols, 8, LANES), 1)
    return (ids < limit).astype(jnp.float32)


def window_limit(extents_ref, cols):
    place = lax.axis_index("tile")
    reach = jnp.where(place == lax.axis_size("tile") - 1, 0, extents_ref[place])
    return cols - INTERSECTION + reach


def blend_ramp(extents_ref, shape):
    place = lax.axis_index("tile")
    prior = jnp.where(place == 0, 0, extents_ref[jnp.maximum(place - 1, 0)])
    positions = lax.broadcasted_iota(jnp.int32, shape, 0).astype(jnp.float32) + 0.5
    limit = jnp.broadcast_to((2 * prior).astype(jnp.float32), shape)
    denom = jnp.broadcast_to((2 * jnp.maximum(prior, 1)).astype(jnp.float32), shape)
    return jnp.where(positions < limit, positions / denom, 1.0)


def owner_of(slot):
    step = (slot + 1) // 2
    ahead = (lax.axis_index("sub") == 0) == (slot % 2 == 1)
    return lax.axis_index("tile") + jnp.where(ahead, step, -step)


def prepare(limit, gain_refs, win_refs, h_ref, source_ref):
    clip, chan = lax.axis_index("groups"), lax.axis_index("chan")
    frames, cols, rows, width = win_refs[0].shape
    count = limit.astype(jnp.float32) * (2 * frames * rows)
    mask = column_mask(cols, limit)
    for away, gain_ref in enumerate(gain_refs):
        for piece in range(width // LANES):
            lanes = slice(piece * LANES, (piece + 1) * LANES)
            both = [win_refs[2 * turn + away][:, :, :, lanes] for turn in range(2)]
            values = jnp.concatenate(both, 0).astype(jnp.float32)
            values = jnp.where(mask > 0, values, 0.0)
            done = normalized(values, gain_ref[:, lanes], count, mask).astype(jnp.bfloat16)
            block = (chan ^ away) * (width // LANES) + piece
            for turn in range(2):
                rows_at = pl.ds((clip ^ turn) * frames, frames)
                h_ref[block, rows_at] = done[turn * frames : (turn + 1) * frames]
                if away == 0:

                    @pl.when(clip == piece)
                    def _(rows_at=rows_at, turn=turn, both=both):
                        source_ref[rows_at] = both[turn]


def fill_patches(h_ref, block, patch_ref):
    frames, cols, rows, width = h_ref.shape[1:]
    ids = lax.broadcasted_iota(jnp.int32, (cols, rows, width), 1)
    empty = jnp.zeros((rows, width), jnp.float32)
    blank = jnp.zeros((2 * rows, width), jnp.bfloat16)
    for t in range(frames):
        here = h_ref[block, t].astype(jnp.float32)
        for b in range(3):
            if b == 1:
                moved = here
            else:
                moved = pltpu.roll(here, 1 if b == 0 else rows - 1, 1)
                moved = jnp.where(ids == (0 if b == 0 else rows - 1), 0.0, moved)
            flat = moved.reshape(cols * rows, width)
            for d in range(3):
                if d == 0:
                    piece = jnp.concatenate([empty, flat], 0).astype(jnp.bfloat16)
                    onward = jnp.concatenate([piece[2 * rows :], blank], 0)
                elif d == 1:
                    piece = jnp.concatenate([flat, empty], 0).astype(jnp.bfloat16)
                else:
                    piece = onward
                lane = (b * 3 + d) * width
                patch_ref[t + 2, :, lane : lane + width] = piece
                if t == 0:
                    patch_ref[0, :, lane : lane + width] = piece
                    patch_ref[1, :, lane : lane + width] = piece


def add_block(h_ref, block, weight_ref, patch_ref, wide_ref, acc_ref):
    fill_patches(h_ref, block, patch_ref)
    frames = h_ref.shape[1]
    pitch, depth = patch_ref.shape[1:]
    left = patch_ref[: frames + 1].reshape((frames + 1) * pitch, depth)
    wide_ref[...] += jnp.dot(
        left, weight_ref[:, : 2 * LANES], preferred_element_type=jnp.float32
    )
    left = patch_ref[2:].reshape(frames * pitch, depth)
    acc_ref[...] += jnp.dot(
        left, weight_ref[:, 2 * LANES :], preferred_element_type=jnp.float32
    )


def block_copies(weight_ref, held_ref, sem_ref, i):
    return [
        pltpu.make_async_copy(
            weight_ref.at[a], held_ref.at[i, :, a * LANES : (a + 1) * LANES], sem_ref.at[i, a]
        )
        for a in range(3)
    ]


def weight_copies(slots, weight_refs, held_ref, sem_ref):
    copies = []
    for i, (slot, weight_ref) in enumerate(zip(slots, weight_refs)):
        owner = owner_of(slot)
        there = (owner >= 0) & (owner < lax.axis_size("tile"))
        copies.append((owner, there, block_copies(weight_ref, held_ref, sem_ref, i)))
    return copies


def start_weights(copies):
    for _, there, parts in copies:

        @pl.when(there)
        def _(parts=parts):
            for copy in parts:
                copy.start()


def add_blocks(copies, h_ref, held_ref, patch_ref, wide_ref, acc_ref):
    wide_ref[...] = jnp.zeros_like(wide_ref)
    for i, (owner, there, parts) in enumerate(copies):

        @pl.when(there)
        def _(i=i, owner=owner, parts=parts):
            for copy in parts:
                copy.wait()
            add_block(h_ref, owner, held_ref.at[i], patch_ref, wide_ref, acc_ref)

    join_wide(patch_ref, wide_ref, acc_ref)


def join_wide(patch_ref, wide_ref, acc_ref):
    shift = patch_ref.shape[1]
    count = acc_ref.shape[0]
    acc_ref[...] += wide_ref[:count, :LANES] + wide_ref[shift : shift + count, LANES:]


def result_of(acc_ref, frames, cols, rows):
    pitch = acc_ref.shape[0] // frames
    whole = acc_ref[...].reshape(frames, pitch, LANES)
    return whole[:, : cols * rows].reshape(frames, cols, rows, LANES)


def fetch_blocks(near_refs, h_ref, sem_ref):
    own = lax.axis_index("chan") * 2 + lax.axis_index("groups")
    copies = [
        pltpu.make_async_copy(near_ref, h_ref.at[own ^ code], sem_ref.at[code])
        for code, near_ref in enumerate(near_refs)
    ]
    for copy in copies:
        copy.start()
    return copies


def first_begin(slots, extents_ref, gain_ref, far_gain_ref, *refs):
    used = 4 + len(slots)
    win_refs, weight_refs = refs[:4], refs[4:used]
    h_ref, source_ref, acc_ref, patch_ref, wide_ref, held_ref, sem_ref = refs[used:]
    copies = weight_copies(slots, weight_refs, held_ref, sem_ref)
    start_weights(copies)
    limit = window_limit(extents_ref, h_ref.shape[2])
    prepare(limit, (gain_ref, far_gain_ref), win_refs, h_ref, source_ref)
    acc_ref[...] = jnp.zeros_like(acc_ref)
    add_blocks(copies, h_ref, held_ref, patch_ref, wide_ref, acc_ref)


def first_end(slots, extents_ref, gain_ref, h_ref, begun_ref, *refs):
    weight_refs = refs[: len(slots)]
    out_ref, acc_ref, patch_ref, wide_ref, held_ref, sem_ref = refs[len(slots) :]
    copies = weight_copies(slots, weight_refs, held_ref, sem_ref)
    start_weights(copies)
    acc_ref[...] = begun_ref[...]
    add_blocks(copies, h_ref, held_ref, patch_ref, wide_ref, acc_ref)
    frames, cols, rows = h_ref.shape[1:4]
    limit = window_limit(extents_ref, cols)
    mask = column_mask(cols, limit)
    count = limit.astype(jnp.float32) * (frames * rows)
    first = (result_of(acc_ref, frames, cols, rows) * mask).astype(jnp.bfloat16)
    share = pl.multiple_of(lax.axis_index("groups") * LANES, LANES)
    gain = gain_ref[:, pl.ds(share, LANES)]
    done = normalized(first.astype(jnp.float32), gain, count, mask)
    out_ref[...] = done.astype(jnp.bfloat16)


def second_kernel(slots, extents_ref, source_hbm_ref, *refs):
    used = 4 + len(slots)
    near_refs, weight_refs, out_refs = refs[:4], refs[4:used], refs[used : used + 3]
    source_ref, source_sem, h_ref, h_sem_ref, acc_ref, spare_ref = refs[used + 3 : used + 9]
    patch_ref, wide_ref, held_ref, sem_ref = refs[used + 9 :]
    fetched = fetch_blocks(near_refs, h_ref, h_sem_ref)
    for slot, weight_ref in zip(slots, weight_refs):
        owner = owner_of(slot)

        @pl.when((owner >= 0) & (owner < lax.axis_size("tile")))
        def _(owner=owner, weight_ref=weight_ref):
            for copy in block_copies(weight_ref, held_ref, sem_ref, owner):
                copy.start()

    source_copy = pltpu.make_async_copy(source_hbm_ref, source_ref, source_sem)
    source_copy.start()
    acc_ref[...] = jnp.zeros_like(acc_ref)
    wide_ref[...] = jnp.zeros_like(wide_ref)
    for copy in fetched:
        copy.wait()
    for block in range(h_ref.shape[0]):
        for copy in block_copies(weight_refs[0], held_ref, sem_ref, block):
            copy.wait()
        buffer_ref = (patch_ref, spare_ref)[block % 2]
        add_block(h_ref, block, held_ref.at[block], buffer_ref, wide_ref, acc_ref)
    join_wide(patch_ref, wide_ref, acc_ref)
    frames, cols, rows = h_ref.shape[1:4]
    mask = column_mask(cols, window_limit(extents_ref, cols))
    source_copy.wait()
    source = source_ref[...].astype(jnp.float32)
    done = (source + result_of(acc_ref, frames, cols, rows)) * mask
    done = done.astype(jnp.bfloat16)
    out_refs[0][...] = done[:, : cols - INTERSECTION]
    out_refs[1][...] = done[:, cols - INTERSECTION :]
    out_refs[2][...] = blend_ramp(extents_ref, out_refs[2].shape)


def relayed(weight):
    tiles, subs = lax.axis_size("tile"), lax.axis_size("sub")
    out_share = weight.shape[4] // lax.axis_size("groups")
    own = lax.dynamic_slice_in_dim(weight, lax.axis_index("groups") * out_share, out_share, 4)
    own = own.reshape(3, -1, out_share)
    held, pieces = own, [own]
    for step in range(1, tiles):
        pairs = [(z * subs, (z + 1) * subs + 1) for z in range(step - 1, tiles - 1)]
        pairs += [(z * subs + 1, (z - 1) * subs) for z in range(1, tiles - step + 1)]
        arrived = lax.ppermute(held, ("tile", "sub"), pairs)
        held = lax.ppermute(arrived, "sub", [(0, 1), (1, 0)])
        pieces += [arrived, held]
    return pieces


def by_distance(array):
    got = [array]
    for code in range(1, 4):
        pairs = [(i, i ^ code) for i in range(4)]
        got.append(lax.ppermute(array, ("groups", "chan"), pairs))
    return got


def share_plan(latent, extents, gain_one, weight_one, gain_two, weight_two):
    frame_count, row_count, col_count, chan_count = latent.shape
    tiles, clips = lax.axis_size("tile"), lax.axis_size("groups")
    sub = lax.axis_index("sub")
    span = col_count + INTERSECTION
    share = chan_count // clips
    frames = clips * frame_count
    pitch = (span + 1) * row_count
    taps = weight_one.shape[1] * weight_one.shape[2]
    vmem, smem = pl.BlockSpec(memory_space=pltpu.VMEM), pl.BlockSpec(memory_space=pltpu.SMEM)
    anywhere = pl.BlockSpec(memory_space=pl.ANY)
    final = jax.ShapeDtypeStruct((frames, span, row_count, share), jnp.bfloat16)
    blocks = jax.ShapeDtypeStruct((tiles,) + final.shape, jnp.bfloat16)
    total = jax.ShapeDtypeStruct((frames * pitch, share), jnp.float32)

    def scratch(slots):
        return [
            pltpu.VMEM((frames + 2, pitch, taps * LANES), jnp.bfloat16),
            pltpu.VMEM(((frames + 1) * pitch, 2 * share), jnp.float32),
            pltpu.VMEM((len(slots), taps * LANES, 3 * share), jnp.bfloat16),
            pltpu.SemaphoreType.DMA((len(slots), 3)),
        ]

    def chosen(weights, slots):
        return [weights[slot] for slot in slots]

    acc_scratch = [pltpu.VMEM(total.shape, jnp.float32)]

    by_col = jnp.transpose(latent, (0, 2, 1, 3))
    incoming = shifted(by_col[:, :INTERSECTION], "tile", -1)
    window = jnp.concatenate([by_col, incoming], axis=1)
    windows = []
    for turn in range(2):
        for away in range(2):
            pairs = [
                ((c * 2 + (x ^ away)) * 2 + (g ^ turn), (g * 2 + x) * 2 + c)
                for g in range(2)
                for x in range(2)
                for c in range(2)
            ]
            windows.append(lax.ppermute(window, ("groups", "chan", "sub"), pairs))
    first_weights = relayed(weight_one)
    second_weights = relayed(weight_two)
    own_gain = gain_one.reshape(1, -1)
    other_gain = lax.ppermute(own_gain, "chan", [(0, 1), (1, 0)])
    slots = tuple(range(2 * tiles - 1))
    early, late = slots[:-2], slots[-2:]
    hidden, source, begun = pl.pallas_call(
        functools.partial(first_begin, early),
        out_shape=(blocks, final, total),
        in_specs=[smem] + [vmem] * 6 + [anywhere] * len(early),
        out_specs=(vmem,) * 3,
        scratch_shapes=scratch(early),
        compiler_params=pltpu.CompilerParams(vmem_limit_bytes=GRANT),
    )(extents, own_gain, other_gain, *windows, *chosen(first_weights, early))
    hidden_two = pl.pallas_call(
        functools.partial(first_end, late),
        out_shape=final,
        in_specs=[smem] + [vmem] * 3 + [anywhere] * len(late),
        out_specs=vmem,
        scratch_shapes=acc_scratch + scratch(late),
        compiler_params=pltpu.CompilerParams(vmem_limit_bytes=GRANT),
    )(extents, gain_two.reshape(1, -1), hidden, begun, *chosen(first_weights, late))
    near = by_distance(hidden_two)
    near = [near[0], near[2], near[1], near[3]]
    kept = jax.ShapeDtypeStruct((frames, col_count, row_count, share), jnp.bfloat16)
    ramps = jax.ShapeDtypeStruct((2 * INTERSECTION, row_count, chan_count), jnp.float32)
    passed = jax.ShapeDtypeStruct((frames, INTERSECTION, row_count, share), jnp.bfloat16)
    own, tail, ramp = pl.pallas_call(
        functools.partial(second_kernel, slots),
        out_shape=(kept, passed, ramps),
        in_specs=[smem] + [anywhere] * (1 + tiles + len(slots)),
        out_specs=(vmem,) * 3,
        scratch_shapes=[
            pltpu.VMEM(final.shape, jnp.bfloat16),
            pltpu.SemaphoreType.DMA,
            pltpu.VMEM(blocks.shape, jnp.bfloat16),
            pltpu.SemaphoreType.DMA((tiles,)),
        ]
        + acc_scratch
        + scratch(slots[:tiles])[:1]
        + scratch(slots[:tiles]),
        compiler_params=pltpu.CompilerParams(vmem_limit_bytes=LAST_GRANT),
    )(extents, source, *near, *chosen(second_weights, slots))

    onward = [
        ((g * tiles + z) * 2 + c, (c * tiles + z + 1) * 2 + g)
        for g in range(2)
        for z in range(tiles - 1)
        for c in range(2)
    ]
    tail = lax.ppermute(tail, ("groups", "tile", "sub"), onward)
    own = lax.ppermute(own, ("groups", "sub"), [(0, 0), (1, 2), (2, 1), (3, 3)])

    def frames_here(array):
        halves = array.reshape((2, frame_count) + array.shape[1:])
        mine = lax.dynamic_index_in_dim(halves, sub, 0, keepdims=False)
        other = lax.dynamic_index_in_dim(halves, 1 - sub, 0, keepdims=False)
        other = lax.ppermute(other, "sub", [(0, 1), (1, 0)])
        straight = jnp.concatenate([mine, other], axis=3)
        crossed = jnp.concatenate([other, mine], axis=3)
        return jnp.where(sub == 0, straight, crossed)

    own, tail = frames_here(own), frames_here(tail)
    ramp = ramp[None]
    head = jnp.repeat(own[:, :INTERSECTION].astype(jnp.float32), 2, axis=1) * ramp + jnp.repeat(
        tail.astype(jnp.float32), 2, axis=1
    ) * (1.0 - ramp)
    rest = jnp.repeat(own[:, INTERSECTION:], 2, axis=1)
    decoded = jnp.concatenate([head.astype(jnp.bfloat16), rest], axis=1)
    decoded = jnp.repeat(decoded, 2, axis=2)
    return jnp.transpose(decoded, (0, 2, 1, 3))


def solution(mesh):
    placed = (
        P(("groups", "sub"), None, "tile", "chan"),
        P(),
        P("chan"),
        P(None, None, None, "tile", "chan"),
        P("chan"),
        P(None, None, None, "tile", "chan"),
    )
    sizes = mesh.shape
    pairs_up = sizes["groups"] == 2 and sizes["sub"] == 2 and sizes["chan"] == 2
    few = pairs_up and CH // sizes["tile"] == LANES

    def body(*arrays):
        return (share_plan if few else gather_plan)(*arrays)

    return jax.shard_map(
        body,
        mesh=mesh,
        in_specs=placed,
        out_specs=P(("groups", "sub"), None, "tile", "chan"),
        check_vma=False,
    )
```

```python
import functools

import jax
import jax.numpy as jnp
from jax import lax
from jax.experimental import pallas as pl
from jax.experimental.pallas import tpu as pltpu
from jax.sharding import PartitionSpec as P


CH = 512
GROUPS = 32
INTERSECTION = 4
LANES = 128
GRANT = 12 * 2**20
LAST_GRANT = 44 * 2**20


eps = 1e-06


def shifted(array, axis, by):
    peers = lax.axis_size(axis)
    pairs = [(i, i + by) for i in range(peers) if 0 <= i + by < peers]
    return lax.ppermute(array, axis, pairs)


def ramp_after(prior):
    positions = jnp.arange(2 * INTERSECTION).astype(jnp.float32) + 0.5
    limit = (2 * prior).astype(jnp.float32)[..., None]
    denom = (2 * jnp.maximum(prior, 1)).astype(jnp.float32)[..., None]
    return jnp.where(positions < limit, positions / denom, 1.0)


def convolve(inputs, kernel):
    result = lax.conv_general_dilated(
        inputs[None],
        kernel,
        (1, 1, 1),
        [(0, 0), (1, 1), (1, 1)],
        dimension_numbers=("NDHWC", "DHWIO", "NDHWC"),
        preferred_element_type=jnp.float32,
    )
    return result[0]


def group_norm(values, gain, count):
    group_size = CH // GROUPS
    grouped = values.reshape(values.shape[:-1] + (values.shape[-1] // group_size, group_size))
    totals, squares = lax.psum(
        (jnp.sum(grouped, axis=(0, 1, 2, 4)), jnp.sum(grouped * grouped, axis=(0, 1, 2, 4))), "sub"
    )
    size = count * group_size
    mean_val = totals / size
    variance = squares / size - mean_val * mean_val
    scaled = (grouped - mean_val[:, None]) * lax.rsqrt(variance + eps)[:, None]
    return scaled.reshape(values.shape) * gain


def causal_pad(values):
    earlier = shifted(values[-2:], "sub", 1)
    repeated = jnp.concatenate([values[:1], values[:1]], axis=0)
    leading = jnp.where(lax.axis_index("sub") == 0, repeated, earlier)
    return jnp.concatenate([leading, values], axis=0)


def channel_conv(padded_in, weight):
    full_in = lax.all_gather(padded_in, "chan", axis=3, tiled=True)
    out_count = weight.shape[4]
    share = weight.shape[3] // lax.axis_size("sub")
    portion = lax.dynamic_slice_in_dim(weight, lax.axis_index("sub") * share, share, 3)
    fetched = lax.all_gather(portion, "tile", axis=3, tiled=True)
    sectioned = fetched.reshape(3, 3, 3, lax.axis_size("tile"), 1, share, out_count)
    whole = lax.all_gather(sectioned, "sub", axis=4, tiled=True).reshape(3, 3, 3, -1, out_count)
    return convolve(full_in, whole)


def upscale(values):
    return jnp.repeat(jnp.repeat(values, 2, axis=1), 2, axis=2)


def reach_and_prior(extents):
    tile_count = lax.axis_size("tile")
    place = lax.axis_index("tile")
    tile_ids = jnp.arange(tile_count, dtype=jnp.int32)
    reaches = jnp.where(tile_ids == tile_count - 1, 0, extents)
    reach = jnp.sum(jnp.where(tile_ids == place, reaches, 0))
    prior = jnp.sum(jnp.where(tile_ids == place - 1, reaches, 0))
    return reach, prior


def gather_plan(latent, extents, gain_one, weight_one, gain_two, weight_two):
    frame_count, row_count, col_count, _ = latent.shape
    reach, prior = reach_and_prior(extents)
    incoming = shifted(latent[:, :, :INTERSECTION, :], "tile", -1)
    window = jnp.concatenate([latent, incoming], axis=2)
    valid = (jnp.arange(col_count + INTERSECTION, dtype=jnp.int32) < col_count + reach).astype(
        jnp.float32
    )
    mask = valid[None, None, :, None]
    window = jnp.where(mask > 0, window, jnp.zeros_like(window))
    count = (col_count + reach).astype(jnp.float32) * (
        frame_count * lax.axis_size("sub") * row_count
    )
    source = window.astype(jnp.float32)
    hidden = (jax.nn.silu(group_norm(source, gain_one, count)) * mask).astype(jnp.bfloat16)
    first = (channel_conv(causal_pad(hidden), weight_one) * mask).astype(jnp.bfloat16)
    first = lax.optimization_barrier(first)
    hidden_two = (
        jax.nn.silu(group_norm(first.astype(jnp.float32), gain_two, count)) * mask
    ).astype(jnp.bfloat16)
    second = channel_conv(causal_pad(hidden_two), weight_two)
    result = ((source + second) * mask).astype(jnp.bfloat16)
    larger = upscale(result)
    own = larger[:, :, : 2 * col_count]
    arrived = shifted(larger[:, :, 2 * col_count :], "tile", 1)
    ramp = ramp_after(prior)[None, None, :, None]
    head = own[:, :, : 2 * INTERSECTION].astype(jnp.float32) * ramp + arrived.astype(
        jnp.float32
    ) * (1.0 - ramp)
    return jnp.concatenate([head.astype(jnp.bfloat16), own[:, :, 2 * INTERSECTION :]], axis=2)


def normalized(values, gain, count, mask):
    chans = values.shape[-1]
    group_size = CH // GROUPS
    rows = lax.broadcasted_iota(jnp.int32, (chans, chans), 0) // group_size
    cols = lax.broadcasted_iota(jnp.int32, (chans, chans), 1) // group_size
    same = (rows == cols).astype(jnp.float32)
    total = jnp.sum(values, axis=(0, 1, 2)).reshape(1, chans)
    square = jnp.sum(values * values, axis=(0, 1, 2)).reshape(1, chans)
    both = jnp.concatenate([jnp.broadcast_to(total, (8, chans)), jnp.broadcast_to(square, (8, chans))], 0)
    sums = jnp.dot(both, same, precision=lax.Precision.HIGHEST, preferred_element_type=jnp.float32)
    size = count * group_size
    mean = sums[0:1] / size
    variance = sums[8:9] / size - mean * mean
    rate = lax.rsqrt(variance + eps)
    shape = (1, 1, 1, chans)
    scaled = (values - mean.reshape(shape)) * rate.reshape(shape) * gain.reshape(shape)
    return (scaled / (1.0 + jnp.exp(-scaled))) * mask


def column_mask(cols, limit):
    ids = lax.broadcasted_iota(jnp.int32, (1, cols, 8, LANES), 1)
    return (ids < limit).astype(jnp.float32)


def window_limit(extents_ref, cols):
    place = lax.axis_index("tile")
    reach = jnp.where(place == lax.axis_size("tile") - 1, 0, extents_ref[place])
    return cols - INTERSECTION + reach


def blend_ramp(extents_ref, shape):
    place = lax.axis_index("tile")
    prior = jnp.where(place == 0, 0, extents_ref[jnp.maximum(place - 1, 0)])
    positions = lax.broadcasted_iota(jnp.int32, shape, 0).astype(jnp.float32) + 0.5
    limit = jnp.broadcast_to((2 * prior).astype(jnp.float32), shape)
    denom = jnp.broadcast_to((2 * jnp.maximum(prior, 1)).astype(jnp.float32), shape)
    return jnp.where(positions < limit, positions / denom, 1.0)


def owner_of(slot):
    step = (slot + 1) // 2
    ahead = (lax.axis_index("sub") == 0) == (slot % 2 == 1)
    return lax.axis_index("tile") + jnp.where(ahead, step, -step)


def prepare(limit, gain_refs, win_refs, h_ref, source_ref):
    clip, chan = lax.axis_index("groups"), lax.axis_index("chan")
    frames, cols, rows, width = win_refs[0].shape
    count = limit.astype(jnp.float32) * (2 * frames * rows)
    mask = column_mask(cols, limit)
    for away, gain_ref in enumerate(gain_refs):
        for piece in range(width // LANES):
            lanes = slice(piece * LANES, (piece + 1) * LANES)
            both = [win_refs[2 * turn + away][:, :, :, lanes] for turn in range(2)]
            values = jnp.concatenate(both, 0).astype(jnp.float32)
            values = jnp.where(mask > 0, values, 0.0)
            done = normalized(values, gain_ref[:, lanes], count, mask).astype(jnp.bfloat16)
            block = (chan ^ away) * (width // LANES) + piece
            for turn in range(2):
                rows_at = pl.ds((clip ^ turn) * frames, frames)
                h_ref[block, rows_at] = done[turn * frames : (turn + 1) * frames]
                if away == 0:

                    @pl.when(clip == piece)
                    def _(rows_at=rows_at, turn=turn, both=both):
                        source_ref[rows_at] = both[turn]


def fill_patches(h_ref, block, patch_ref):
    frames, cols, rows, width = h_ref.shape[1:]
    ids = lax.broadcasted_iota(jnp.int32, (cols, rows, width), 1)
    empty = jnp.zeros((rows, width), jnp.float32)
    blank = jnp.zeros((2 * rows, width), jnp.bfloat16)
    for t in range(frames):
        here = h_ref[block, t].astype(jnp.float32)
        for b in range(3):
            if b == 1:
                moved = here
            else:
                moved = pltpu.roll(here, 1 if b == 0 else rows - 1, 1)
                moved = jnp.where(ids == (0 if b == 0 else rows - 1), 0.0, moved)
            flat = moved.reshape(cols * rows, width)
            for d in range(3):
                if d == 0:
                    piece = jnp.concatenate([empty, flat], 0).astype(jnp.bfloat16)
                    onward = jnp.concatenate([piece[2 * rows :], blank], 0)
                elif d == 1:
                    piece = jnp.concatenate([flat, empty], 0).astype(jnp.bfloat16)
                else:
                    piece = onward
                lane = (b * 3 + d) * width
                patch_ref[t + 2, :, lane : lane + width] = piece
                if t == 0:
                    patch_ref[0, :, lane : lane + width] = piece
                    patch_ref[1, :, lane : lane + width] = piece


def add_block(h_ref, block, weight_ref, patch_ref, wide_ref, acc_ref):
    fill_patches(h_ref, block, patch_ref)
    frames = h_ref.shape[1]
    pitch, depth = patch_ref.shape[1:]
    both = jnp.concatenate([weight_ref[0], weight_ref[1]], axis=1)
    left = patch_ref[: frames + 1].reshape((frames + 1) * pitch, depth)
    wide_ref[...] += jnp.dot(
        left, both, preferred_element_type=jnp.float32
    )
    left = patch_ref[2:].reshape(frames * pitch, depth)
    acc_ref[...] += jnp.dot(
        left, weight_ref[2], preferred_element_type=jnp.float32
    )


def add_blocks(slots, weight_refs, h_ref, patch_ref, wide_ref, acc_ref):
    wide_ref[...] = jnp.zeros_like(wide_ref)
    for slot, weight_ref in zip(slots, weight_refs):
        owner = owner_of(slot)

        @pl.when((owner >= 0) & (owner < lax.axis_size("tile")))
        def _(owner=owner, weight_ref=weight_ref):
            add_block(h_ref, owner, weight_ref, patch_ref, wide_ref, acc_ref)

    join_wide(patch_ref, wide_ref, acc_ref)


def join_wide(patch_ref, wide_ref, acc_ref):
    shift = patch_ref.shape[1]
    count = acc_ref.shape[0]
    acc_ref[...] += wide_ref[:count, :LANES] + wide_ref[shift : shift + count, LANES:]


def result_of(acc_ref, frames, cols, rows):
    pitch = acc_ref.shape[0] // frames
    whole = acc_ref[...].reshape(frames, pitch, LANES)
    return whole[:, : cols * rows].reshape(frames, cols, rows, LANES)


def fetch_blocks(near_refs, h_ref, sem_ref):
    own = lax.axis_index("chan") * 2 + lax.axis_index("groups")
    copies = [
        pltpu.make_async_copy(near_ref, h_ref.at[own ^ code], sem_ref.at[code])
        for code, near_ref in enumerate(near_refs)
    ]
    for copy in copies:
        copy.start()
    return copies


def first_begin(slots, extents_ref, gain_ref, far_gain_ref, *refs):
    used = 4 + len(slots)
    win_refs, weight_refs = refs[:4], refs[4:used]
    h_ref, source_ref, acc_ref, patch_ref, wide_ref = refs[used:]
    limit = window_limit(extents_ref, h_ref.shape[2])
    prepare(limit, (gain_ref, far_gain_ref), win_refs, h_ref, source_ref)
    acc_ref[...] = jnp.zeros_like(acc_ref)
    add_blocks(slots, weight_refs, h_ref, patch_ref, wide_ref, acc_ref)


def first_end(slots, extents_ref, gain_ref, h_ref, begun_ref, *refs):
    weight_refs = refs[: len(slots)]
    out_ref, acc_ref, patch_ref, wide_ref = refs[len(slots) :]
    acc_ref[...] = begun_ref[...]
    add_blocks(slots, weight_refs, h_ref, patch_ref, wide_ref, acc_ref)
    frames, cols, rows = h_ref.shape[1:4]
    limit = window_limit(extents_ref, cols)
    mask = column_mask(cols, limit)
    count = limit.astype(jnp.float32) * (frames * rows)
    first = (result_of(acc_ref, frames, cols, rows) * mask).astype(jnp.bfloat16)
    share = pl.multiple_of(lax.axis_index("groups") * LANES, LANES)
    gain = gain_ref[:, pl.ds(share, LANES)]
    done = normalized(first.astype(jnp.float32), gain, count, mask)
    out_ref[...] = done.astype(jnp.bfloat16)


def second_kernel(slots, extents_ref, source_hbm_ref, *refs):
    used = 4 + len(slots)
    near_refs, weight_refs, out_refs = refs[:4], refs[4:used], refs[used : used + 3]
    source_ref, source_sem, h_ref, h_sem_ref, acc_ref = refs[used + 3 : used + 8]
    patch_ref, wide_ref = refs[used + 8 :]
    fetched = fetch_blocks(near_refs, h_ref, h_sem_ref)
    source_copy = pltpu.make_async_copy(source_hbm_ref, source_ref, source_sem)
    source_copy.start()
    acc_ref[...] = jnp.zeros_like(acc_ref)
    for copy in fetched:
        copy.wait()
    add_blocks(slots, weight_refs, h_ref, patch_ref, wide_ref, acc_ref)
    frames, cols, rows = h_ref.shape[1:4]
    mask = column_mask(cols, window_limit(extents_ref, cols))
    source_copy.wait()
    source = source_ref[...].astype(jnp.float32)
    done = (source + result_of(acc_ref, frames, cols, rows)) * mask
    done = done.astype(jnp.bfloat16)
    out_refs[0][...] = done[:, : cols - INTERSECTION]
    out_refs[1][...] = done[:, cols - INTERSECTION :]
    out_refs[2][...] = blend_ramp(extents_ref, out_refs[2].shape)


def relayed(weight):
    tiles, subs = lax.axis_size("tile"), lax.axis_size("sub")
    out_share = weight.shape[4] // lax.axis_size("groups")
    own = lax.dynamic_slice_in_dim(weight, lax.axis_index("groups") * out_share, out_share, 4)
    own = own.reshape(3, -1, out_share)
    held, pieces = own, [own]
    for step in range(1, tiles):
        pairs = [(z * subs, (z + 1) * subs + 1) for z in range(step - 1, tiles - 1)]
        pairs += [(z * subs + 1, (z - 1) * subs) for z in range(1, tiles - step + 1)]
        arrived = lax.ppermute(held, ("tile", "sub"), pairs)
        held = lax.ppermute(arrived, "sub", [(0, 1), (1, 0)])
        pieces += [arrived, held]
    return pieces


def by_distance(array):
    got = [array]
    for code in range(1, 4):
        pairs = [(i, i ^ code) for i in range(4)]
        got.append(lax.ppermute(array, ("groups", "chan"), pairs))
    return got


def share_plan(latent, extents, gain_one, weight_one, gain_two, weight_two):
    frame_count, row_count, col_count, chan_count = latent.shape
    tiles, clips = lax.axis_size("tile"), lax.axis_size("groups")
    sub = lax.axis_index("sub")
    span = col_count + INTERSECTION
    share = chan_count // clips
    frames = clips * frame_count
    pitch = (span + 1) * row_count
    taps = weight_one.shape[1] * weight_one.shape[2]
    vmem, smem = pl.BlockSpec(memory_space=pltpu.VMEM), pl.BlockSpec(memory_space=pltpu.SMEM)
    anywhere = pl.BlockSpec(memory_space=pl.ANY)
    final = jax.ShapeDtypeStruct((frames, span, row_count, share), jnp.bfloat16)
    blocks = jax.ShapeDtypeStruct((tiles,) + final.shape, jnp.bfloat16)
    total = jax.ShapeDtypeStruct((frames * pitch, share), jnp.float32)

    def scratch():
        return [
            pltpu.VMEM((frames + 2, pitch, taps * LANES), jnp.bfloat16),
            pltpu.VMEM(((frames + 1) * pitch, 2 * share), jnp.float32),
        ]

    def chosen(weights, slots):
        return [weights[slot] for slot in slots]

    acc_scratch = [pltpu.VMEM(total.shape, jnp.float32)]

    by_col = jnp.transpose(latent, (0, 2, 1, 3))
    incoming = shifted(by_col[:, :INTERSECTION], "tile", -1)
    window = jnp.concatenate([by_col, incoming], axis=1)
    windows = []
    for turn in range(2):
        for away in range(2):
            pairs = [
                ((c * 2 + (x ^ away)) * 2 + (g ^ turn), (g * 2 + x) * 2 + c)
                for g in range(2)
                for x in range(2)
                for c in range(2)
            ]
            windows.append(lax.ppermute(window, ("groups", "chan", "sub"), pairs))
    first_weights = relayed(weight_one)
    second_weights = relayed(weight_two)
    own_gain = gain_one.reshape(1, -1)
    other_gain = lax.ppermute(own_gain, "chan", [(0, 1), (1, 0)])
    slots = tuple(range(2 * tiles - 1))
    early, late = slots[:-2], slots[-2:]
    hidden, source, begun = pl.pallas_call(
        functools.partial(first_begin, early),
        out_shape=(blocks, final, total),
        in_specs=[smem] + [vmem] * (6 + len(early)),
        out_specs=(vmem,) * 3,
        scratch_shapes=scratch(),
        compiler_params=pltpu.CompilerParams(vmem_limit_bytes=GRANT),
    )(extents, own_gain, other_gain, *windows, *chosen(first_weights, early))
    hidden_two = pl.pallas_call(
        functools.partial(first_end, late),
        out_shape=final,
        in_specs=[smem] + [vmem] * (3 + len(late)),
        out_specs=vmem,
        scratch_shapes=acc_scratch + scratch(),
        compiler_params=pltpu.CompilerParams(vmem_limit_bytes=GRANT),
    )(extents, gain_two.reshape(1, -1), hidden, begun, *chosen(first_weights, late))
    near = by_distance(hidden_two)
    near = [near[0], near[2], near[1], near[3]]
    kept = jax.ShapeDtypeStruct((frames, col_count, row_count, share), jnp.bfloat16)
    ramps = jax.ShapeDtypeStruct((2 * INTERSECTION, row_count, chan_count), jnp.float32)
    passed = jax.ShapeDtypeStruct((frames, INTERSECTION, row_count, share), jnp.bfloat16)
    own, tail, ramp = pl.pallas_call(
        functools.partial(second_kernel, slots),
        out_shape=(kept, passed, ramps),
        in_specs=[smem] + [anywhere] * (1 + tiles) + [vmem] * len(slots),
        out_specs=(vmem,) * 3,
        scratch_shapes=[
            pltpu.VMEM(final.shape, jnp.bfloat16),
            pltpu.SemaphoreType.DMA,
            pltpu.VMEM(blocks.shape, jnp.bfloat16),
            pltpu.SemaphoreType.DMA((tiles,)),
        ]
        + acc_scratch
        + scratch(),
        compiler_params=pltpu.CompilerParams(vmem_limit_bytes=LAST_GRANT),
    )(extents, source, *near, *chosen(second_weights, slots))

    onward = [
        ((g * tiles + z) * 2 + c, (c * tiles + z + 1) * 2 + g)
        for g in range(2)
        for z in range(tiles - 1)
        for c in range(2)
    ]
    tail = lax.ppermute(tail, ("groups", "tile", "sub"), onward)
    own = lax.ppermute(own, ("groups", "sub"), [(0, 0), (1, 2), (2, 1), (3, 3)])

    def frames_here(array):
        halves = array.reshape((2, frame_count) + array.shape[1:])
        mine = lax.dynamic_index_in_dim(halves, sub, 0, keepdims=False)
        other = lax.dynamic_index_in_dim(halves, 1 - sub, 0, keepdims=False)
        other = lax.ppermute(other, "sub", [(0, 1), (1, 0)])
        straight = jnp.concatenate([mine, other], axis=3)
        crossed = jnp.concatenate([other, mine], axis=3)
        return jnp.where(sub == 0, straight, crossed)

    own, tail = frames_here(own), frames_here(tail)
    ramp = ramp[None]
    head = jnp.repeat(own[:, :INTERSECTION].astype(jnp.float32), 2, axis=1) * ramp + jnp.repeat(
        tail.astype(jnp.float32), 2, axis=1
    ) * (1.0 - ramp)
    rest = jnp.repeat(own[:, INTERSECTION:], 2, axis=1)
    decoded = jnp.concatenate([head.astype(jnp.bfloat16), rest], axis=1)
    decoded = jnp.repeat(decoded, 2, axis=2)
    return jnp.transpose(decoded, (0, 2, 1, 3))


def solution(mesh):
    placed = (
        P(("groups", "sub"), None, "tile", "chan"),
        P(),
        P("chan"),
        P(None, None, None, "tile", "chan"),
        P("chan"),
        P(None, None, None, "tile", "chan"),
    )
    sizes = mesh.shape
    pairs_up = sizes["groups"] == 2 and sizes["sub"] == 2 and sizes["chan"] == 2
    few = pairs_up and CH // sizes["tile"] == LANES

    def body(*arrays):
        return (share_plan if few else gather_plan)(*arrays)

    return jax.shard_map(
        body,
        mesh=mesh,
        in_specs=placed,
        out_specs=P(("groups", "sub"), None, "tile", "chan"),
        check_vma=False,
    )
```
